32 devices in a mesh: wide: 8 (over y, x, core), narrow: 4 (over z).
Axes of the slice: x: 2, y: 2, z: 4, core: 2. Of those that a mesh axis runs over, the one named last changes fastest.
Arguments:
- hidden: bfloat16 [2, 2048, 768], P(None, 'wide'), may hold values from -6 to 6
- encoded: bfloat16 [2, 6144, 768], P(None, 'wide'), may hold values from -6 to 6
- token_lengths: int32 [2, 8], replicated, may hold values from 64 to 448, as said below
- frame_counts: int32 [2, 8], replicated, may hold values from 36 to 1500, as said below
- ln_gain: float32 [3, 768], replicated, may hold values from 0.1 to 1.9
- ln_bias: float32 [3, 768], replicated, may hold values from -1.5 to 1.5
- head_bias: float32 [4, 768], P(None, 'narrow'), may hold values from -2.5 to 2.5
- out_bias: float32 [3, 768], replicated, may hold values from -1 to 1
- fc_bias: float32 [3072], P('narrow'), may hold values from -2.5 to 2.5
- self_proj: bfloat16 [3, 768, 768], P(None, 'wide', 'narrow'), may hold values from -0.21875 to 0.21875
- cross_proj: bfloat16 [3, 768, 768], P(None, 'wide', 'narrow'), may hold values from -0.21875 to 0.21875
- out_proj: bfloat16 [2, 768, 768], P(None, 'narrow', 'wide'), may hold values from -1.25 to 1.25
- fc_in: bfloat16 [768, 3072], P('wide', 'narrow'), may hold values from -0.21875 to 0.21875
- fc_out: bfloat16 [3072, 768], P('narrow', 'wide'), may hold values from -0.109375 to 0.109375
- cotangent: bfloat16 [2, 2048, 768], P(None, 'wide'), may hold values from -6 to 6
Outputs:
- output: bfloat16 [2, 2048, 768], P(None, 'wide')
- input_grad: float32 [2, 2048, 768], P(None, 'wide')
- encoded_grad: float32 [2, 6144, 768], P(None, 'wide')
- grad_ln_gain: float32 [3, 768], replicated
- grad_ln_bias: float32 [3, 768], replicated
- grad_head_bias: float32 [4, 768], P(None, 'narrow')
- grad_out_bias: float32 [3, 768], replicated
- grad_fc_bias: float32 [3072], P('narrow')
- grad_self_proj: float32 [3, 768, 768], P(None, 'wide', 'narrow')
- grad_cross_proj: float32 [3, 768, 768], P(None, 'wide', 'narrow')
- grad_out_proj: float32 [2, 768, 768], P(None, 'narrow', 'wide')
- grad_fc_in: float32 [768, 3072], P('wide', 'narrow')
- grad_fc_out: float32 [3072, 768], P('narrow', 'wide')
The draws below stay inside these ranges and needn't reach their ends.
Inputs may be any that keep to these rules, and one draw needn't show every extreme that they name: `token_lengths`: each row holds the token counts of the 8 items of one micro-batch in packing order; a row sums to 2048, the end of item i lies within (192) / 2 tokens of 256 times (i + 1), and item 2 of every row has 448 tokens. `frame_counts`: each row holds the frame counts of the 8 items of one micro-batch in packing order; items 2k and 2k + 1 together have 3 times their tokens, each item's count differs from 3 times its tokens by at most 156, and item 2 of every row has 1500 frames. So the frames of an item lie within the frame shards of the wide indices from two below the first to two above the last that hold its tokens.
All inputs are finite; a program needn't handle non-finite values.
Results may differ from the reference program's by a relative error of at most 0.03.
Values may be sent and summed in bfloat16 or wider, within the bound.
No kernel may reach another device: no remote copies, remote signals or barrier semaphores. Data moves between devices by JAX's collectives and lax.ppermute only.
A program may use at most 192 MiB of HBM per device.

```python
import jax
import jax.numpy as jnp
from jax import lax

D = 768
HEADS = 12
HD = 64
FF = 3072
MAXLEN = 448
MB = 2
ITEM_MEAN = 256
FR_TOK = 3
JITTER = 156
TOK_DEV = 256
FR_DEV = 768
TOKENS = 2048
ITEMS = 8
FRAMES = 6144


def item_layout(key):
    swing = (MAXLEN - ITEM_MEAN) // 2
    offsets = jax.random.randint(jax.random.fold_in(key, 11), (MB, ITEMS), -swing, swing + 1)
    offsets = offsets.at[:, 1].set(-swing).at[:, 2].set(swing).at[:, ITEMS - 1].set(0)
    ends = ITEM_MEAN * (jnp.arange(ITEMS, dtype=jnp.int32)[None, :] + 1) + offsets
    starts = jnp.concatenate([jnp.zeros((MB, 1), jnp.int32), ends[:, :-1]], axis=1)
    lengths = ends - starts
    jitters = jax.random.randint(jax.random.fold_in(key, 12), (MB, ITEMS // 2), 0, JITTER + 1)
    jitters = jitters.at[:, 1].set(JITTER)
    signed = jnp.stack([jitters, -jitters], axis=2).reshape(MB, ITEMS)
    frames = FR_TOK * lengths + signed
    return (lengths.astype(jnp.int32), frames.astype(jnp.int32))


def draw_token_lengths(key, part):
    return item_layout(key)[0]


def draw_frame_counts(key, part):
    return item_layout(key)[1]


def with_spikes(array, own_key, source, target, blocks, factor):
    def block_of(position):
        return (jnp.arange(array.shape[position]) // (array.shape[position] // blocks)).reshape((-1,) + (1,) * (array.ndim - 1 - position))

    one_side = jax.random.permutation(own_key, blocks)[block_of(target)]
    other_side = (block_of(target) + blocks // 2) % blocks
    return jnp.where((block_of(source) == one_side) | (block_of(source) == other_side), factor * array, array)


def levels(stream_key, dims, pieces, least, largest):
    level, own = 1.0, jax.random.fold_in(stream_key, 6)
    for dim, shards_of in pieces:
        steps = jnp.exp(jax.random.uniform(jax.random.fold_in(own, dim), (shards_of,), jnp.float32, least / len(pieces), largest / len(pieces)))
        level = level * jnp.repeat(steps, dims[dim] // shards_of).reshape([-1 if axis == dim else 1 for axis in range(len(dims))])
    return level


def scatter_about(key, extent, scale, bound, split=(), held_as=jnp.bfloat16):
    entries = scale * jax.random.normal(key, extent, jnp.float32)
    if split:
        entries = entries * levels(key, extent, split, -0.22, 0.18)
    return jnp.clip(entries, -bound, bound).astype(held_as)


def noise_with(stream_key, extent, width, most, split, heavy, held_as=jnp.bfloat16):
    entries = width * jax.random.normal(stream_key, extent, jnp.float32)
    if split:
        entries = entries * levels(stream_key, extent, split, -0.22, 0.18)
    return jnp.clip(with_spikes(entries, jax.random.fold_in(stream_key, 3), *heavy), -most, most).astype(held_as)


def setup_inputs(seed: int = 0) -> dict:
    keys = jax.random.split(jax.random.key(seed), 16)
    hidden = noise_with(keys[0], (MB, TOKENS, D), 1.0, 6.0, ((1, 8),), (1, 2, 8, 2.0))
    encoded = scatter_about(keys[1], (MB, FRAMES, D), 1.0, 6.0, ((1, 8),))
    token_lengths = draw_token_lengths(jax.random.fold_in(keys[15], 71), 0)
    frame_counts = draw_frame_counts(jax.random.fold_in(keys[15], 71), 0)
    ln_gain = jnp.clip(1.0 + 0.18 * jax.random.normal(keys[4], (3, D), jnp.float32), 0.1, 1.9)
    ln_bias = scatter_about(keys[5], (3, D), 0.3, 1.5, (), jnp.float32)
    head_bias = scatter_about(keys[6], (4, D), 0.5, 2.5, ((1, 4),), jnp.float32)
    out_bias = scatter_about(keys[7], (3, D), 0.2, 1.0, (), jnp.float32)
    fc_bias = scatter_about(keys[8], (FF,), 0.5, 2.5, ((0, 4),), jnp.float32)
    self_proj = scatter_about(keys[9], (3, D, D), D ** -0.5, 0.21875, ((1, 8), (2, 4)))
    cross_proj = scatter_about(keys[10], (3, D, D), D ** -0.5, 0.21875, ((1, 8), (2, 4)))
    out_proj = scatter_about(keys[11], (2, D, D), (D // 32) ** -0.5, 1.25, ((1, 4), (2, 8)))
    fc_in = scatter_about(keys[12], (D, FF), D ** -0.5, 0.21875, ((0, 8), (1, 4)))
    fc_out = scatter_about(keys[13], (FF, D), FF ** -0.5, 0.109375, ((0, 4), (1, 8)))
    cotangent = noise_with(keys[14], (MB, TOKENS, D), 1.0, 6.0, ((1, 8),), (1, 2, 8, 2.0))
    return dict(hidden=hidden, encoded=encoded, token_lengths=token_lengths, frame_counts=frame_counts, ln_gain=ln_gain, ln_bias=ln_bias, head_bias=head_bias, out_bias=out_bias, fc_bias=fc_bias, self_proj=self_proj, cross_proj=cross_proj, out_proj=out_proj, fc_in=fc_in, fc_out=fc_out, cotangent=cotangent)


@jax.custom_vjp
def low(v):
    return lax.optimization_barrier(v.astype(jnp.bfloat16)).astype(jnp.float32)

@jax.custom_vjp
def low_back(v):
    return v

def low_keep(v):
    return (low(v), None)

def low_pass(kept, grad):
    return (grad,)

def back_keep(v):
    return (v, None)

def back_low(kept, grad):
    return (low(grad),)
low.defvjp(low_keep, low_pass)
low_back.defvjp(back_keep, back_low)
epsilon = 1e-05

def matmul(left, right):
    return jnp.dot(left, right, precision=lax.Precision.HIGHEST)

def layer_norm(values, gain, offset):
    centre = values - lax.optimization_barrier(jnp.mean(values, axis=-1, keepdims=True))
    spread = lax.optimization_barrier(jnp.mean(centre * centre, axis=-1, keepdims=True))
    return centre * lax.rsqrt(spread + epsilon) * gain + offset

def owners(places, lengths):
    ends = jnp.cumsum(lengths)
    return lax.optimization_barrier(jnp.sum((places[:, None] >= ends[None, :]).astype(jnp.int32), axis=1))

def attend(queries, key_rows, value_rows, allowed):
    query_count = queries.shape[0]
    key_count = key_rows.shape[0]
    split_q = queries.reshape(query_count, HEADS, HD)
    split_k = key_rows.reshape(key_count, HEADS, HD)
    split_v = value_rows.reshape(key_count, HEADS, HD)
    raw = jnp.einsum('qhc,khc->hqk', split_q, split_k, precision=lax.Precision.HIGHEST) * HD ** (-0.5)
    scores = low_back(raw)
    weights = jnp.where(allowed[None], jnp.exp(scores), 0.0)
    denominator = lax.optimization_barrier(jnp.sum(weights, axis=2))
    summed = low_back(jnp.einsum('hqk,khc->qhc', low(weights), split_v, precision=lax.Precision.HIGHEST))
    return (summed / denominator.T[:, :, None]).reshape(query_count, D)

def windows(table, filler):
    blocks = TOKENS // TOK_DEV
    padded = jnp.concatenate([jnp.full((2 * TOK_DEV,) + table.shape[1:], filler, table.dtype), table], axis=0)
    farthest = padded[:TOKENS].reshape((blocks, TOK_DEV) + table.shape[1:])
    nearer = padded[TOK_DEV:TOK_DEV + TOKENS].reshape((blocks, TOK_DEV) + table.shape[1:])
    behind = padded[2 * TOK_DEV:].reshape((blocks, TOK_DEV) + table.shape[1:])
    return jnp.concatenate([farthest, nearer, behind], axis=1)

def framed(table, filler):
    border = jnp.full((2 * FR_DEV,) + table.shape[1:], filler, table.dtype)
    return jnp.concatenate([border, table, border], axis=0)

def block_forward(params, states, memory, tok_item, frame_item):
    ln_gain, ln_bias, head_bias, out_bias, fc_bias, self_proj, cross_proj, out_proj, fc_in, fc_out = params
    blocks = TOKENS // TOK_DEV
    norm_one = low(layer_norm(states, ln_gain[0], ln_bias[0]))
    queries = low(low_back(matmul(norm_one, self_proj[0]) + head_bias[0]))
    key_rows = low(low_back(matmul(norm_one, self_proj[1])))
    value_rows = low(low_back(matmul(norm_one, self_proj[2]) + head_bias[1]))
    query_places = jnp.arange(TOKENS, dtype=jnp.int32).reshape(blocks, TOK_DEV)
    key_places = jnp.arange(blocks, dtype=jnp.int32)[:, None] * TOK_DEV - 2 * TOK_DEV + jnp.arange(3 * TOK_DEV, dtype=jnp.int32)[None, :]

    def self_block(inputs):
        q_rows, k_rows, v_rows, q_place, k_place, q_item, k_item = inputs
        allowed = (k_place[None, :] <= q_place[:, None]) & (k_item[None, :] == q_item[:, None]) & (k_place[None, :] >= 0)
        return attend(q_rows, k_rows, v_rows, allowed)
    attended = lax.map(jax.checkpoint(self_block), (queries.reshape(blocks, TOK_DEV, D), windows(key_rows, 0.0), windows(value_rows, 0.0), query_places, key_places, tok_item.reshape(blocks, TOK_DEV), windows(tok_item, -1)))
    self_low = low(low_back(attended.reshape(TOKENS, D)))
    resid_one = states + (low_back(matmul(self_low, out_proj[0])) + out_bias[0])
    norm_two = low(layer_norm(resid_one, ln_gain[1], ln_bias[1]))
    cross_q = low(low_back(matmul(norm_two, cross_proj[0]) + head_bias[2]))
    cross_k = low(low_back(matmul(memory, cross_proj[1])))
    cross_v = low(low_back(matmul(memory, cross_proj[2]) + head_bias[3]))
    padded_keys = framed(cross_k, 0.0)
    padded_values = framed(cross_v, 0.0)
    padded_items = framed(frame_item, -1)

    def cross_block(inputs):
        q_rows, q_item, section = inputs
        first_row = (section * FR_DEV).astype(jnp.int32)
        key_window = lax.dynamic_slice_in_dim(padded_keys, first_row, 5 * FR_DEV, 0)
        value_window = lax.dynamic_slice_in_dim(padded_values, first_row, 5 * FR_DEV, 0)
        item_window = lax.dynamic_slice_in_dim(padded_items, first_row, 5 * FR_DEV, 0)
        allowed = q_item[:, None] == item_window[None, :]
        return attend(q_rows, key_window, value_window, allowed)
    crossed = lax.map(jax.checkpoint(cross_block), (cross_q.reshape(blocks, TOK_DEV, D), tok_item.reshape(blocks, TOK_DEV), jnp.arange(blocks, dtype=jnp.int32)))
    cross_low = low(low_back(crossed.reshape(TOKENS, D)))
    resid_two = resid_one + (low_back(matmul(cross_low, out_proj[1])) + out_bias[1])
    norm_three = low(layer_norm(resid_two, ln_gain[2], ln_bias[2]))
    pre_act = low_back(matmul(norm_three, fc_in) + fc_bias)
    act_low = low(jax.nn.gelu(pre_act, approximate=False))
    return resid_two + (low_back(matmul(act_low, fc_out)) + out_bias[2])

def reference(hidden, encoded, token_lengths, frame_counts, ln_gain, ln_bias, head_bias, out_bias, fc_bias, self_proj, cross_proj, out_proj, fc_in, fc_out, cotangent):
    params = tuple((tensor.astype(jnp.float32) for tensor in (ln_gain, ln_bias, head_bias, out_bias, fc_bias, self_proj, cross_proj, out_proj, fc_in, fc_out)))
    tok_places = jnp.arange(TOKENS, dtype=jnp.int32)
    frame_places = jnp.arange(FRAMES, dtype=jnp.int32)
    totals = jax.tree.map(jnp.zeros_like, params)
    outputs = []
    input_grads = []
    frame_grads = []
    for microbatch in range(MB):
        tok_item = owners(tok_places, token_lengths[microbatch])
        frame_item = owners(frame_places, frame_counts[microbatch])

        def forward(weights, states, memory):
            return block_forward(weights, states, memory, tok_item, frame_item)
        result, pullback = jax.vjp(forward, params, hidden[microbatch].astype(jnp.float32), encoded[microbatch].astype(jnp.float32))
        grads_w, grads_h, grads_e = pullback(cotangent[microbatch].astype(jnp.float32))
        totals = jax.tree.map(jnp.add, totals, grads_w)
        outputs.append(result)
        input_grads.append(grads_h)
        frame_grads.append(grads_e)
    return (jnp.stack(outputs).astype(jnp.bfloat16), jnp.stack(input_grads), jnp.stack(frame_grads), totals[0], totals[1], totals[2], totals[3], totals[4], totals[5], totals[6], totals[7], totals[8], totals[9])
```

```python
from functools import partial

import jax
import jax.numpy as jnp
from jax import lax
from jax.experimental import pallas as pl
from jax.experimental.pallas import tpu as pltpu
from jax.sharding import PartitionSpec as P

HD = 64
LANES = 128
MAXLEN = 448
JITTER = 156
EPSILON = 1e-05
F32 = jnp.float32
BF16 = jnp.bfloat16
NN = (((1,), (0,)), ((), ()))
NT = (((1,), (1,)), ((), ()))
TN = (((0,), (0,)), ((), ()))
AXES = ("wide", "narrow")


def mm(left, right, dims=NN):
    return lax.dot_general(left, right, dims, preferred_element_type=F32)


def normalise(values):
    centre = values - jnp.mean(values, axis=-1, keepdims=True)
    spread = jnp.mean(centre * centre, axis=-1, keepdims=True)
    inverse = lax.rsqrt(spread + EPSILON)
    return centre * inverse, inverse


def norm_back(grad_rows, unit_rows, inverse, gain):
    scaled = grad_rows * gain
    centred = scaled - jnp.mean(scaled, axis=-1, keepdims=True)
    return (centred - unit_rows * jnp.mean(scaled * unit_rows, axis=-1, keepdims=True)) * inverse


def erf(x):
    x = jnp.clip(x, -3.832506856900711, 3.832506856900711)
    x2 = x * x
    top = x2 * 0.00022905065861350646 + 0.0034082910107109506
    top = top * x2 + 0.050955695062380861
    top = top * x2 + 0.18520832239976145
    top = top * x2 + 1.128379143519084
    low = x2 * -1.1791602954361697e-7 + 0.000023547966471313185
    low = low * x2 + 0.0010179625278914885
    low = low * x2 + 0.014070470171167667
    low = low * x2 + 0.11098505178285362
    low = low * x2 + 0.49746925110067538
    low = low * x2 + 1.0
    return x * top / low


def fetch(scalars, blocks, whole, sems):
    rows = blocks[0].shape[0]
    here = scalars[0]
    copies = []
    for j, block in enumerate(blocks):
        at = pl.multiple_of(rows * jnp.bitwise_xor(here, j), rows)
        copies.append(pltpu.make_async_copy(block, whole.at[pl.ds(at, rows), :], sems.at[j]))
    for copy in copies:
        copy.start()
    return copies


def first_half(shape):
    return lax.broadcasted_iota(jnp.int32, shape, len(shape) - 1) < HD


def self_forward(
    scalars, hidden, gains, shifts, biases, w0, w1, w2, w3,
    norm_out, q_out, k_out, v_out, o_out, den_out, part_out, whole, sems,
):
    copies = fetch(scalars, (w0, w1, w2, w3), whole, sems)
    rows = hidden.shape[0]
    pairs = q_out.shape[0]
    cols = pairs * LANES
    unit, _ = normalise(hidden[...].astype(F32))
    norm = (unit * gains[0:1, :] + shifts[0:1, :]).astype(BF16)
    norm_out[...] = norm
    lo, hi = scalars[1], scalars[2]
    place = lax.broadcasted_iota(jnp.int32, (rows, 1), 0)
    valid = (place >= lo) & (place < hi)
    for copy in copies:
        copy.wait()
    query = (mm(norm, whole[:, :cols]) + biases[0:1, :]).astype(BF16).astype(F32)
    query = jnp.where(valid, query * HD ** -0.5, 0.0).astype(BF16)
    key = mm(norm, whole[:, cols : 2 * cols]).astype(BF16)
    value = (mm(norm, whole[:, 2 * cols : 3 * cols]) + biases[1:2, :]).astype(BF16)
    for p in range(pairs):
        q_out[p] = query[:, p * LANES : (p + 1) * LANES]
        k_out[p] = key[:, p * LANES : (p + 1) * LANES]
        v_out[p] = value[:, p * LANES : (p + 1) * LANES]
    q_place = lax.broadcasted_iota(jnp.int32, (rows, rows), 0)
    k_place = lax.broadcasted_iota(jnp.int32, (rows, rows), 1)
    allowed = (k_place <= q_place) & (k_place >= lo)
    half = first_half((rows, LANES))
    zero = jnp.zeros((), BF16)

    def one_pair(p, carry):
        q_pair, k_pair, v_pair = q_out[p], k_out[p], v_out[p]
        outs, dens = [], []
        for keep in (half, jnp.logical_not(half)):
            raw = mm(jnp.where(keep, q_pair, zero), k_pair, NT)
            weights = jnp.where(allowed, jnp.exp(raw), 0.0)
            total = jnp.sum(weights, axis=1, keepdims=True)
            total = jnp.where(total > 0.0, total, 1.0)
            outs.append(mm(weights.astype(BF16), v_pair) / total)
            dens.append(jnp.broadcast_to(total, (rows, LANES)))
        o_out[p] = jnp.where(half, outs[0], outs[1])
        den_out[p] = jnp.where(half, dens[0], dens[1])
        return carry

    lax.fori_loop(0, pairs, one_pair, 0)
    low = jnp.concatenate([o_out[p] for p in range(pairs)], axis=1).astype(BF16)
    part_out[...] = mm(low, whole[:, 3 * cols :], NT).astype(BF16)


def frame_project(scalars, frames, biases, w0, w1, w2, w3, k_out, v_out, whole, sems):
    copies = fetch(scalars, (w0, w1, w2, w3), whole, sems)
    pairs = k_out.shape[0]
    cols = pairs * LANES
    for copy in copies:
        copy.wait()
    key = mm(frames[...], whole[:, cols : 2 * cols]).astype(BF16)
    for p in range(pairs):
        k_out[p] = key[:, p * LANES : (p + 1) * LANES]
    value = (mm(frames[...], whole[:, 2 * cols : 3 * cols]) + biases[3:4, :]).astype(BF16)
    for p in range(pairs):
        v_out[p] = value[:, p * LANES : (p + 1) * LANES]


def cross_forward(
    scalars, hidden, mine, other, gains, shifts, outs_bias, biases, k_all, v_all, w0, w1, w2, w3,
    resid_out, norm_out, q_out, o_out, den_out, part_out, whole, sems,
):
    copies = fetch(scalars, (w0, w1, w2, w3), whole, sems)
    rows = hidden.shape[0]
    pairs = q_out.shape[0]
    cols = pairs * LANES
    summed = mine[...].astype(F32) + other[...].astype(F32)
    resid = hidden[...].astype(F32) + (summed + outs_bias[0:1, :])
    resid_out[...] = resid
    unit, _ = normalise(resid)
    norm = (unit * gains[1:2, :] + shifts[1:2, :]).astype(BF16)
    norm_out[...] = norm
    place = lax.broadcasted_iota(jnp.int32, (rows, 1), 0)
    valid = (place >= scalars[1]) & (place < scalars[2])
    for copy in copies:
        copy.wait()
    query = (mm(norm, whole[:, :cols]) + biases[2:3, :]).astype(BF16).astype(F32)
    query = jnp.where(valid, query * HD ** -0.5, 0.0).astype(BF16)
    for p in range(pairs):
        q_out[p] = query[:, p * LANES : (p + 1) * LANES]
    frame = lax.broadcasted_iota(jnp.int32, (1, k_all.shape[1]), 1)
    allowed = (frame >= scalars[3]) & (frame < scalars[4])
    half = first_half((rows, LANES))
    zero = jnp.zeros((), BF16)

    def one_pair(p, carry):
        q_pair, k_pair, v_pair = q_out[p], k_all[p], v_all[p]
        outs, dens = [], []
        for keep in (half, jnp.logical_not(half)):
            raw = mm(jnp.where(keep, q_pair, zero), k_pair, NT)
            weights = jnp.where(allowed, jnp.exp(raw), 0.0)
            total = jnp.sum(weights, axis=1, keepdims=True)
            outs.append(mm(weights.astype(BF16), v_pair) / total)
            dens.append(jnp.broadcast_to(total, (rows, LANES)))
        o_out[p] = jnp.where(half, outs[0], outs[1])
        den_out[p] = jnp.where(half, dens[0], dens[1])
        return carry

    lax.fori_loop(0, pairs, one_pair, 0)
    low = jnp.concatenate([o_out[p] for p in range(pairs)], axis=1).astype(BF16)
    part_out[...] = mm(low, whole[:, 3 * cols :], NT).astype(BF16)


CHUNK = 256


def unit_forward(
    scalars, resid, mine, other, gains, shifts, outs_bias, fc_bias, cotangent,
    a0, a1, a2, a3, d0, d1, d2, d3,
    resid_out, norm_out, act_out, pre_out, part_out, back_out, sum_out,
    whole_in, whole_back, sems_in, sems_back,
):
    copies = fetch(scalars, (a0, a1, a2, a3), whole_in, sems_in)
    copies += fetch(scalars, (d0, d1, d2, d3), whole_back, sems_back)
    summed = mine[...].astype(F32) + other[...].astype(F32)
    resid_two = resid[...] + (summed + outs_bias[1:2, :])
    resid_out[...] = resid_two
    unit, _ = normalise(resid_two)
    norm_out[...] = (unit * gains[2:3, :] + shifts[2:3, :]).astype(BF16)
    for copy in copies:
        copy.wait()

    def one_chunk(j, carry):
        at = pl.ds(pl.multiple_of(j * CHUNK, CHUNK), CHUNK)
        pre = mm(norm_out[...], whole_in[:, at]) + fc_bias[:, at]
        cdf = 0.5 * (1.0 + erf(pre * 0.7071067811865476))
        act_out[:, at] = (pre * cdf).astype(BF16)
        slope = cdf + pre * (jnp.exp(-0.5 * pre * pre) * 0.3989422804014327)
        grad = (slope * mm(cotangent[...], whole_back[:, at])).astype(BF16)
        pre_out[:, at] = grad
        sum_out[:, at] = jnp.sum(grad.astype(F32), axis=0, keepdims=True)
        return carry

    lax.fori_loop(0, act_out.shape[1] // CHUNK, one_chunk, 0)
    back_out[...] = mm(pre_out[...], whole_in[...], NT).astype(BF16)
    part_out[...] = mm(act_out[...], whole_back[...], NT).astype(BF16)


def finish_output(scalars, resid, mine, other, outs_bias, out):
    rows = resid.shape[0]
    place = lax.broadcasted_iota(jnp.int32, (rows, 1), 0)
    valid = (place >= scalars[1]) & (place < scalars[2])
    summed = mine[...].astype(F32) + other[...].astype(F32)
    total = resid[...] + (summed + outs_bias[2:3, :])
    out[...] = jnp.where(valid, total, 0.0).astype(BF16)


def column_sum(values):
    return jnp.sum(values, axis=0, keepdims=True)


def cross_backward(
    scalars, resid, cotangent, mine, other, gains, q_all, k_all, v_all, o_all, den_all,
    w0, w1, w2, w3,
    grad_out, low_out, att_out, dq_out, dk_out, dv_out, part_out, sums_out, heads_out,
    drop, whole, sems,
):
    copies = fetch(scalars, (w0, w1, w2, w3), whole, sems)
    rows = resid.shape[0]
    pairs = q_all.shape[0]
    cols = pairs * LANES
    unit, inverse = normalise(resid[...])
    grad_norm = mine[...].astype(F32) + other[...].astype(F32)
    top = cotangent[...].astype(F32)
    grad = top + norm_back(grad_norm, unit, inverse, gains[2:3, :])
    sums_out[0:1, :] = column_sum(grad_norm * unit)
    sums_out[1:2, :] = column_sum(grad_norm)
    sums_out[2:3, :] = column_sum(top)
    sums_out[3:4, :] = column_sum(grad)
    grad_out[...] = grad
    low = grad.astype(BF16)
    low_out[...] = low
    for p in range(pairs):
        att_out[:, p * LANES : (p + 1) * LANES] = o_all[p].astype(BF16)
    for copy in copies:
        copy.wait()
    attended = mm(low, whole[:, 3 * cols :]).astype(BF16)
    for p in range(pairs):
        drop[p] = attended[:, p * LANES : (p + 1) * LANES]
    count = k_all.shape[1]
    frame = lax.broadcasted_iota(jnp.int32, (count, 1), 0)
    allowed = (frame >= scalars[3]) & (frame < scalars[4])
    attend_back(pairs, rows, allowed, drop, q_all, k_all, v_all, o_all, den_all, dq_out, dk_out, dv_out)
    dq = jnp.concatenate([dq_out[p] for p in range(pairs)], axis=1)
    part_out[...] = mm(dq, whole[:, :cols], NT).astype(BF16)
    for p in range(pairs):
        heads_out[0:1, p * LANES : (p + 1) * LANES] = column_sum(dq_out[p].astype(F32))
        heads_out[1:2, p * LANES : (p + 1) * LANES] = column_sum(dv_out[p].astype(F32))


def attend_back(pairs, rows, allowed, drop, q_all, k_all, v_all, o_all, den_all, dq_out, dk_out, dv_out):
    count = k_all.shape[1]
    half = first_half((count, LANES))
    zero = jnp.zeros((), BF16)
    upper = lax.broadcasted_iota(jnp.int32, (LANES, rows), 0) < HD

    def one_pair(p, carry):
        q_pair, k_pair, v_pair = q_all[p], k_all[p], v_all[p]
        grad = drop[p].astype(F32)
        den = den_all[p]
        grad_sums = (grad / den).astype(BF16)
        drift_all = (grad * o_all[p] / den).T
        found = []
        for t in range(2):
            keep = half if t == 0 else jnp.logical_not(half)
            drift = jnp.sum(drift_all[t * HD : (t + 1) * HD, :], axis=0, keepdims=True)
            raw = mm(jnp.where(keep, k_pair, zero), q_pair, NT)
            weights = jnp.where(allowed, jnp.exp(raw), 0.0)
            prob = mm(jnp.where(keep, v_pair, zero), grad_sums, NT)
            score = (weights * (prob - drift)).astype(BF16)
            found.append(
                (
                    mm(k_pair, score, TN),
                    mm(score, q_pair),
                    mm(weights.astype(BF16), grad_sums),
                )
            )
        dq_out[p] = (jnp.where(upper, found[0][0], found[1][0]).T * HD ** -0.5).astype(BF16)
        dk_out[p] = jnp.where(half, found[0][1], found[1][1]).astype(dk_out.dtype)
        dv_out[p] = jnp.where(half, found[0][2], found[1][2]).astype(dv_out.dtype)
        return carry

    lax.fori_loop(0, pairs, one_pair, 0)


def self_backward(
    scalars, resid, top, mine, other, gains, q_all, k_all, v_all, o_all, den_all,
    w0, w1, w2, w3,
    grad_out, low_out, att_out, dq_out, dk_out, dv_out, part_out, sums_out, heads_out,
    drop, whole, sems,
):
    copies = fetch(scalars, (w0, w1, w2, w3), whole, sems)
    rows = resid.shape[0]
    pairs = q_all.shape[0]
    cols = pairs * LANES
    unit, inverse = normalise(resid[...])
    grad_norm = mine[...].astype(F32) + other[...].astype(F32)
    grad = top[...] + norm_back(grad_norm, unit, inverse, gains[1:2, :])
    sums_out[0:1, :] = column_sum(grad_norm * unit)
    sums_out[1:2, :] = column_sum(grad_norm)
    sums_out[2:3, :] = column_sum(grad)
    grad_out[...] = grad
    low = grad.astype(BF16)
    low_out[...] = low
    for p in range(pairs):
        att_out[:, p * LANES : (p + 1) * LANES] = o_all[p].astype(BF16)
    for copy in copies:
        copy.wait()
    attended = mm(low, whole[:, 3 * cols :]).astype(BF16)
    for p in range(pairs):
        drop[p] = attended[:, p * LANES : (p + 1) * LANES]
    k_place = lax.broadcasted_iota(jnp.int32, (rows, rows), 0)
    q_place = lax.broadcasted_iota(jnp.int32, (rows, rows), 1)
    allowed = (k_place <= q_place) & (k_place >= scalars[1])
    attend_back(pairs, rows, allowed, drop, q_all, k_all, v_all, o_all, den_all, dq_out, dk_out, dv_out)
    total = jnp.zeros((rows, part_out.shape[1]), F32)
    for index, piece in enumerate((dq_out, dk_out, dv_out)):
        joined = jnp.concatenate([piece[p] for p in range(pairs)], axis=1)
        total = total + mm(joined, whole[:, index * cols : (index + 1) * cols], NT)
    part_out[...] = total.astype(BF16)
    for p in range(pairs):
        heads_out[0:1, p * LANES : (p + 1) * LANES] = column_sum(dq_out[p].astype(F32))
        heads_out[1:2, p * LANES : (p + 1) * LANES] = column_sum(dv_out[p].astype(F32))


def input_backward(hidden, top, mine, other, gains, out, sums_out):
    unit, inverse = normalise(hidden[...].astype(F32))
    grad_norm = mine[...].astype(F32) + other[...].astype(F32)
    grad = top[...] + norm_back(grad_norm, unit, inverse, gains[0:1, :])
    sums_out[0:1, :] = column_sum(grad_norm * unit)
    sums_out[1:2, :] = column_sum(grad_norm)
    out[...] = grad.astype(BF16)


def frame_backward(scalars, dk_all, dv_all, w0, w1, w2, w3, out, whole, sems):
    copies = fetch(scalars, (w0, w1, w2, w3), whole, sems)
    pairs = dk_all.shape[0]
    cols = pairs * LANES
    dk = jnp.concatenate([dk_all[p] for p in range(pairs)], axis=1)
    dv = jnp.concatenate([dv_all[p] for p in range(pairs)], axis=1)
    for copy in copies:
        copy.wait()
    total = mm(dk, whole[:, cols : 2 * cols], NT) + mm(dv, whole[:, 2 * cols : 3 * cols], NT)
    out[...] = total.astype(BF16)


def weight_grads(layout, scalars, *refs):
    count = 1 + max(max(pair) for pair in layout)
    operands = refs[:count]
    outs = refs[count : count + 4]
    whole, sems = refs[count + 4 :]
    at = 0
    for left, right in layout:
        ref = operands[right]
        if len(ref.shape) == 3:
            grads = jnp.concatenate([ref[p] for p in range(ref.shape[0])], axis=1)
        else:
            grads = ref[...]
        size = grads.shape[1]
        whole[:, at : at + size] = mm(operands[left][...], grads, TN).astype(BF16)
        at += size
    rows = outs[0].shape[0]
    copies = []
    for j, out in enumerate(outs):
        start = pl.multiple_of(rows * jnp.bitwise_xor(scalars[0], j), rows)
        copies.append(pltpu.make_async_copy(whole.at[pl.ds(start, rows), :], out, sems.at[j]))
    for copy in copies:
        copy.start()
    for copy in copies:
        copy.wait()


SMEM = pl.BlockSpec(memory_space=pltpu.SMEM)
VMEM = pl.BlockSpec(memory_space=pltpu.VMEM)
ANY = pl.BlockSpec(memory_space=pl.ANY)


def shape(dims, dtype):
    return jax.ShapeDtypeStruct(tuple(dims), dtype)


def kernel_call(kernel, name, operands, spaces, outs, out_spaces=None, scratch=()):
    return pl.pallas_call(
        kernel,
        out_shape=tuple(outs),
        in_specs=list(spaces),
        out_specs=tuple(out_spaces or [VMEM] * len(outs)),
        scratch_shapes=list(scratch),
        compiler_params=pltpu.CompilerParams(vmem_limit_bytes=56 * 1024 * 1024),
        name=name,
    )(*operands)


def body(
    hidden, encoded, token_lengths, frame_counts, ln_gain, ln_bias, head_bias, out_bias, fc_bias,
    self_proj, cross_proj, out_proj, fc_in, fc_out, cotangent,
):
    wide = lax.axis_size("wide")
    depth = lax.axis_size("narrow")
    tok_rows, width = hidden.shape[1:]
    frame_rows = encoded.shape[1]
    swing = (MAXLEN - tok_rows) // 2
    ratio = frame_rows // tok_rows
    near = ratio * swing
    far = frame_rows - near
    assert far >= near + JITTER and far + near == frame_rows and depth == 4 and hidden.shape[0] == 2
    rows = tok_rows + 2 * swing
    frames = near + frame_rows + far
    shard = width // wide
    heads_cols = head_bias.shape[1]
    cols = 2 * heads_cols
    pairs = cols // LANES
    units = 2 * fc_bias.shape[0]

    w = lax.axis_index("wide")
    n = lax.axis_index("narrow")
    chip = w // 2
    core = w % 2
    batch = n // 2
    odd = n % 2
    item = 2 * chip + odd
    relay = wide == 8

    def move(value, rule):
        pairs_list = []
        for ws in range(wide):
            for ns in range(depth):
                target = rule(ws, ns)
                if target is not None and 0 <= target[0] < wide:
                    pairs_list.append((ws * depth + ns, target[0] * depth + target[1]))
        return lax.ppermute(value, AXES, pairs_list)

    def swap(value):
        return move(value, lambda a, z: (a ^ 1, z))

    def pick(value, index):
        return lax.dynamic_index_in_dim(value, index, 0, keepdims=False)

    def ordered(own, partner):
        return jnp.where(
            core == 0,
            jnp.concatenate([own, partner], axis=0),
            jnp.concatenate([partner, own], axis=0),
        )

    def halo(piece):
        def rule(target, a, z):
            if z % 2 == 0 and a % 2 == 1:
                return (a + 1 + target, z)
            if z % 2 == 1 and a % 2 == 0:
                return (a - 2 + target, z)
            return None

        found = [move(piece, partial(rule, target)) for target in range(2)]
        return jnp.where(core == 0, found[0], found[1])

    def window(own, margin, size, step):
        edge = jnp.where(odd == 0, own[-margin:], own[:margin])
        side = halo(edge)
        joined = jnp.concatenate([side, ordered(own, swap(own)), side], axis=0)
        return lax.dynamic_slice_in_dim(joined, odd * step, size, 0)

    hidden_rows = window(pick(hidden, batch), swing, rows, tok_rows)
    lengths = pick(token_lengths, batch)
    counts = pick(frame_counts, batch)
    items = jnp.arange(lengths.shape[0], dtype=jnp.int32)
    tok_lo = jnp.sum(jnp.where(items < item, lengths, 0)) - (tok_rows * item - swing)
    tok_hi = tok_lo + jnp.sum(jnp.where(items == item, lengths, 0))
    frame_start = frame_rows * item - jnp.where(odd == 0, near, far)
    frame_lo = jnp.sum(jnp.where(items < item, counts, 0)) - frame_start
    frame_hi = frame_lo + jnp.sum(jnp.where(items == item, counts, 0))
    here = chip if relay else jnp.zeros((), jnp.int32)
    scalars = jnp.stack([here, tok_lo, tok_hi, frame_lo, frame_hi]).astype(jnp.int32)

    def group(stack, out):
        parts = [stack[0], stack[1], stack[2], out.T]
        return jnp.concatenate(parts, axis=1)

    pieces = [
        group(self_proj, out_proj[0]),
        group(cross_proj, out_proj[1]),
        fc_in,
        fc_out.T,
    ]
    sizes = [piece.shape[1] for piece in pieces]
    own_piece = jnp.concatenate(pieces, axis=1)
    partner_piece = move(own_piece, lambda a, z: (a ^ 1, z) if a % 2 != z // 2 else None)
    chip_piece = ordered(own_piece, partner_piece)

    def spread(value):
        def rule(step, a, z):
            return (a, z ^ step) if a % 2 == z // 2 else None

        got = [None] + [move(value, partial(rule, step)) for step in (1, 2, 3)]
        same = jnp.where(core == batch, value, got[2])
        across = jnp.where(core == batch, got[1], got[3])
        return jnp.where(odd == 0, same, across), jnp.where(odd == 0, across, same)

    def gathered(index):
        start = sum(sizes[:index])
        first, second = spread(chip_piece[:, start : start + sizes[index]])
        splits = 4 if index < 2 else 1
        joined = jnp.stack(
            [x.reshape(2 * shard, splits, -1) for x in (first, second)], axis=2
        ).reshape(2 * shard, 2 * sizes[index])
        if relay:
            half = shard
            side_x = move(joined, lambda a, z: (a ^ 2, z))
            side_y = move(joined, lambda a, z: (a ^ 4, z))
            far_one = move(side_y[:half], lambda a, z: (a ^ 2, z))
            far_two = move(side_x[half:], lambda a, z: (a ^ 4, z))
            return [joined, side_x, side_y, jnp.concatenate([far_one, far_two], axis=0)]
        groups = [list(range(k, wide, 2)) for k in range(2)]
        full = lax.all_gather(joined, "wide", axis=0, tiled=True, axis_index_groups=groups)
        return [full[width // 4 * j : width // 4 * (j + 1)] for j in range(4)]

    bias_vector = jnp.concatenate([head_bias.reshape(-1), fc_bias])
    all_bias = lax.all_gather(bias_vector, "narrow", axis=0, tiled=False)
    core_bias = lax.dynamic_slice_in_dim(all_bias, 2 * core, 2, 0)
    biases = jnp.swapaxes(core_bias[:, : head_bias.size].reshape(2, 4, heads_cols), 0, 1).reshape(4, cols)
    fc_biases = core_bias[:, head_bias.size :].reshape(1, units)

    self_w = gathered(0)
    cross_w = gathered(1)
    in_w = gathered(2)
    back_w = gathered(3)

    frame_window = window(pick(encoded, batch), near, frames, 2 * near)
    place = jnp.arange(rows, dtype=jnp.int32)[:, None]
    valid = (place >= tok_lo) & (place < tok_hi)
    top_rows = jnp.where(
        valid, window(pick(cotangent, batch), swing, rows, tok_rows), jnp.zeros((), BF16)
    )

    act_shape = shape((rows, width), BF16)
    wide_f32 = shape((rows, width), F32)
    head_b = shape((pairs, rows, LANES), BF16)
    head_f = shape((pairs, rows, LANES), F32)
    frame_b = shape((pairs, frames, LANES), BF16)
    weight_scratch = [pltpu.VMEM((width, 4 * cols), BF16), pltpu.SemaphoreType.DMA((4,))]

    low_one, self_q, self_k, self_v, self_o, self_den, part = kernel_call(
        self_forward,
        "self_forward",
        (scalars, hidden_rows, ln_gain, ln_bias, biases, *self_w),
        [SMEM] + [VMEM] * 4 + [ANY] * 4,
        [act_shape, head_b, head_b, head_b, head_f, head_f, act_shape],
        scratch=weight_scratch,
    )
    other = swap(part)
    cross_k, cross_v = kernel_call(
        frame_project,
        "frame_project",
        (scalars, frame_window, biases, *cross_w),
        [SMEM] + [VMEM] * 2 + [ANY] * 4,
        [frame_b, frame_b],
        scratch=weight_scratch,
    )
    resid_one, low_two, cross_q, cross_o, cross_den, part_two = kernel_call(
        cross_forward,
        "cross_forward",
        (scalars, hidden_rows, part, other, ln_gain, ln_bias, out_bias, biases, cross_k, cross_v, *cross_w),
        [SMEM] + [VMEM] * 9 + [ANY] * 4,
        [wide_f32, act_shape, head_b, head_f, head_f, act_shape],
        scratch=weight_scratch,
    )
    other_two = swap(part_two)
    resid_two, low_three, low_act, grad_pre, part_three, back_three, unit_sums = kernel_call(
        unit_forward,
        "unit_forward",
        (scalars, resid_one, part_two, other_two, ln_gain, ln_bias, out_bias, fc_biases, top_rows, *in_w, *back_w),
        [SMEM] + [VMEM] * 8 + [ANY] * 8,
        [
            wide_f32, act_shape, shape((rows, units), BF16), shape((rows, units), BF16),
            act_shape, act_shape, shape((1, units), F32),
        ],
        scratch=[weight_scratch[0]] * 2 + [weight_scratch[1]] * 2,
    )
    other_back = swap(back_three)
    other_three = swap(part_three)
    grad_block = [shape((width // 4, 4 * cols), BF16)] * 4

    def grads_of(layout, name, *operands):
        return kernel_call(
            partial(weight_grads, layout),
            name,
            (scalars, *operands),
            [SMEM] + [VMEM] * len(operands),
            grad_block,
            [ANY] * 4,
            scratch=weight_scratch,
        )

    back_grads = grads_of(((0, 1),), "back_grads", top_rows, low_act)
    in_grads = grads_of(((0, 1),), "in_grads", low_three, grad_pre)
    final = kernel_call(
        finish_output,
        "finish_output",
        (scalars, resid_two, part_three, other_three, out_bias),
        [SMEM] + [VMEM] * 4,
        [act_shape],
    )[0]
    sums_shape = shape((8, width), F32)
    heads_shape = shape((8, cols), F32)
    drop_scratch = [pltpu.VMEM((pairs, rows, LANES), BF16)]
    grad_two, low_grad_two, low_cross, cq_grad, ck_grad, cv_grad, back_two, sums_two, heads_two = kernel_call(
        cross_backward,
        "cross_backward",
        (scalars, resid_two, top_rows, back_three, other_back, ln_gain, cross_q, cross_k, cross_v, cross_o, cross_den, *cross_w),
        [SMEM] + [VMEM] * 10 + [ANY] * 4,
        [wide_f32, act_shape, shape((rows, cols), BF16), head_b, frame_b, frame_b, act_shape, sums_shape, heads_shape],
        scratch=drop_scratch + weight_scratch,
    )
    other_back_two = swap(back_two)
    frame_part = kernel_call(
        frame_backward,
        "frame_backward",
        (scalars, ck_grad, cv_grad, *cross_w),
        [SMEM] + [VMEM] * 2 + [ANY] * 4,
        [shape((frames, width), BF16)],
        scratch=weight_scratch,
    )[0]
    cross_grads = grads_of(
        ((0, 1), (2, 3), (2, 4), (5, 6)),
        "cross_grads",
        low_two, cq_grad, frame_window, ck_grad, cv_grad, low_grad_two, low_cross,
    )
    grad_one, low_grad_one, low_self, sq_grad, sk_grad, sv_grad, back_one, sums_one, heads_one = kernel_call(
        self_backward,
        "self_backward",
        (scalars, resid_one, grad_two, back_two, other_back_two, ln_gain, self_q, self_k, self_v, self_o, self_den, *self_w),
        [SMEM] + [VMEM] * 10 + [ANY] * 4,
        [wide_f32, act_shape, shape((rows, cols), BF16), head_b, head_b, head_b, act_shape, sums_shape, heads_shape],
        scratch=drop_scratch + weight_scratch,
    )
    other_back_one = swap(back_one)
    self_grads = grads_of(
        ((0, 1), (0, 2), (0, 3), (4, 5)),
        "self_grads",
        low_one, sq_grad, sk_grad, sv_grad, low_grad_one, low_self,
    )
    input_rows, sums_zero = kernel_call(
        input_backward,
        "input_backward",
        (hidden_rows, grad_one, back_one, other_back_one, ln_gain),
        [VMEM] * 5,
        [act_shape, sums_shape],
    )

    main = core == odd

    def to_slices(middle, before, after):
        def head_rule(a, z):
            if a % 2 == z % 2:
                return None
            return (a, z ^ 1) if z % 2 == 1 else (a - 2, z ^ 1)

        def tail_rule(a, z):
            if a % 2 == z % 2:
                return None
            return (a, z ^ 1) if z % 2 == 0 else (a + 2, z ^ 1)

        from_above = move(before, head_rule)
        from_below = move(after, tail_rule)
        gap = jnp.zeros((middle.shape[0] - before.shape[0], middle.shape[1]), middle.dtype)
        lower = jnp.concatenate([gap, from_above], axis=0)
        gap = jnp.zeros((middle.shape[0] - after.shape[0], middle.shape[1]), middle.dtype)
        return middle + lower + jnp.concatenate([from_below, gap], axis=0)

    def to_copies(block, dtype):
        def rule(step, a, z):
            return (a, z ^ step) if a % 2 == z % 2 else None

        got = [None] + [move(block, partial(rule, step)) for step in (1, 2, 3)]
        near_copy = jnp.where(main, block, got[1]).astype(dtype)
        far_copy = jnp.where(main, got[2], got[3]).astype(dtype)
        return jnp.stack([jnp.where(batch == 0, near_copy, far_copy), jnp.where(batch == 0, far_copy, near_copy)])

    def token_output(block, dtype):
        mid = block[swing : swing + tok_rows]
        return to_copies(to_slices(mid, block[:swing], block[swing + tok_rows :]), dtype)

    output = token_output(final, BF16)
    input_grad = token_output(input_rows, F32)

    lead = jnp.where(odd == 0, near, far)
    mid_part = lax.dynamic_slice_in_dim(frame_part, lead, frame_rows, 0)
    outer_part = jnp.where(
        odd == 0,
        jnp.concatenate([frame_part[:near], frame_part[near + frame_rows :]], axis=0),
        jnp.concatenate([frame_part[far + frame_rows :], frame_part[:far]], axis=0),
    )
    kept = jnp.where(main, mid_part, outer_part)
    given = jnp.where(main, outer_part, mid_part)
    half_sum = (kept.astype(F32) + swap(given).astype(F32)).astype(BF16)

    def frame_cross_rule(a, z):
        if a % 2 == z % 2:
            return None
        return (a - 2, z ^ 1) if z % 2 == 0 else (a + 2, z ^ 1)

    def frame_pair_rule(a, z):
        return None if a % 2 == z % 2 else (a, z ^ 1)

    from_near = move(half_sum[:near], frame_cross_rule)
    from_far = move(half_sum[near:], frame_pair_rule)
    first_rows = jnp.concatenate([from_far, jnp.zeros((frame_rows - far, width), BF16)], axis=0)
    last_rows = jnp.concatenate([jnp.zeros((frame_rows - near, width), BF16), from_near], axis=0)
    odd_first = jnp.concatenate([jnp.zeros((frame_rows - far, width), BF16), from_far], axis=0)
    odd_last = jnp.concatenate([from_near, jnp.zeros((frame_rows - near, width), BF16)], axis=0)
    extra = jnp.where(odd == 1, first_rows + last_rows, odd_first + odd_last)
    encoded_grad = to_copies(half_sum + extra, F32)

    def scattered(blocks, index):
        half = shard
        if relay:
            got_x = move(blocks[3][half:], lambda a, z: (a ^ 2, z))
            got_y = move(blocks[3][:half], lambda a, z: (a ^ 4, z))
            to_x = jnp.concatenate([(blocks[1][:half].astype(F32) + got_y.astype(F32)).astype(BF16), blocks[1][half:]], axis=0)
            to_y = jnp.concatenate([blocks[2][:half], (blocks[2][half:].astype(F32) + got_x.astype(F32)).astype(BF16)], axis=0)
            from_x = move(to_x, lambda a, z: (a ^ 2, z))
            from_y = move(to_y, lambda a, z: (a ^ 4, z))
            total = blocks[0].astype(F32) + from_x.astype(F32) + from_y.astype(F32)
        else:
            groups = [list(range(k, wide, 2)) for k in range(2)]
            total = lax.psum_scatter(
                jnp.concatenate(blocks, axis=0), "wide", scatter_dimension=0, tiled=True, axis_index_groups=groups
            ).astype(F32)
        splits = 4 if index < 2 else 1
        parts = total.astype(BF16).reshape(2 * shard, splits, 2, -1)
        parts = [parts[:, :, k].reshape(2 * shard, -1) for k in range(2)]
        same = jnp.where(odd == 0, parts[0], parts[1])
        across = jnp.where(odd == 0, parts[1], parts[0])

        def rule(step, a, z):
            return (a, z ^ step) if a % 2 == (z ^ step) // 2 else None

        got = [move(across if step != 2 else same, partial(rule, step)) for step in (1, 2, 3)]
        summed = same.astype(F32) + got[0].astype(F32) + got[1].astype(F32) + got[2].astype(F32)
        keep = jnp.where(core == 0, summed[:shard], summed[shard:])
        give = jnp.where(core == 0, summed[shard:], summed[:shard])
        passed = move(give, lambda a, z: (a ^ 1, z) if a % 2 == z // 2 else None)
        return jnp.where(core == batch, keep, passed)

    grad_back = scattered(back_grads, 3)
    grad_in = scattered(in_grads, 2)
    grad_cross = scattered(cross_grads, 1)
    grad_self = scattered(self_grads, 0)

    def unpacked(grad):
        stack = jnp.stack([grad[:, heads_cols * k : heads_cols * (k + 1)] for k in range(3)])
        return stack, grad[:, 3 * heads_cols :].T

    grad_self_proj, grad_out_one = unpacked(grad_self)
    grad_cross_proj, grad_out_two = unpacked(grad_cross)

    only = jnp.where(core == 0, 1.0, 0.0)
    head_rows = jnp.stack([heads_one[0], heads_one[1], heads_two[0], heads_two[1]])
    head_full = lax.dynamic_update_slice(
        jnp.zeros((4, depth * heads_cols), F32), head_rows, (0, cols * core)
    )
    unit_full = lax.dynamic_update_slice(jnp.zeros((1, 2 * units), F32), unit_sums, (0, units * core))
    vectors = jnp.concatenate(
        [
            jnp.stack([sums_zero[0], sums_one[0], sums_two[0], sums_zero[1], sums_one[1], sums_two[1], sums_one[2], sums_two[3], sums_two[2]]).reshape(-1) * only,
            head_full.reshape(-1),
            unit_full.reshape(-1),
        ]
    )
    vectors = lax.psum(vectors, AXES)
    grad_gain = vectors[: 3 * width].reshape(3, width)
    grad_shift = vectors[3 * width : 6 * width].reshape(3, width)
    grad_outs = vectors[6 * width : 9 * width].reshape(3, width)
    grad_heads = vectors[9 * width : 9 * width + 4 * depth * heads_cols].reshape(4, depth * heads_cols)
    grad_heads = lax.dynamic_slice_in_dim(grad_heads, heads_cols * n, heads_cols, 1)
    grad_units = vectors[9 * width + 4 * depth * heads_cols :]
    grad_units = lax.dynamic_slice_in_dim(grad_units, units // 2 * n, units // 2, 0)
    return (
        output,
        input_grad,
        encoded_grad,
        grad_gain,
        grad_shift,
        grad_heads,
        grad_outs,
        grad_units,
        grad_self_proj,
        grad_cross_proj,
        jnp.stack([grad_out_one, grad_out_two]),
        grad_in,
        grad_back.T,
    )


def solution(mesh):
    in_specs = (
        P(None, "wide", None),
        P(None, "wide", None),
        P(),
        P(),
        P(),
        P(),
        P(None, "narrow"),
        P(),
        P("narrow"),
        P(None, "wide", "narrow"),
        P(None, "wide", "narrow"),
        P(None, "narrow", "wide"),
        P("wide", "narrow"),
        P("narrow", "wide"),
        P(None, "wide", None),
    )
    out_specs = (
        P(None, "wide", None),
        P(None, "wide", None),
        P(None, "wide", None),
        P(),
        P(),
        P(None, "narrow"),
        P(),
        P("narrow"),
        P(None, "wide", "narrow"),
        P(None, "wide", "narrow"),
        P(None, "narrow", "wide"),
        P("wide", "narrow"),
        P("narrow", "wide"),
    )
    return jax.shard_map(body, mesh=mesh, in_specs=in_specs, out_specs=out_specs, check_vma=False)
```

```python
from functools import partial

import jax
import jax.numpy as jnp
from jax import lax
from jax.experimental import pallas as pl
from jax.experimental.pallas import tpu as pltpu
from jax.sharding import PartitionSpec as P

HD = 64
LANES = 128
MAXLEN = 448
JITTER = 156
EPSILON = 1e-05
F32 = jnp.float32
BF16 = jnp.bfloat16
NN = (((1,), (0,)), ((), ()))
NT = (((1,), (1,)), ((), ()))
TN = (((0,), (0,)), ((), ()))
AXES = ("wide", "narrow")


def mm(left, right, dims=NN):
    return lax.dot_general(left, right, dims, preferred_element_type=F32)


def normalise(values):
    centre = values - jnp.mean(values, axis=-1, keepdims=True)
    spread = jnp.mean(centre * centre, axis=-1, keepdims=True)
    inverse = lax.rsqrt(spread + EPSILON)
    return centre * inverse, inverse


def norm_back(grad_rows, unit_rows, inverse, gain):
    scaled = grad_rows * gain
    centred = scaled - jnp.mean(scaled, axis=-1, keepdims=True)
    return (centred - unit_rows * jnp.mean(scaled * unit_rows, axis=-1, keepdims=True)) * inverse


def erf(x):
    x = jnp.clip(x, -3.832506856900711, 3.832506856900711)
    x2 = x * x
    top = x2 * 0.00022905065861350646 + 0.0034082910107109506
    top = top * x2 + 0.050955695062380861
    top = top * x2 + 0.18520832239976145
    top = top * x2 + 1.128379143519084
    low = x2 * -1.1791602954361697e-7 + 0.000023547966471313185
    low = low * x2 + 0.0010179625278914885
    low = low * x2 + 0.014070470171167667
    low = low * x2 + 0.11098505178285362
    low = low * x2 + 0.49746925110067538
    low = low * x2 + 1.0
    return x * top / low


def fetch(scalars, blocks, whole, sems, mixed=False, column=0):
    rows = whole.shape[1] // 8
    copies = []
    for group in range(2):
        for chip in range(4):
            for half in range(2):
                first = (2 * group + half) * rows
                if len(blocks) == 4:
                    source, place = blocks[chip], jnp.bitwise_xor(scalars[0], chip)
                else:
                    source, place = blocks[0], chip
                    first += 4 * chip * rows
                    if mixed:
                        core = scalars[5]
                        first = 4 * jnp.bitwise_xor(core, half) + 2 * core + jnp.bitwise_xor(scalars[6], group)
                        first = pl.multiple_of(rows * (8 * chip + first), rows)
                at = 2 * rows * place + rows * jnp.bitwise_xor(scalars[5], half)
                copies.append(
                    pltpu.make_async_copy(
                        source.at[pl.ds(first, rows), pl.ds(column, whole.shape[2])],
                        whole.at[group, pl.ds(pl.multiple_of(at, rows), rows), :],
                        sems.at[len(copies)],
                    )
                )
    for copy in copies:
        copy.start()
    return copies


def first_half(shape):
    return lax.broadcasted_iota(jnp.int32, shape, len(shape) - 1) < HD


def lay_window(scalars, own, partner, halo, out, margin, other):
    size = own.shape[0]
    odd = scalars[6]
    main = scalars[7] == 1
    before = jnp.where(odd == 0, margin, other)
    out[pl.ds(pl.multiple_of(before, 32), size), :] = jnp.where(main, own[...], partner[...])
    near_side = jnp.where(main, partner[:other, :], own[:other, :])
    far_side = jnp.where(main, partner[size - other :, :], own[size - other :, :])

    @pl.when(odd == 0)
    def _():
        out[:margin, :] = halo[...]
        out[margin + size :, :] = near_side

    @pl.when(odd == 1)
    def _():
        out[other + size :, :] = halo[...]
        out[:other, :] = far_side


def valid_rows(scalars, rows):
    place = lax.broadcasted_iota(jnp.int32, (rows, 1), 0)
    return (place >= scalars[1]) & (place < scalars[2])


def both(first, second, at, size):
    return jnp.concatenate([first[:, at : at + size], second[:, at : at + size]], axis=1)


def bias_row(biases, at, size):
    parts = biases[:, at : at + size].astype(F32)
    rows = [parts[8 * g : 8 * g + 1] + parts[8 * g + 2 : 8 * g + 3] + parts[8 * g + 4 : 8 * g + 5] for g in range(2)]
    return jnp.concatenate(rows, axis=1)


def halves(refs, cols):
    joined = jnp.concatenate([refs[p] for p in range(refs.shape[0])], axis=1)
    return joined[:, :cols], joined[:, cols:]


def by_pairs(values, out):
    for p in range(out.shape[0]):
        out[p] = values[:, p * LANES : (p + 1) * LANES]


def attend(pairs, rows, allowed, guard, q_all, k_all, v_all, o_out, den_out):
    half = first_half((rows, LANES))
    zero = jnp.zeros((), BF16)

    def one_pair(p, carry):
        q_pair, k_pair, v_pair = q_all[p], k_all[p], v_all[p]
        outs, dens = [], []
        for keep in (half, jnp.logical_not(half)):
            raw = mm(jnp.where(keep, q_pair, zero), k_pair, NT)
            weights = jnp.where(allowed, jnp.exp(raw), 0.0)
            total = jnp.sum(weights, axis=1, keepdims=True)
            if guard:
                total = jnp.where(total > 0.0, total, 1.0)
            outs.append(mm(weights.astype(BF16), v_pair) / total)
            dens.append(jnp.broadcast_to(total, (rows, LANES)))
        o_out[p] = jnp.where(half, outs[0], outs[1])
        den_out[p] = jnp.where(half, dens[0], dens[1])
        return carry

    lax.fori_loop(0, pairs, one_pair, 0)


def out_product(o_all, whole, cols):
    first, second = halves(o_all, cols)
    first, second = first.astype(BF16), second.astype(BF16)
    return mm(first, whole[0, :, 3 * cols :], NT) + mm(second, whole[1, :, 3 * cols :], NT)


def self_forward(
    scalars, own, partner, halo, gains, shifts, biases, w0, w1, w2, w3,
    hidden_out, norm_out, q_out, k_out, v_out, o_out, den_out, part_out, whole, sems,
):
    copies = fetch(scalars, (w0, w1, w2, w3), whole, sems)
    rows = hidden_out.shape[0]
    pairs = q_out.shape[0]
    cols = pairs * LANES // 2
    margin = halo.shape[0]
    lay_window(scalars, own, partner, halo, hidden_out, margin, margin)
    unit, _ = normalise(hidden_out[...].astype(F32))
    norm = (unit * gains[0:1, :] + shifts[0:1, :]).astype(BF16)
    norm_out[...] = norm
    valid = valid_rows(scalars, rows)
    for copy in copies:
        copy.wait()
    first = mm(norm, whole[0, :, : 3 * cols])
    second = mm(norm, whole[1, :, : 3 * cols])
    query = (both(first, second, 0, cols) + bias_row(biases, 0 * cols, cols)).astype(BF16).astype(F32)
    by_pairs(jnp.where(valid, query * HD ** -0.5, 0.0).astype(BF16), q_out)
    by_pairs(both(first, second, cols, cols).astype(BF16), k_out)
    by_pairs((both(first, second, 2 * cols, cols) + bias_row(biases, 1 * cols, cols)).astype(BF16), v_out)
    q_place = lax.broadcasted_iota(jnp.int32, (rows, rows), 0)
    k_place = lax.broadcasted_iota(jnp.int32, (rows, rows), 1)
    allowed = (k_place <= q_place) & (k_place >= scalars[1])
    attend(pairs, rows, allowed, True, q_out, k_out, v_out, o_out, den_out)
    part_out[...] = out_product(o_out, whole, cols).astype(BF16)


def frame_project(
    mixed, scalars, own, partner, halo, biases, w0, frame_out, k_out, v_out, whole, sems
):
    copies = fetch(scalars, (w0,), whole, sems, mixed)
    pairs = k_out.shape[0]
    cols = pairs * LANES // 2
    margin = halo.shape[0]
    lay_window(scalars, own, partner, halo, frame_out, margin, own.shape[0] - margin)
    for copy in copies:
        copy.wait()
    first = mm(frame_out[...], whole[0, :, cols : 3 * cols])
    second = mm(frame_out[...], whole[1, :, cols : 3 * cols])
    by_pairs(both(first, second, 0, cols).astype(BF16), k_out)
    by_pairs((both(first, second, cols, cols) + bias_row(biases, 3 * cols, cols)).astype(BF16), v_out)


def cross_forward(
    mixed, scalars, hidden, mine, other, gains, shifts, outs_bias, biases, k_all, v_all, w0,
    resid_out, norm_out, q_out, o_out, den_out, part_out, whole, sems,
):
    copies = fetch(scalars, (w0,), whole, sems, mixed)
    rows = hidden.shape[0]
    pairs = q_out.shape[0]
    cols = pairs * LANES // 2
    summed = mine[...].astype(F32) + other[...].astype(F32)
    resid = hidden[...].astype(F32) + (summed + outs_bias[0:1, :])
    resid_out[...] = resid
    unit, _ = normalise(resid)
    norm = (unit * gains[1:2, :] + shifts[1:2, :]).astype(BF16)
    norm_out[...] = norm
    valid = valid_rows(scalars, rows)
    for copy in copies:
        copy.wait()
    query = jnp.concatenate([mm(norm, whole[0, :, :cols]), mm(norm, whole[1, :, :cols])], axis=1)
    query = (query + bias_row(biases, 2 * cols, cols)).astype(BF16).astype(F32)
    by_pairs(jnp.where(valid, query * HD ** -0.5, 0.0).astype(BF16), q_out)
    frame = lax.broadcasted_iota(jnp.int32, (1, k_all.shape[1]), 1)
    allowed = (frame >= scalars[3]) & (frame < scalars[4])
    attend(pairs, rows, allowed, False, q_out, k_all, v_all, o_out, den_out)
    part_out[...] = out_product(o_out, whole, cols).astype(BF16)


CHUNK = 256


def unit_forward(
    mixed, scalars, resid, mine, other, gains, shifts, outs_bias, fc_bias, own, partner, halo,
    w0,
    resid_out, norm_out, top_out, act_out, pre_out, part_out, back_out, sum_out, whole, sems,
):
    copies = fetch(scalars, (w0,), whole, sems, mixed, whole.shape[1])
    margin = halo.shape[0]
    lay_window(scalars, own, partner, halo, top_out, margin, margin)
    valid = valid_rows(scalars, resid.shape[0])
    top_out[...] = jnp.where(valid, top_out[...], jnp.zeros((), BF16))
    summed = mine[...].astype(F32) + other[...].astype(F32)
    resid_two = resid[...] + (summed + outs_bias[1:2, :])
    resid_out[...] = resid_two
    unit, _ = normalise(resid_two)
    norm_out[...] = (unit * gains[2:3, :] + shifts[2:3, :]).astype(BF16)
    for copy in copies:
        copy.wait()
    units = act_out.shape[1] // 2
    steps = units // CHUNK

    def one_chunk(j, carry):
        group = j // steps
        at_in = pl.ds(pl.multiple_of((j - group * steps) * CHUNK, CHUNK), CHUNK)
        at_back = pl.ds(pl.multiple_of(units + (j - group * steps) * CHUNK, CHUNK), CHUNK)
        at = pl.ds(pl.multiple_of(j * CHUNK, CHUNK), CHUNK)
        parts = fc_bias[:, at_in].astype(F32)
        parts = jnp.where(group == 0, parts[:8], parts[8:])
        pre = mm(norm_out[...], whole[group, :, at_in]) + (parts[1:2] + parts[3:4] + parts[5:6])
        cdf = 0.5 * (1.0 + erf(pre * 0.7071067811865476))
        act_out[:, at] = (pre * cdf).astype(BF16)
        slope = cdf + pre * (jnp.exp(-0.5 * pre * pre) * 0.3989422804014327)
        grad = (slope * mm(top_out[...], whole[group, :, at_back])).astype(BF16)
        pre_out[:, at] = grad
        sum_out[:, at] = jnp.sum(grad.astype(F32), axis=0, keepdims=True)
        return carry

    lax.fori_loop(0, 2 * steps, one_chunk, 0)
    back_out[...] = (
        mm(pre_out[:, :units], whole[0, :, :units], NT) + mm(pre_out[:, units:], whole[1, :, :units], NT)
    ).astype(BF16)
    part_out[...] = (
        mm(act_out[:, :units], whole[0, :, units:], NT) + mm(act_out[:, units:], whole[1, :, units:], NT)
    ).astype(BF16)


def send_rows(scalars, total, mid_out, pair_out, cross_out):
    margin = pair_out.shape[0]
    size = mid_out.shape[0]
    odd = scalars[6] == 1
    low = total.astype(BF16)
    head = low[:margin]
    tail = low[margin + size :]
    mid_out[...] = low[margin : margin + size]
    pair_out[...] = jnp.where(odd, head, tail)
    cross_out[...] = jnp.where(odd, tail, head)


def finish_output(scalars, resid, mine, other, outs_bias, mid_out, pair_out, cross_out):
    summed = mine[...].astype(F32) + other[...].astype(F32)
    total = resid[...] + (summed + outs_bias[2:3, :])
    total = jnp.where(valid_rows(scalars, resid.shape[0]), total, 0.0)
    send_rows(scalars, total, mid_out, pair_out, cross_out)


def column_sum(values):
    return jnp.sum(values, axis=0, keepdims=True)


def attend_back(pairs, rows, allowed, drop, q_all, k_all, v_all, o_all, den_all, dq_out, dk_out, dv_out):
    count = k_all.shape[1]
    half = first_half((count, LANES))
    zero = jnp.zeros((), BF16)
    upper = lax.broadcasted_iota(jnp.int32, (LANES, rows), 0) < HD

    def one_pair(p, carry):
        q_pair, k_pair, v_pair = q_all[p], k_all[p], v_all[p]
        grad = drop[p].astype(F32)
        den = den_all[p]
        grad_sums = (grad / den).astype(BF16)
        drift_all = (grad * o_all[p] / den).T
        found = []
        for t in range(2):
            keep = half if t == 0 else jnp.logical_not(half)
            drift = jnp.sum(drift_all[t * HD : (t + 1) * HD, :], axis=0, keepdims=True)
            raw = mm(jnp.where(keep, k_pair, zero), q_pair, NT)
            weights = jnp.where(allowed, jnp.exp(raw), 0.0)
            prob = mm(jnp.where(keep, v_pair, zero), grad_sums, NT)
            score = (weights * (prob - drift)).astype(BF16)
            found.append(
                (
                    mm(k_pair, score, TN),
                    mm(score, q_pair),
                    mm(weights.astype(BF16), grad_sums),
                )
            )
        dq_out[p] = (jnp.where(upper, found[0][0], found[1][0]).T * HD ** -0.5).astype(BF16)
        dk_out[p] = jnp.where(half, found[0][1], found[1][1]).astype(dk_out.dtype)
        dv_out[p] = jnp.where(half, found[0][2], found[1][2]).astype(dv_out.dtype)
        return carry

    lax.fori_loop(0, pairs, one_pair, 0)


def open_gradient(grad, whole, o_all, grad_out, low_out, att_out, drop, copies):
    pairs = drop.shape[0]
    cols = pairs * LANES // 2
    grad_out[...] = grad
    low = grad.astype(BF16)
    low_out[...] = low
    for p in range(pairs):
        att_out[:, p * LANES : (p + 1) * LANES] = o_all[p].astype(BF16)
    for copy in copies:
        copy.wait()
    first = mm(low, whole[0, :, 3 * cols :]).astype(BF16)
    second = mm(low, whole[1, :, 3 * cols :]).astype(BF16)
    by_pairs(jnp.concatenate([first, second], axis=1), drop)


def head_sums(dq_out, dv_out, heads_out):
    for p in range(dq_out.shape[0]):
        heads_out[0:1, p * LANES : (p + 1) * LANES] = column_sum(dq_out[p].astype(F32))
        heads_out[1:2, p * LANES : (p + 1) * LANES] = column_sum(dv_out[p].astype(F32))


def cross_backward(
    mixed, scalars, resid, cotangent, mine, other, gains, q_all, k_all, v_all, o_all, den_all,
    w0,
    grad_out, low_out, att_out, dq_out, dk_out, dv_out, part_out, sums_out, heads_out,
    drop, whole, sems,
):
    copies = fetch(scalars, (w0,), whole, sems, mixed)
    rows = resid.shape[0]
    pairs = q_all.shape[0]
    cols = pairs * LANES // 2
    unit, inverse = normalise(resid[...])
    grad_norm = mine[...].astype(F32) + other[...].astype(F32)
    top = cotangent[...].astype(F32)
    grad = top + norm_back(grad_norm, unit, inverse, gains[2:3, :])
    sums_out[0:1, :] = column_sum(grad_norm * unit)
    sums_out[1:2, :] = column_sum(grad_norm)
    sums_out[2:3, :] = column_sum(top)
    sums_out[3:4, :] = column_sum(grad)
    open_gradient(grad, whole, o_all, grad_out, low_out, att_out, drop, copies)
    frame = lax.broadcasted_iota(jnp.int32, (k_all.shape[1], 1), 0)
    allowed = (frame >= scalars[3]) & (frame < scalars[4])
    attend_back(pairs, rows, allowed, drop, q_all, k_all, v_all, o_all, den_all, dq_out, dk_out, dv_out)
    first, second = halves(dq_out, cols)
    part_out[...] = (mm(first, whole[0, :, :cols], NT) + mm(second, whole[1, :, :cols], NT)).astype(BF16)
    head_sums(dq_out, dv_out, heads_out)


def self_backward(
    scalars, resid, top, mine, other, gains, q_all, k_all, v_all, o_all, den_all,
    w0, w1, w2, w3,
    grad_out, low_out, att_out, dq_out, dk_out, dv_out, part_out, sums_out, heads_out,
    drop, whole, sems,
):
    copies = fetch(scalars, (w0, w1, w2, w3), whole, sems)
    rows = resid.shape[0]
    pairs = q_all.shape[0]
    cols = pairs * LANES // 2
    unit, inverse = normalise(resid[...])
    grad_norm = mine[...].astype(F32) + other[...].astype(F32)
    grad = top[...] + norm_back(grad_norm, unit, inverse, gains[1:2, :])
    sums_out[0:1, :] = column_sum(grad_norm * unit)
    sums_out[1:2, :] = column_sum(grad_norm)
    sums_out[2:3, :] = column_sum(grad)
    open_gradient(grad, whole, o_all, grad_out, low_out, att_out, drop, copies)
    k_place = lax.broadcasted_iota(jnp.int32, (rows, rows), 0)
    q_place = lax.broadcasted_iota(jnp.int32, (rows, rows), 1)
    allowed = (k_place <= q_place) & (k_place >= scalars[1])
    attend_back(pairs, rows, allowed, drop, q_all, k_all, v_all, o_all, den_all, dq_out, dk_out, dv_out)
    pieces = [halves(piece, cols) for piece in (dq_out, dk_out, dv_out)]
    total = jnp.zeros((rows, part_out.shape[1]), F32)
    for group in range(2):
        joined = jnp.concatenate([piece[group] for piece in pieces], axis=1)
        total = total + mm(joined, whole[group, :, : 3 * cols], NT)
    part_out[...] = total.astype(BF16)
    head_sums(dq_out, dv_out, heads_out)


def input_backward(
    scalars, hidden, top, mine, other, gains, sums_one, sums_two, heads_one, heads_two, unit_sums,
    mid_out, pair_out, cross_out, vec_out,
):
    unit, inverse = normalise(hidden[...].astype(F32))
    grad_norm = mine[...].astype(F32) + other[...].astype(F32)
    grad = top[...] + norm_back(grad_norm, unit, inverse, gains[0:1, :])
    send_rows(scalars, grad, mid_out, pair_out, cross_out)
    heads = [heads_one[0:1, :], heads_one[1:2, :], heads_two[0:1, :], heads_two[1:2, :]]
    cols = heads[0].shape[1] // 2
    units = unit_sums.shape[1] // 2
    own = jnp.concatenate([row[:, :cols] for row in heads], axis=1)
    rest = jnp.concatenate([row[:, cols:] for row in heads], axis=1)
    own_units, rest_units = unit_sums[:, :units], unit_sums[:, units:]
    odd = scalars[6] == 1
    rows = [
        column_sum(grad_norm * unit), sums_one[0:1, :], sums_two[0:1, :],
        column_sum(grad_norm), sums_one[1:2, :], sums_two[1:2, :],
        sums_one[2:3, :], sums_two[3:4, :], sums_two[2:3, :],
        jnp.where(odd, rest, own), jnp.where(odd, rest_units, own_units),
        jnp.where(odd, own, rest), jnp.where(odd, own_units, rest_units),
    ]
    for k, row in enumerate(rows):
        vec_out[k : k + 1, :] = row
    vec_out[len(rows) :, :] = jnp.zeros((vec_out.shape[0] - len(rows), vec_out.shape[1]), F32)


def frame_backward(mixed, scalars, dk_all, dv_all, w0, kept_out, given_out, total, whole, sems):
    copies = fetch(scalars, (w0,), whole, sems, mixed)
    pairs = dk_all.shape[0]
    cols = pairs * LANES // 2
    size = kept_out.shape[0]
    frames = dk_all.shape[1]
    near = (frames - size) * 3 // 8
    far = frames - size - near
    keys = halves(dk_all, cols)
    values = halves(dv_all, cols)
    for copy in copies:
        copy.wait()
    for group in range(2):
        joined = jnp.concatenate([keys[group], values[group]], axis=1)
        part = mm(joined, whole[group, :, cols : 3 * cols], NT)
        total[...] = part if group == 0 else total[...] + part
    odd = scalars[6]
    main = scalars[7] == 1
    lead = pl.multiple_of(jnp.where(odd == 0, near, far), 32)
    near_at = pl.multiple_of(jnp.where(odd == 0, 0, far + size), 32)
    far_at = pl.multiple_of(jnp.where(odd == 0, near + size, 0), 32)
    mid = total[pl.ds(lead, size), :].astype(BF16)
    near_part = total[pl.ds(near_at, near), :].astype(BF16)
    far_part = total[pl.ds(far_at, far), :].astype(BF16)

    @pl.when(main)
    def _():
        kept_out[...] = mid
        given_out[:near, :] = near_part
        given_out[near:, :] = far_part

    @pl.when(jnp.logical_not(main))
    def _():
        given_out[...] = mid
        kept_out[:near, :] = near_part
        kept_out[near:, :] = far_part


def send_grads(scalars, whole, out, sems, extra=None):
    rows = whole.shape[1] // 8
    added = 0 if extra is None else extra.shape[0]
    copies = []
    for chip in range(4):
        start = chip * (4 * rows + added)
        for group in range(2):
            for half in range(2):
                at = 2 * rows * chip + rows * jnp.bitwise_xor(scalars[5], half)
                copies.append(
                    pltpu.make_async_copy(
                        whole.at[group, pl.ds(pl.multiple_of(at, rows), rows), :],
                        out.at[pl.ds(start + (2 * group + half) * rows, rows), :],
                        sems.at[len(copies)],
                    )
                )
        if added:
            copies.append(
                pltpu.make_async_copy(extra, out.at[pl.ds(start + 4 * rows, added), :], sems.at[len(copies)])
            )
    for copy in copies:
        copy.start()
    for copy in copies:
        copy.wait()


def unit_grads(scalars, norm, pre, top, act, out, whole, sems):
    units = pre.shape[1] // 2
    for group in range(2):
        at = slice(group * units, (group + 1) * units)
        whole[group, :, :units] = mm(norm[...], pre[:, at], TN).astype(BF16)
        whole[group, :, units:] = mm(top[...], act[:, at], TN).astype(BF16)
    send_grads(scalars, whole, out, sems)


def cross_grads(scalars, norm, frames, low, att, dq, dk, dv, vectors, out, low_vectors, whole, sems):
    low_vectors[...] = vectors[...].astype(BF16)
    cols = att.shape[1] // 2
    parts = [halves(piece, cols) for piece in (dq, dk, dv)]
    for group in range(2):
        at = slice(group * cols, (group + 1) * cols)
        joined = jnp.concatenate([parts[1][group], parts[2][group]], axis=1)
        found = [mm(norm[...], parts[0][group], TN), mm(frames[...], joined, TN), mm(low[...], att[:, at], TN)]
        whole[group] = jnp.concatenate(found, axis=1).astype(BF16)
    send_grads(scalars, whole, out, sems, low_vectors)


def self_grads(scalars, norm, low, att, dq, dk, dv, out, whole, sems):
    cols = att.shape[1] // 2
    parts = [halves(piece, cols) for piece in (dq, dk, dv)]
    for group in range(2):
        at = slice(group * cols, (group + 1) * cols)
        joined = jnp.concatenate([part[group] for part in parts], axis=1)
        found = [mm(norm[...], joined, TN), mm(low[...], att[:, at], TN)]
        whole[group] = jnp.concatenate(found, axis=1).astype(BF16)
    send_grads(scalars, whole, out, sems)


SMEM = pl.BlockSpec(memory_space=pltpu.SMEM)
VMEM = pl.BlockSpec(memory_space=pltpu.VMEM)
ANY = pl.BlockSpec(memory_space=pl.ANY)


def shape(dims, dtype):
    return jax.ShapeDtypeStruct(tuple(dims), dtype)


def kernel_call(kernel, name, cost, operands, spaces, outs, out_spaces=None, scratch=()):
    return pl.pallas_call(
        kernel,
        out_shape=tuple(outs),
        in_specs=list(spaces),
        out_specs=tuple(out_spaces or [VMEM] * len(outs)),
        scratch_shapes=list(scratch),
        compiler_params=pltpu.CompilerParams(vmem_limit_bytes=56 * 1024 * 1024),
        cost_estimate=pl.CostEstimate(flops=int(cost * 1e9), transcendentals=0, bytes_accessed=1 << 20),
        name=name,
    )(*operands)


def body(
    hidden, encoded, token_lengths, frame_counts, ln_gain, ln_bias, head_bias, out_bias, fc_bias,
    self_proj, cross_proj, out_proj, fc_in, fc_out, cotangent,
):
    wide = lax.axis_size("wide")
    depth = lax.axis_size("narrow")
    tok_rows, width = hidden.shape[1:]
    frame_rows = encoded.shape[1]
    swing = (MAXLEN - tok_rows) // 2
    ratio = frame_rows // tok_rows
    near = ratio * swing
    far = frame_rows - near
    assert far >= near + JITTER and 8 * near == 3 * frame_rows
    assert depth == 4 and hidden.shape[0] == 2
    rows = tok_rows + 2 * swing
    frames = near + frame_rows + far
    shard = width // wide
    block = 2 * shard
    head_cols = head_bias.shape[1]
    cols = 2 * head_cols
    pairs = cols // LANES
    hidden_units = fc_bias.shape[0]
    units = 2 * hidden_units

    w = lax.axis_index("wide")
    n = lax.axis_index("narrow")
    chip = w // 2
    core = w % 2
    batch = n // 2
    odd = n % 2
    item = 2 * chip + odd
    main = core == odd
    home = core == batch
    relay = wide == 8

    def move(value, rule):
        pairs_list = []
        for ws in range(wide):
            for ns in range(depth):
                target = rule(ws, ns)
                if target is not None and 0 <= target[0] < wide:
                    pairs_list.append((ws * depth + ns, target[0] * depth + target[1]))
        return lax.ppermute(value, AXES, pairs_list)

    def swap(value):
        return move(value, lambda a, z: (a ^ 1, z))

    def after(value, *events):
        return lax.optimization_barrier((value, *events))[0]

    def pick(value, index):
        return lax.dynamic_index_in_dim(value, index, 0, keepdims=False)

    bias_vector = jnp.concatenate([head_bias.reshape(-1), fc_bias])
    bias_high = lax.reduce_precision(bias_vector, 8, 7)
    bias_rest = bias_vector - bias_high
    bias_middle = lax.reduce_precision(bias_rest, 8, 7)
    bias_parts = jnp.stack([bias_high, bias_middle, bias_rest - bias_middle]).astype(BF16)
    bias_parts = jnp.concatenate([bias_parts.reshape(6, width), jnp.zeros((2, width), BF16)], axis=0)

    def group(stack, out):
        return jnp.concatenate([stack[0], stack[1], stack[2], out.T], axis=1)

    def away(value):
        return move(value, lambda a, z: (a ^ 1, z) if a % 2 != z // 2 else None)

    def two_groups(value):
        opposite = move(value, lambda a, z: (a, z ^ 2) if a % 2 == z // 2 else None)
        same = jnp.where(home, value, opposite)
        return same, move(same, lambda a, z: (a, z ^ 1))

    groups = [list(range(k, wide, 2)) for k in range(2)]

    def in_quarters(joined):
        if relay:
            return lax.all_gather(joined, "wide", axis=0, tiled=True, axis_index_groups=groups)
        size = joined.shape[1]
        full = lax.all_gather(joined.reshape(2, 2, shard, size), "wide", axis_index_groups=groups)
        full = jnp.where(core == 0, full, full[:, :, ::-1])
        full = jnp.swapaxes(full, 0, 1).reshape(2, 4, width // 4, size)
        return jnp.swapaxes(full, 0, 1).reshape(-1, size)

    def between_chips(joined, *events):
        if relay:
            joined = after(joined, *events)
            return [joined] + [move(joined, partial(lambda k, a, z: (a ^ k, z), 2 * k)) for k in (1, 2, 3)]
        full = in_quarters(joined)
        return [full[j * width // 2 : (j + 1) * width // 2] for j in range(4)]

    def edge(value, margin):
        start = jnp.where(odd == 0, value.shape[1] - margin, 0)
        return lax.dynamic_slice(value, (batch, start, 0), (1, margin, width))[0]

    def halo_rule(a, z):
        if a % 2 == z % 2:
            return None
        return (a + 1, z) if z % 2 == 0 else (a - 1, z)

    edges = jnp.concatenate([edge(hidden, swing), edge(cotangent, swing), edge(encoded, near)], axis=0)
    halo = move(edges, halo_rule)
    halo = jnp.where(main, halo, move(halo, lambda a, z: (a ^ 1, z) if a % 2 == z % 2 else None))
    hidden_halo, top_halo, frame_halo = halo[:swing], halo[swing : 2 * swing], halo[2 * swing :]

    rest_piece = jnp.concatenate([group(cross_proj, out_proj[1]), fc_in, fc_out.T], axis=1)
    if relay:
        rest_w = lax.all_gather(rest_piece, AXES, axis=0, tiled=True)
    else:
        rest_here = jnp.concatenate([rest_piece, away(rest_piece)], axis=0)
        rest_w = in_quarters(jnp.concatenate(two_groups(rest_here), axis=0))
    self_piece = group(self_proj, out_proj[0])
    self_got = two_groups(jnp.concatenate([self_piece, away(self_piece), bias_parts], axis=0))
    self_own = after(jnp.concatenate([x[:block] for x in self_got], axis=0), halo)
    self_w = between_chips(self_own)
    biases = jnp.concatenate([x[block:] for x in self_got], axis=0)

    own_hidden = pick(hidden, batch)
    own_top = pick(after(cotangent, self_own), batch)
    own_frames = pick(after(encoded, self_own), batch)
    token_lengths = after(token_lengths, self_own)
    lengths = pick(token_lengths, batch)
    counts = pick(frame_counts, batch)
    items = jnp.arange(lengths.shape[0], dtype=jnp.int32)
    tok_lo = jnp.sum(jnp.where(items < item, lengths, 0)) - (tok_rows * item - swing)
    tok_hi = tok_lo + jnp.sum(jnp.where(items == item, lengths, 0))
    frame_start = frame_rows * item - jnp.where(odd == 0, near, far)
    frame_lo = jnp.sum(jnp.where(items < item, counts, 0)) - frame_start
    frame_hi = frame_lo + jnp.sum(jnp.where(items == item, counts, 0))
    nothing = jnp.zeros((), jnp.int32)
    here, order = (chip, core) if relay else (nothing, nothing)
    scalars = jnp.stack(
        [here, tok_lo, tok_hi, frame_lo, frame_hi, order, odd, main.astype(jnp.int32)]
    ).astype(jnp.int32)

    low_shape = shape((rows, width), BF16)
    wide_f32 = shape((rows, width), F32)
    head_b = shape((pairs, rows, LANES), BF16)
    head_f = shape((pairs, rows, LANES), F32)
    frame_b = shape((pairs, frames, LANES), BF16)
    att_shape = shape((rows, cols), BF16)
    frame_full = shape((frames, width), BF16)
    sems = pltpu.SemaphoreType.DMA((20,))
    head_scratch = [pltpu.VMEM((2, width, width), BF16), sems]
    unit_scratch = [pltpu.VMEM((2, width, 2 * hidden_units), BF16), sems]

    hidden_rows, low_one, self_q, self_k, self_v, self_o, self_den, part = kernel_call(
        self_forward, "self_forward", 8,
        (scalars, own_hidden, swap(own_hidden), hidden_halo, ln_gain, ln_bias, biases, *self_w),
        [SMEM] + [VMEM] * 6 + [ANY] * 4,
        [low_shape, low_shape, head_b, head_b, head_b, head_f, head_f, low_shape],
        scratch=head_scratch,
    )
    frame_window, cross_k, cross_v = kernel_call(
        partial(frame_project, relay), "frame_project", 7,
        (scalars, own_frames, swap(own_frames), after(frame_halo, part), biases, rest_w),
        [SMEM] + [VMEM] * 4 + [ANY],
        [frame_full, frame_b, frame_b],
        scratch=head_scratch,
    )
    resid_one, low_two, cross_q, cross_o, cross_den, part_two = kernel_call(
        partial(cross_forward, relay), "cross_forward", 11,
        (scalars, hidden_rows, part, swap(part), ln_gain, ln_bias, out_bias, biases, cross_k, cross_v, rest_w),
        [SMEM] + [VMEM] * 9 + [ANY],
        [wide_f32, low_shape, head_b, head_f, head_f, low_shape],
        scratch=head_scratch,
    )
    act_shape = shape((rows, units), BF16)
    resid_two, low_three, top_rows, low_act, grad_pre, part_three, back_three, unit_sums = kernel_call(
        partial(unit_forward, relay), "unit_forward", 14,
        (scalars, resid_one, part_two, swap(part_two), ln_gain, ln_bias, out_bias, biases, own_top, swap(own_top), top_halo, rest_w),
        [SMEM] + [VMEM] * 10 + [ANY],
        [wide_f32, low_shape, low_shape, act_shape, act_shape, low_shape, low_shape, shape((1, units), F32)],
        scratch=unit_scratch,
    )
    other_back = swap(back_three)
    other_three = swap(part_three)

    def between_back(grads):
        if relay:
            return lax.psum_scatter(grads, "wide", scatter_dimension=0, tiled=True, axis_index_groups=groups)
        size = grads.shape[1]
        full = jnp.swapaxes(grads.reshape(4, 2, width // 4, size), 0, 1).reshape(2, wide // 2, 2, shard, size)
        full = jnp.swapaxes(jnp.where(core == 0, full, full[:, :, ::-1]), 0, 1)
        total = lax.psum_scatter(full, "wide", scatter_dimension=0, axis_index_groups=groups)
        return total.reshape(2 * block, size)

    def from_opposite(paired):
        return move(paired, lambda a, z: (a, z ^ 2) if a % 2 != z // 2 else None)

    def to_owner(paired, opposite):
        summed = paired.astype(F32) + opposite.astype(F32)
        passed = move(summed[shard:], lambda a, z: (a ^ 1, z) if a % 2 == z // 2 else None)
        return jnp.where(home, summed[:shard], passed)

    def grads_of(kernel, name, cost, size, scratch, *operands, added=0):
        return kernel_call(
            kernel, name, cost, (scalars, *operands),
            [SMEM] + [VMEM] * len(operands),
            [shape((2 * width + 4 * added, size), BF16)],
            [ANY],
            scratch=scratch,
        )[0]

    grads_unit = grads_of(
        unit_grads, "unit_grads", 9, 2 * hidden_units, unit_scratch, low_three, grad_pre, top_rows, low_act
    )
    unit_total = between_back(grads_unit)
    sums_shape = shape((8, width), F32)
    heads_shape = shape((8, cols), F32)
    drop_scratch = [pltpu.VMEM((pairs, rows, LANES), BF16)]
    grad_two, low_grad_two, low_cross, cq_grad, ck_grad, cv_grad, back_two, sums_two, heads_two = kernel_call(
        partial(cross_backward, relay), "cross_backward", 21,
        (scalars, resid_two, top_rows, back_three, after(other_back, grads_unit), ln_gain, cross_q, cross_k, cross_v, cross_o, cross_den, rest_w),
        [SMEM] + [VMEM] * 10 + [ANY],
        [wide_f32, low_shape, att_shape, head_b, frame_b, frame_b, low_shape, sums_shape, heads_shape],
        scratch=drop_scratch + head_scratch,
    )
    def cross_rule(a, z):
        if a % 2 == z % 2:
            return None
        return (a - 2, z ^ 1) if z % 2 == 0 else (a + 2, z ^ 1)

    def pair_rule(a, z):
        return None if a % 2 == z % 2 else (a, z ^ 1)

    def from_main(value, step):
        return move(value, lambda a, z: (a, z ^ step) if a % 2 == z % 2 else None)

    def per_batch(near_copy, far_copy, dtype):
        near_copy, far_copy = near_copy.astype(dtype), far_copy.astype(dtype)
        return jnp.stack(
            [jnp.where(batch == 0, near_copy, far_copy), jnp.where(batch == 0, far_copy, near_copy)]
        )

    def token_block(mid, from_pair, from_cross):
        above = jnp.where(odd == 1, from_pair, from_cross)
        below = jnp.where(odd == 1, from_cross, from_pair)
        return jnp.concatenate([mid[:swing] + above, mid[swing:-swing], mid[-swing:] + below], axis=0)

    edge_shape = shape((swing, width), BF16)
    slice_shapes = [shape((tok_rows, width), BF16), edge_shape, edge_shape]
    out_mid, out_pair, out_cross = kernel_call(
        finish_output, "finish_output", 3,
        (scalars, resid_two, part_three, after(other_three, grad_two), out_bias),
        [SMEM] + [VMEM] * 4,
        slice_shapes,
    )
    grad_one, low_grad_one, low_self, sq_grad, sk_grad, sv_grad, back_one, sums_one, heads_one = kernel_call(
        self_backward, "self_backward", 12,
        (scalars, resid_one, grad_two, back_two, after(swap(back_two), out_mid), ln_gain, self_q, self_k, self_v, self_o, self_den, *self_w),
        [SMEM] + [VMEM] * 10 + [ANY] * 4,
        [wide_f32, low_shape, att_shape, head_b, head_b, head_b, low_shape, sums_shape, heads_shape],
        scratch=drop_scratch + head_scratch,
    )
    kept, given = kernel_call(
        partial(frame_backward, relay), "frame_backward", 7,
        (scalars, after(ck_grad, back_one), cv_grad, rest_w),
        [SMEM] + [VMEM] * 2 + [ANY],
        [shape((frame_rows, width), BF16)] * 2,
        scratch=[pltpu.VMEM((frames, width), F32)] + head_scratch,
    )
    in_mid, in_pair, in_cross, vectors = kernel_call(
        input_backward, "input_backward", 4,
        (scalars, hidden_rows, grad_one, back_one, after(swap(back_one), kept), ln_gain, sums_one, sums_two, heads_one, heads_two, unit_sums),
        [SMEM] + [VMEM] * 10,
        slice_shapes + [shape((16, width), F32)],
    )
    grads_self = grads_of(
        self_grads, "self_grads", 5, width, head_scratch,
        after(low_one, in_mid), low_grad_one, low_self, sq_grad, sk_grad, sv_grad,
    )
    self_total = between_back(after(grads_self, unit_total))
    half_sum = (kept.astype(F32) + swap(given).astype(F32)).astype(BF16)
    half_sum = after(half_sum, grads_self)
    from_pair = move(jnp.concatenate([half_sum[near:], in_pair, out_pair], axis=0), pair_rule)
    from_cross = move(jnp.concatenate([half_sum[:near], in_cross, out_cross], axis=0), cross_rule)
    added = vectors.shape[0]
    grads_cross = grads_of(
        cross_grads, "cross_grads", 8, width, [pltpu.VMEM((added, width), BF16)] + head_scratch,
        low_two, frame_window, low_grad_two, low_cross, after(cq_grad, half_sum), ck_grad, cv_grad, vectors,
        added=added,
    )
    extra = jnp.where(
        odd == 1,
        jnp.concatenate([from_pair[:far], from_cross[:near]], axis=0),
        jnp.concatenate([from_cross[:near], from_pair[:far]], axis=0),
    )
    frame_block = after(half_sum + extra, grads_cross)
    token_rows = jnp.concatenate(
        [
            token_block(in_mid, from_pair[far:-swing], from_cross[near:-swing]),
            token_block(out_mid, from_pair[-swing:], from_cross[-swing:]),
        ],
        axis=0,
    )
    frame_opposite = from_main(frame_block, 2)
    frame_beside = from_main(frame_block, 1)
    if relay:
        cross_total = between_back(after(grads_cross, self_total, frame_beside))
    else:
        parts = grads_cross.reshape(4, -1, width)[:, : width // 2].reshape(-1, width)
        cross_total = jnp.concatenate(
            [between_back(parts), jnp.zeros((added, width), BF16)], axis=0
        )
    early = jnp.concatenate([unit_total, self_total], axis=1)
    early_across = move(after(early[block:], frame_beside), lambda a, z: (a, z ^ 1))
    early_paired = (early[:block].astype(F32) + early_across.astype(F32)).astype(BF16)
    token_rows = after(token_rows, frame_opposite)
    frame_third = from_main(frame_opposite, 1)
    token_opposite = from_main(token_rows, 2)
    token_beside = from_main(token_rows, 1)
    early_opposite = from_opposite(early_paired)
    cross_total = after(cross_total, early_paired)
    cross_across = move(cross_total[block:], lambda a, z: (a, z ^ 1))
    cross_paired = (cross_total[:block].astype(F32) + cross_across[:block].astype(F32)).astype(BF16)
    if relay:
        vectors = cross_total[2 * block :].astype(F32) + cross_across[block:].astype(F32)
        vectors = vectors + move(vectors, lambda a, z: (a, z ^ 2))
    else:
        vectors = lax.psum(lax.psum(vectors, "narrow"), "wide", axis_index_groups=groups)
    token_third = from_main(after(token_opposite, cross_paired), 1)
    cross_opposite = from_opposite(cross_paired)
    grad_early = to_owner(early_paired, after(early_opposite, cross_paired))
    grad_unit, grad_self = grad_early[:, : 2 * hidden_units], grad_early[:, 2 * hidden_units :]
    grad_cross = to_owner(cross_paired, cross_opposite)

    def copied(first, last, value, opposite, beside, third, dtype):
        near_copy = jnp.where(main, value[first:last], beside[first:last])
        far_copy = jnp.where(main, opposite[first:last], third[first:last])
        return per_batch(near_copy, far_copy, dtype)

    encoded_grad = copied(0, frame_rows, frame_block, frame_opposite, frame_beside, frame_third, F32)
    tokens = (token_rows, token_opposite, token_beside, token_third)
    input_grad = copied(0, tok_rows, *tokens, F32)
    output = copied(tok_rows, 2 * tok_rows, *tokens, BF16)

    def unpacked(grad):
        stack = jnp.stack([grad[:, head_cols * k : head_cols * (k + 1)] for k in range(3)])
        return stack, grad[:, 3 * head_cols :].T

    grad_self_proj, grad_out_one = unpacked(grad_self)
    grad_cross_proj, grad_out_two = unpacked(grad_cross)

    mine = lax.dynamic_slice_in_dim(vectors, 9 + 2 * odd, 2, 0)
    mine = jnp.where(home, mine, swap(mine))
    return (
        output,
        input_grad,
        encoded_grad,
        vectors[:3],
        vectors[3:6],
        mine[0].reshape(4, head_cols),
        vectors[6:9],
        mine[1],
        grad_self_proj,
        grad_cross_proj,
        jnp.stack([grad_out_one, grad_out_two]),
        grad_unit[:, :hidden_units],
        grad_unit[:, hidden_units:].T,
    )


def solution(mesh):
    in_specs = (
        P(None, "wide", None),
        P(None, "wide", None),
        P(),
        P(),
        P(),
        P(),
        P(None, "narrow"),
        P(),
        P("narrow"),
        P(None, "wide", "narrow"),
        P(None, "wide", "narrow"),
        P(None, "narrow", "wide"),
        P("wide", "narrow"),
        P("narrow", "wide"),
        P(None, "wide", None),
    )
    out_specs = (
        P(None, "wide", None),
        P(None, "wide", None),
        P(None, "wide", None),
        P(),
        P(),
        P(None, "narrow"),
        P(),
        P("narrow"),
        P(None, "wide", "narrow"),
        P(None, "wide", "narrow"),
        P(None, "narrow", "wide"),
        P("wide", "narrow"),
        P("narrow", "wide"),
    )
    return jax.shard_map(body, mesh=mesh, in_specs=in_specs, out_specs=out_specs, check_vma=False)
```

```python
from functools import partial

import jax
import jax.numpy as jnp
from jax import lax
from jax.experimental import pallas as pl
from jax.experimental.pallas import tpu as pltpu
from jax.sharding import PartitionSpec as P

HD = 64
LANES = 128
MAXLEN = 448
JITTER = 156
EPSILON = 1e-05
F32 = jnp.float32
BF16 = jnp.bfloat16
NN = (((1,), (0,)), ((), ()))
NT = (((1,), (1,)), ((), ()))
TN = (((0,), (0,)), ((), ()))
AXES = ("wide", "narrow")


def mm(left, right, dims=NN):
    return lax.dot_general(left, right, dims, preferred_element_type=F32)


def normalise(values):
    centre = values - jnp.mean(values, axis=-1, keepdims=True)
    spread = jnp.mean(centre * centre, axis=-1, keepdims=True)
    inverse = lax.rsqrt(spread + EPSILON)
    return centre * inverse, inverse


def norm_back(grad_rows, unit_rows, inverse, gain):
    scaled = grad_rows * gain
    centred = scaled - jnp.mean(scaled, axis=-1, keepdims=True)
    return (centred - unit_rows * jnp.mean(scaled * unit_rows, axis=-1, keepdims=True)) * inverse


def erf(x):
    x = jnp.clip(x, -3.832506856900711, 3.832506856900711)
    x2 = x * x
    top = x2 * 0.00022905065861350646 + 0.0034082910107109506
    top = top * x2 + 0.050955695062380861
    top = top * x2 + 0.18520832239976145
    top = top * x2 + 1.128379143519084
    low = x2 * -1.1791602954361697e-7 + 0.000023547966471313185
    low = low * x2 + 0.0010179625278914885
    low = low * x2 + 0.014070470171167667
    low = low * x2 + 0.11098505178285362
    low = low * x2 + 0.49746925110067538
    low = low * x2 + 1.0
    return x * top / low


def fetch(scalars, blocks, whole, sems, mixed=False, column=0):
    rows = whole.shape[1] // 8
    copies = []
    for group in range(2):
        for chip in range(4):
            for half in range(2):
                first = (2 * group + half) * rows
                if len(blocks) == 4:
                    source, place = blocks[chip], jnp.bitwise_xor(scalars[0], chip)
                else:
                    source, place = blocks[0], chip
                    first += 4 * chip * rows
                    if mixed:
                        core = scalars[5]
                        first = 4 * jnp.bitwise_xor(core, half) + 2 * core + jnp.bitwise_xor(scalars[6], group)
                        first = pl.multiple_of(rows * (8 * chip + first), rows)
                at = 2 * rows * place + rows * jnp.bitwise_xor(scalars[5], half)
                copies.append(
                    pltpu.make_async_copy(
                        source.at[pl.ds(first, rows), pl.ds(column, whole.shape[2])],
                        whole.at[group, pl.ds(pl.multiple_of(at, rows), rows), :],
                        sems.at[len(copies)],
                    )
                )
    for copy in copies:
        copy.start()
    return copies


def first_half(shape):
    return lax.broadcasted_iota(jnp.int32, shape, len(shape) - 1) < HD


def lay_window(scalars, own, partner, halo, out, margin, other):
    size = own.shape[0]
    odd = scalars[6]
    main = scalars[7] == 1
    before = jnp.where(odd == 0, margin, other)
    out[pl.ds(pl.multiple_of(before, 32), size), :] = jnp.where(main, own[...], partner[...])
    near_side = jnp.where(main, partner[:other, :], own[:other, :])
    far_side = jnp.where(main, partner[size - other :, :], own[size - other :, :])

    @pl.when(odd == 0)
    def _():
        out[:margin, :] = halo[...]
        out[margin + size :, :] = near_side

    @pl.when(odd == 1)
    def _():
        out[other + size :, :] = halo[...]
        out[:other, :] = far_side


def valid_rows(scalars, rows):
    place = lax.broadcasted_iota(jnp.int32, (rows, 1), 0)
    return (place >= scalars[1]) & (place < scalars[2])


def both(first, second, at, size):
    return jnp.concatenate([first[:, at : at + size], second[:, at : at + size]], axis=1)


def bias_row(biases, at, size):
    parts = biases[:, at : at + size].astype(F32)
    rows = [parts[8 * g : 8 * g + 1] + parts[8 * g + 2 : 8 * g + 3] + parts[8 * g + 4 : 8 * g + 5] for g in range(2)]
    return jnp.concatenate(rows, axis=1)


def halves(refs, cols):
    joined = jnp.concatenate([refs[p] for p in range(refs.shape[0])], axis=1)
    return joined[:, :cols], joined[:, cols:]


def by_pairs(values, out):
    for p in range(out.shape[0]):
        out[p] = values[:, p * LANES : (p + 1) * LANES]


def attend(pairs, rows, allowed, guard, q_all, k_all, v_all, o_out, den_out):
    half = first_half((rows, LANES))
    zero = jnp.zeros((), BF16)

    def one_pair(p, carry):
        q_pair, k_pair, v_pair = q_all[p], k_all[p], v_all[p]
        outs, dens = [], []
        for keep in (half, jnp.logical_not(half)):
            raw = mm(jnp.where(keep, q_pair, zero), k_pair, NT)
            weights = jnp.where(allowed, jnp.exp(raw), 0.0)
            total = jnp.sum(weights, axis=1, keepdims=True)
            if guard:
                total = jnp.where(total > 0.0, total, 1.0)
            outs.append(mm(weights.astype(BF16), v_pair) / total)
            dens.append(jnp.broadcast_to(total, (rows, LANES)))
        o_out[p] = jnp.where(half, outs[0], outs[1])
        den_out[p] = jnp.where(half, dens[0], dens[1])
        return carry

    lax.fori_loop(0, pairs, one_pair, 0)


def out_product(o_all, whole, cols):
    first, second = halves(o_all, cols)
    first, second = first.astype(BF16), second.astype(BF16)
    return mm(first, whole[0, :, 3 * cols :], NT) + mm(second, whole[1, :, 3 * cols :], NT)


def self_forward(
    scalars, own, partner, halo, gains, shifts, biases, w0, w1, w2, w3,
    hidden_out, norm_out, q_out, k_out, v_out, o_out, den_out, part_out, whole, sems,
):
    copies = fetch(scalars, (w0, w1, w2, w3), whole, sems)
    rows = hidden_out.shape[0]
    pairs = q_out.shape[0]
    cols = pairs * LANES // 2
    margin = halo.shape[0]
    lay_window(scalars, own, partner, halo, hidden_out, margin, margin)
    unit, _ = normalise(hidden_out[...].astype(F32))
    norm = (unit * gains[0:1, :] + shifts[0:1, :]).astype(BF16)
    norm_out[...] = norm
    valid = valid_rows(scalars, rows)
    for copy in copies:
        copy.wait()
    first = mm(norm, whole[0, :, : 3 * cols])
    second = mm(norm, whole[1, :, : 3 * cols])
    query = (both(first, second, 0, cols) + bias_row(biases, 0 * cols, cols)).astype(BF16).astype(F32)
    by_pairs(jnp.where(valid, query * HD ** -0.5, 0.0).astype(BF16), q_out)
    by_pairs(both(first, second, cols, cols).astype(BF16), k_out)
    by_pairs((both(first, second, 2 * cols, cols) + bias_row(biases, 1 * cols, cols)).astype(BF16), v_out)
    q_place = lax.broadcasted_iota(jnp.int32, (rows, rows), 0)
    k_place = lax.broadcasted_iota(jnp.int32, (rows, rows), 1)
    allowed = (k_place <= q_place) & (k_place >= scalars[1])
    attend(pairs, rows, allowed, True, q_out, k_out, v_out, o_out, den_out)
    part_out[...] = out_product(o_out, whole, cols).astype(BF16)


def frame_project(
    mixed, scalars, own, partner, halo, biases, w0, frame_out, k_out, v_out, whole, sems
):
    copies = fetch(scalars, (w0,), whole, sems, mixed)
    pairs = k_out.shape[0]
    cols = pairs * LANES // 2
    margin = halo.shape[0]
    lay_window(scalars, own, partner, halo, frame_out, margin, own.shape[0] - margin)
    for copy in copies:
        copy.wait()
    first = mm(frame_out[...], whole[0, :, cols : 3 * cols])
    second = mm(frame_out[...], whole[1, :, cols : 3 * cols])
    by_pairs(both(first, second, 0, cols).astype(BF16), k_out)
    by_pairs((both(first, second, cols, cols) + bias_row(biases, 3 * cols, cols)).astype(BF16), v_out)


def cross_forward(
    mixed, scalars, hidden, mine, other, gains, shifts, outs_bias, biases, k_all, v_all, w0,
    resid_out, norm_out, q_out, o_out, den_out, part_out, whole, sems,
):
    copies = fetch(scalars, (w0,), whole, sems, mixed)
    rows = hidden.shape[0]
    pairs = q_out.shape[0]
    cols = pairs * LANES // 2
    summed = mine[...].astype(F32) + other[...].astype(F32)
    resid = hidden[...].astype(F32) + (summed + outs_bias[0:1, :])
    resid_out[...] = resid
    unit, _ = normalise(resid)
    norm = (unit * gains[1:2, :] + shifts[1:2, :]).astype(BF16)
    norm_out[...] = norm
    valid = valid_rows(scalars, rows)
    for copy in copies:
        copy.wait()
    query = jnp.concatenate([mm(norm, whole[0, :, :cols]), mm(norm, whole[1, :, :cols])], axis=1)
    query = (query + bias_row(biases, 2 * cols, cols)).astype(BF16).astype(F32)
    by_pairs(jnp.where(valid, query * HD ** -0.5, 0.0).astype(BF16), q_out)
    frame = lax.broadcasted_iota(jnp.int32, (1, k_all.shape[1]), 1)
    allowed = (frame >= scalars[3]) & (frame < scalars[4])
    attend(pairs, rows, allowed, False, q_out, k_all, v_all, o_out, den_out)
    part_out[...] = out_product(o_out, whole, cols).astype(BF16)


CHUNK = 256


def unit_forward(
    mixed, scalars, resid, mine, other, gains, shifts, outs_bias, fc_bias, own, partner, halo,
    w0,
    resid_out, norm_out, top_out, act_out, pre_out, part_out, back_out, sum_out, whole, sems,
):
    copies = fetch(scalars, (w0,), whole, sems, mixed, whole.shape[1])
    margin = halo.shape[0]
    lay_window(scalars, own, partner, halo, top_out, margin, margin)
    valid = valid_rows(scalars, resid.shape[0])
    top_out[...] = jnp.where(valid, top_out[...], jnp.zeros((), BF16))
    summed = mine[...].astype(F32) + other[...].astype(F32)
    resid_two = resid[...] + (summed + outs_bias[1:2, :])
    resid_out[...] = resid_two
    unit, _ = normalise(resid_two)
    norm_out[...] = (unit * gains[2:3, :] + shifts[2:3, :]).astype(BF16)
    for copy in copies:
        copy.wait()
    units = act_out.shape[1] // 2
    steps = units // CHUNK

    def one_chunk(j, carry):
        group = j // steps
        at_in = pl.ds(pl.multiple_of((j - group * steps) * CHUNK, CHUNK), CHUNK)
        at_back = pl.ds(pl.multiple_of(units + (j - group * steps) * CHUNK, CHUNK), CHUNK)
        at = pl.ds(pl.multiple_of(j * CHUNK, CHUNK), CHUNK)
        parts = fc_bias[:, at_in].astype(F32)
        parts = jnp.where(group == 0, parts[:8], parts[8:])
        pre = mm(norm_out[...], whole[group, :, at_in]) + (parts[1:2] + parts[3:4] + parts[5:6])
        cdf = 0.5 * (1.0 + erf(pre * 0.7071067811865476))
        act_out[:, at] = (pre * cdf).astype(BF16)
        slope = cdf + pre * (jnp.exp(-0.5 * pre * pre) * 0.3989422804014327)
        grad = (slope * mm(top_out[...], whole[group, :, at_back])).astype(BF16)
        pre_out[:, at] = grad
        sum_out[:, at] = jnp.sum(grad.astype(F32), axis=0, keepdims=True)
        return carry

    lax.fori_loop(0, 2 * steps, one_chunk, 0)
    back_out[...] = (
        mm(pre_out[:, :units], whole[0, :, :units], NT) + mm(pre_out[:, units:], whole[1, :, :units], NT)
    ).astype(BF16)
    part_out[...] = (
        mm(act_out[:, :units], whole[0, :, units:], NT) + mm(act_out[:, units:], whole[1, :, units:], NT)
    ).astype(BF16)


def send_rows(scalars, total, mid_out, pair_out, cross_out):
    margin = pair_out.shape[0]
    size = mid_out.shape[0]
    odd = scalars[6] == 1
    low = total.astype(BF16)
    head = low[:margin]
    tail = low[margin + size :]
    mid_out[...] = low[margin : margin + size]
    pair_out[...] = jnp.where(odd, head, tail)
    cross_out[...] = jnp.where(odd, tail, head)


def finish_output(scalars, resid, mine, other, outs_bias, mid_out, pair_out, cross_out):
    summed = mine[...].astype(F32) + other[...].astype(F32)
    total = resid[...] + (summed + outs_bias[2:3, :])
    total = jnp.where(valid_rows(scalars, resid.shape[0]), total, 0.0)
    send_rows(scalars, total, mid_out, pair_out, cross_out)


def column_sum(values):
    return jnp.sum(values, axis=0, keepdims=True)


def attend_back(pairs, rows, allowed, drop, q_all, k_all, v_all, o_all, den_all, dq_out, dk_out, dv_out):
    count = k_all.shape[1]
    half = first_half((count, LANES))
    zero = jnp.zeros((), BF16)
    upper = lax.broadcasted_iota(jnp.int32, (LANES, rows), 0) < HD

    def one_pair(p, carry):
        q_pair, k_pair, v_pair = q_all[p], k_all[p], v_all[p]
        grad = drop[p].astype(F32)
        den = den_all[p]
        grad_sums = (grad / den).astype(BF16)
        drift_all = (grad * o_all[p] / den).T
        found = []
        for t in range(2):
            keep = half if t == 0 else jnp.logical_not(half)
            drift = jnp.sum(drift_all[t * HD : (t + 1) * HD, :], axis=0, keepdims=True)
            raw = mm(jnp.where(keep, k_pair, zero), q_pair, NT)
            weights = jnp.where(allowed, jnp.exp(raw), 0.0)
            prob = mm(jnp.where(keep, v_pair, zero), grad_sums, NT)
            score = (weights * (prob - drift)).astype(BF16)
            found.append(
                (
                    mm(k_pair, score, TN),
                    mm(score, q_pair),
                    mm(weights.astype(BF16), grad_sums),
                )
            )
        dq_out[p] = (jnp.where(upper, found[0][0], found[1][0]).T * HD ** -0.5).astype(BF16)
        dk_out[p] = jnp.where(half, found[0][1], found[1][1]).astype(dk_out.dtype)
        dv_out[p] = jnp.where(half, found[0][2], found[1][2]).astype(dv_out.dtype)
        return carry

    lax.fori_loop(0, pairs, one_pair, 0)


def open_gradient(grad, whole, o_all, grad_out, low_out, att_out, drop, copies):
    pairs = drop.shape[0]
    cols = pairs * LANES // 2
    grad_out[...] = grad
    low = grad.astype(BF16)
    low_out[...] = low
    for p in range(pairs):
        att_out[:, p * LANES : (p + 1) * LANES] = o_all[p].astype(BF16)
    for copy in copies:
        copy.wait()
    first = mm(low, whole[0, :, 3 * cols :]).astype(BF16)
    second = mm(low, whole[1, :, 3 * cols :]).astype(BF16)
    by_pairs(jnp.concatenate([first, second], axis=1), drop)


def head_sums(dq_out, dv_out, heads_out):
    for p in range(dq_out.shape[0]):
        heads_out[0:1, p * LANES : (p + 1) * LANES] = column_sum(dq_out[p].astype(F32))
        heads_out[1:2, p * LANES : (p + 1) * LANES] = column_sum(dv_out[p].astype(F32))


def cross_backward(
    mixed, scalars, resid, cotangent, mine, other, gains, q_all, k_all, v_all, o_all, den_all,
    w0,
    grad_out, low_out, att_out, dq_out, dk_out, dv_out, part_out, sums_out, heads_out,
    drop, whole, sems,
):
    copies = fetch(scalars, (w0,), whole, sems, mixed)
    rows = resid.shape[0]
    pairs = q_all.shape[0]
    cols = pairs * LANES // 2
    unit, inverse = normalise(resid[...])
    grad_norm = mine[...].astype(F32) + other[...].astype(F32)
    top = cotangent[...].astype(F32)
    grad = top + norm_back(grad_norm, unit, inverse, gains[2:3, :])
    sums_out[0:1, :] = column_sum(grad_norm * unit)
    sums_out[1:2, :] = column_sum(grad_norm)
    sums_out[2:3, :] = column_sum(top)
    sums_out[3:4, :] = column_sum(grad)
    open_gradient(grad, whole, o_all, grad_out, low_out, att_out, drop, copies)
    frame = lax.broadcasted_iota(jnp.int32, (k_all.shape[1], 1), 0)
    allowed = (frame >= scalars[3]) & (frame < scalars[4])
    attend_back(pairs, rows, allowed, drop, q_all, k_all, v_all, o_all, den_all, dq_out, dk_out, dv_out)
    first, second = halves(dq_out, cols)
    part_out[...] = (mm(first, whole[0, :, :cols], NT) + mm(second, whole[1, :, :cols], NT)).astype(BF16)
    head_sums(dq_out, dv_out, heads_out)


def self_backward(
    scalars, resid, top, mine, other, gains, q_all, k_all, v_all, o_all, den_all,
    w0, w1, w2, w3,
    grad_out, low_out, att_out, dq_out, dk_out, dv_out, part_out, sums_out, heads_out,
    drop, whole, sems,
):
    copies = fetch(scalars, (w0, w1, w2, w3), whole, sems)
    rows = resid.shape[0]
    pairs = q_all.shape[0]
    cols = pairs * LANES // 2
    unit, inverse = normalise(resid[...])
    grad_norm = mine[...].astype(F32) + other[...].astype(F32)
    grad = top[...] + norm_back(grad_norm, unit, inverse, gains[1:2, :])
    sums_out[0:1, :] = column_sum(grad_norm * unit)
    sums_out[1:2, :] = column_sum(grad_norm)
    sums_out[2:3, :] = column_sum(grad)
    open_gradient(grad, whole, o_all, grad_out, low_out, att_out, drop, copies)
    k_place = lax.broadcasted_iota(jnp.int32, (rows, rows), 0)
    q_place = lax.broadcasted_iota(jnp.int32, (rows, rows), 1)
    allowed = (k_place <= q_place) & (k_place >= scalars[1])
    attend_back(pairs, rows, allowed, drop, q_all, k_all, v_all, o_all, den_all, dq_out, dk_out, dv_out)
    pieces = [halves(piece, cols) for piece in (dq_out, dk_out, dv_out)]
    total = jnp.zeros((rows, part_out.shape[1]), F32)
    for group in range(2):
        joined = jnp.concatenate([piece[group] for piece in pieces], axis=1)
        total = total + mm(joined, whole[group, :, : 3 * cols], NT)
    part_out[...] = total.astype(BF16)
    head_sums(dq_out, dv_out, heads_out)


def input_backward(
    scalars, hidden, top, mine, other, gains, sums_one, sums_two, heads_one, heads_two, unit_sums,
    mid_out, pair_out, cross_out, vec_out,
):
    unit, inverse = normalise(hidden[...].astype(F32))
    grad_norm = mine[...].astype(F32) + other[...].astype(F32)
    grad = top[...] + norm_back(grad_norm, unit, inverse, gains[0:1, :])
    send_rows(scalars, grad, mid_out, pair_out, cross_out)
    heads = [heads_one[0:1, :], heads_one[1:2, :], heads_two[0:1, :], heads_two[1:2, :]]
    cols = heads[0].shape[1] // 2
    units = unit_sums.shape[1] // 2
    own = jnp.concatenate([row[:, :cols] for row in heads], axis=1)
    rest = jnp.concatenate([row[:, cols:] for row in heads], axis=1)
    own_units, rest_units = unit_sums[:, :units], unit_sums[:, units:]
    odd = scalars[6] == 1
    rows = [
        column_sum(grad_norm * unit), sums_one[0:1, :], sums_two[0:1, :],
        column_sum(grad_norm), sums_one[1:2, :], sums_two[1:2, :],
        sums_one[2:3, :], sums_two[3:4, :], sums_two[2:3, :],
        jnp.where(odd, rest, own), jnp.where(odd, rest_units, own_units),
        jnp.where(odd, own, rest), jnp.where(odd, own_units, rest_units),
    ]
    for k, row in enumerate(rows):
        vec_out[k : k + 1, :] = row
    vec_out[len(rows) :, :] = jnp.zeros((vec_out.shape[0] - len(rows), vec_out.shape[1]), F32)


def frame_backward(mixed, scalars, dk_all, dv_all, w0, kept_out, given_out, total, whole, sems):
    copies = fetch(scalars, (w0,), whole, sems, mixed)
    pairs = dk_all.shape[0]
    cols = pairs * LANES // 2
    size = kept_out.shape[0]
    frames = dk_all.shape[1]
    near = (frames - size) * 3 // 8
    far = frames - size - near
    keys = halves(dk_all, cols)
    values = halves(dv_all, cols)
    for copy in copies:
        copy.wait()
    for group in range(2):
        joined = jnp.concatenate([keys[group], values[group]], axis=1)
        part = mm(joined, whole[group, :, cols : 3 * cols], NT)
        total[...] = part if group == 0 else total[...] + part
    odd = scalars[6]
    main = scalars[7] == 1
    lead = pl.multiple_of(jnp.where(odd == 0, near, far), 32)
    near_at = pl.multiple_of(jnp.where(odd == 0, 0, far + size), 32)
    far_at = pl.multiple_of(jnp.where(odd == 0, near + size, 0), 32)
    mid = total[pl.ds(lead, size), :].astype(BF16)
    near_part = total[pl.ds(near_at, near), :].astype(BF16)
    far_part = total[pl.ds(far_at, far), :].astype(BF16)

    @pl.when(main)
    def _():
        kept_out[...] = mid
        given_out[:near, :] = near_part
        given_out[near:, :] = far_part

    @pl.when(jnp.logical_not(main))
    def _():
        given_out[...] = mid
        kept_out[:near, :] = near_part
        kept_out[near:, :] = far_part


def send_grads(scalars, whole, out, sems, extra=None):
    rows = whole.shape[1] // 8
    added = 0 if extra is None else extra.shape[0]
    copies = []
    for chip in range(4):
        start = chip * (4 * rows + added)
        for group in range(2):
            for half in range(2):
                at = 2 * rows * chip + rows * jnp.bitwise_xor(scalars[5], half)
                copies.append(
                    pltpu.make_async_copy(
                        whole.at[group, pl.ds(pl.multiple_of(at, rows), rows), :],
                        out.at[pl.ds(start + (2 * group + half) * rows, rows), :],
                        sems.at[len(copies)],
                    )
                )
        if added:
            copies.append(
                pltpu.make_async_copy(extra, out.at[pl.ds(start + 4 * rows, added), :], sems.at[len(copies)])
            )
    for copy in copies:
        copy.start()
    for copy in copies:
        copy.wait()


def unit_grads(scalars, norm, pre, top, act, out, whole, sems):
    units = pre.shape[1] // 2
    for group in range(2):
        at = slice(group * units, (group + 1) * units)
        whole[group, :, :units] = mm(norm[...], pre[:, at], TN).astype(BF16)
        whole[group, :, units:] = mm(top[...], act[:, at], TN).astype(BF16)
    send_grads(scalars, whole, out, sems)


def cross_grads(scalars, norm, frames, low, att, dq, dk, dv, out, whole, sems):
    cols = att.shape[1] // 2
    parts = [halves(piece, cols) for piece in (dq, dk, dv)]
    for group in range(2):
        at = slice(group * cols, (group + 1) * cols)
        joined = jnp.concatenate([parts[1][group], parts[2][group]], axis=1)
        found = [mm(norm[...], parts[0][group], TN), mm(frames[...], joined, TN), mm(low[...], att[:, at], TN)]
        whole[group] = jnp.concatenate(found, axis=1).astype(BF16)
    send_grads(scalars, whole, out, sems)


def self_grads(scalars, norm, low, att, dq, dk, dv, vectors, out, low_vectors, whole, sems):
    low_vectors[...] = vectors[...].astype(BF16)
    cols = att.shape[1] // 2
    parts = [halves(piece, cols) for piece in (dq, dk, dv)]
    for group in range(2):
        at = slice(group * cols, (group + 1) * cols)
        joined = jnp.concatenate([part[group] for part in parts], axis=1)
        found = [mm(norm[...], joined, TN), mm(low[...], att[:, at], TN)]
        whole[group] = jnp.concatenate(found, axis=1).astype(BF16)
    send_grads(scalars, whole, out, sems, low_vectors)


SMEM = pl.BlockSpec(memory_space=pltpu.SMEM)
VMEM = pl.BlockSpec(memory_space=pltpu.VMEM)
ANY = pl.BlockSpec(memory_space=pl.ANY)


def shape(dims, dtype):
    return jax.ShapeDtypeStruct(tuple(dims), dtype)


def kernel_call(kernel, name, cost, operands, spaces, outs, out_spaces=None, scratch=()):
    return pl.pallas_call(
        kernel,
        out_shape=tuple(outs),
        in_specs=list(spaces),
        out_specs=tuple(out_spaces or [VMEM] * len(outs)),
        scratch_shapes=list(scratch),
        compiler_params=pltpu.CompilerParams(vmem_limit_bytes=56 * 1024 * 1024),
        cost_estimate=pl.CostEstimate(flops=int(cost * 1e9), transcendentals=0, bytes_accessed=1 << 20),
        name=name,
    )(*operands)


def body(
    hidden, encoded, token_lengths, frame_counts, ln_gain, ln_bias, head_bias, out_bias, fc_bias,
    self_proj, cross_proj, out_proj, fc_in, fc_out, cotangent,
):
    wide = lax.axis_size("wide")
    depth = lax.axis_size("narrow")
    tok_rows, width = hidden.shape[1:]
    frame_rows = encoded.shape[1]
    swing = (MAXLEN - tok_rows) // 2
    ratio = frame_rows // tok_rows
    near = ratio * swing
    far = frame_rows - near
    assert far >= near + JITTER and 8 * near == 3 * frame_rows
    assert depth == 4 and hidden.shape[0] == 2
    rows = tok_rows + 2 * swing
    frames = near + frame_rows + far
    shard = width // wide
    block = 2 * shard
    head_cols = head_bias.shape[1]
    cols = 2 * head_cols
    pairs = cols // LANES
    hidden_units = fc_bias.shape[0]
    units = 2 * hidden_units

    w = lax.axis_index("wide")
    n = lax.axis_index("narrow")
    chip = w // 2
    core = w % 2
    batch = n // 2
    odd = n % 2
    item = 2 * chip + odd
    main = core == odd
    home = core == batch
    relay = wide == 8

    def move(value, rule):
        pairs_list = []
        for ws in range(wide):
            for ns in range(depth):
                target = rule(ws, ns)
                if target is not None and 0 <= target[0] < wide:
                    pairs_list.append((ws * depth + ns, target[0] * depth + target[1]))
        return lax.ppermute(value, AXES, pairs_list)

    def swap(value):
        return move(value, lambda a, z: (a ^ 1, z))

    def after(value, *events):
        return lax.optimization_barrier((value, *events))[0]

    def pick(value, index):
        return lax.dynamic_index_in_dim(value, index, 0, keepdims=False)

    bias_vector = jnp.concatenate([head_bias.reshape(-1), fc_bias])
    bias_high = lax.reduce_precision(bias_vector, 8, 7)
    bias_rest = bias_vector - bias_high
    bias_middle = lax.reduce_precision(bias_rest, 8, 7)
    bias_parts = jnp.stack([bias_high, bias_middle, bias_rest - bias_middle]).astype(BF16)
    bias_parts = jnp.concatenate([bias_parts.reshape(6, width), jnp.zeros((2, width), BF16)], axis=0)

    def group(stack, out):
        return jnp.concatenate([stack[0], stack[1], stack[2], out.T], axis=1)

    def away(value):
        return move(value, lambda a, z: (a ^ 1, z) if a % 2 != z // 2 else None)

    def two_groups(value):
        opposite = move(value, lambda a, z: (a, z ^ 2) if a % 2 == z // 2 else None)
        same = jnp.where(home, value, opposite)
        return same, move(same, lambda a, z: (a, z ^ 1))

    groups = [list(range(k, wide, 2)) for k in range(2)]

    def in_quarters(joined):
        if relay:
            return lax.all_gather(joined, "wide", axis=0, tiled=True, axis_index_groups=groups)
        size = joined.shape[1]
        full = lax.all_gather(joined.reshape(2, 2, shard, size), "wide", axis_index_groups=groups)
        full = jnp.where(core == 0, full, full[:, :, ::-1])
        full = jnp.swapaxes(full, 0, 1).reshape(2, 4, width // 4, size)
        return jnp.swapaxes(full, 0, 1).reshape(-1, size)

    def between_chips(joined, *events):
        if relay:
            joined = after(joined, *events)
            return [joined] + [move(joined, partial(lambda k, a, z: (a ^ k, z), 2 * k)) for k in (1, 2, 3)]
        full = in_quarters(joined)
        return [full[j * width // 2 : (j + 1) * width // 2] for j in range(4)]

    def edge(value, margin):
        start = jnp.where(odd == 0, value.shape[1] - margin, 0)
        return lax.dynamic_slice(value, (batch, start, 0), (1, margin, width))[0]

    def halo_rule(a, z):
        if a % 2 == z % 2:
            return None
        return (a + 1, z) if z % 2 == 0 else (a - 1, z)

    edges = jnp.concatenate([edge(hidden, swing), edge(cotangent, swing), edge(encoded, near)], axis=0)
    halo = move(edges, halo_rule)
    halo = jnp.where(main, halo, move(halo, lambda a, z: (a ^ 1, z) if a % 2 == z % 2 else None))
    hidden_halo, top_halo, frame_halo = halo[:swing], halo[swing : 2 * swing], halo[2 * swing :]

    rest_piece = jnp.concatenate([group(cross_proj, out_proj[1]), fc_in, fc_out.T], axis=1)
    if relay:
        rest_w = lax.all_gather(rest_piece, AXES, axis=0, tiled=True)
    else:
        rest_here = jnp.concatenate([rest_piece, away(rest_piece)], axis=0)
        rest_w = in_quarters(jnp.concatenate(two_groups(rest_here), axis=0))
    self_piece = group(self_proj, out_proj[0])
    self_got = two_groups(jnp.concatenate([self_piece, away(self_piece), bias_parts], axis=0))
    self_own = after(jnp.concatenate([x[:block] for x in self_got], axis=0), halo)
    self_w = between_chips(self_own)
    biases = jnp.concatenate([x[block:] for x in self_got], axis=0)

    own_hidden = pick(hidden, batch)
    own_top = pick(after(cotangent, self_own), batch)
    own_frames = pick(after(encoded, self_own), batch)
    token_lengths = after(token_lengths, self_own)
    lengths = pick(token_lengths, batch)
    counts = pick(frame_counts, batch)
    items = jnp.arange(lengths.shape[0], dtype=jnp.int32)
    tok_lo = jnp.sum(jnp.where(items < item, lengths, 0)) - (tok_rows * item - swing)
    tok_hi = tok_lo + jnp.sum(jnp.where(items == item, lengths, 0))
    frame_start = frame_rows * item - jnp.where(odd == 0, near, far)
    frame_lo = jnp.sum(jnp.where(items < item, counts, 0)) - frame_start
    frame_hi = frame_lo + jnp.sum(jnp.where(items == item, counts, 0))
    nothing = jnp.zeros((), jnp.int32)
    here, order = (chip, core) if relay else (nothing, nothing)
    scalars = jnp.stack(
        [here, tok_lo, tok_hi, frame_lo, frame_hi, order, odd, main.astype(jnp.int32)]
    ).astype(jnp.int32)

    low_shape = shape((rows, width), BF16)
    wide_f32 = shape((rows, width), F32)
    head_b = shape((pairs, rows, LANES), BF16)
    head_f = shape((pairs, rows, LANES), F32)
    frame_b = shape((pairs, frames, LANES), BF16)
    att_shape = shape((rows, cols), BF16)
    frame_full = shape((frames, width), BF16)
    sems = pltpu.SemaphoreType.DMA((20,))
    head_scratch = [pltpu.VMEM((2, width, width), BF16), sems]
    unit_scratch = [pltpu.VMEM((2, width, 2 * hidden_units), BF16), sems]

    hidden_rows, low_one, self_q, self_k, self_v, self_o, self_den, part = kernel_call(
        self_forward, "self_forward", 8,
        (scalars, own_hidden, swap(own_hidden), hidden_halo, ln_gain, ln_bias, biases, *self_w),
        [SMEM] + [VMEM] * 6 + [ANY] * 4,
        [low_shape, low_shape, head_b, head_b, head_b, head_f, head_f, low_shape],
        scratch=head_scratch,
    )
    frame_window, cross_k, cross_v = kernel_call(
        partial(frame_project, relay), "frame_project", 7,
        (scalars, own_frames, swap(own_frames), after(frame_halo, part), biases, rest_w),
        [SMEM] + [VMEM] * 4 + [ANY],
        [frame_full, frame_b, frame_b],
        scratch=head_scratch,
    )
    resid_one, low_two, cross_q, cross_o, cross_den, part_two = kernel_call(
        partial(cross_forward, relay), "cross_forward", 11,
        (scalars, hidden_rows, part, swap(part), ln_gain, ln_bias, out_bias, biases, cross_k, cross_v, rest_w),
        [SMEM] + [VMEM] * 9 + [ANY],
        [wide_f32, low_shape, head_b, head_f, head_f, low_shape],
        scratch=head_scratch,
    )
    act_shape = shape((rows, units), BF16)
    resid_two, low_three, top_rows, low_act, grad_pre, part_three, back_three, unit_sums = kernel_call(
        partial(unit_forward, relay), "unit_forward", 14,
        (scalars, resid_one, part_two, swap(part_two), ln_gain, ln_bias, out_bias, biases, own_top, swap(own_top), top_halo, rest_w),
        [SMEM] + [VMEM] * 10 + [ANY],
        [wide_f32, low_shape, low_shape, act_shape, act_shape, low_shape, low_shape, shape((1, units), F32)],
        scratch=unit_scratch,
    )
    other_back = swap(back_three)
    other_three = swap(part_three)

    def between_back(grads):
        if relay:
            return lax.psum_scatter(grads, "wide", scatter_dimension=0, tiled=True, axis_index_groups=groups)
        size = grads.shape[1]
        full = jnp.swapaxes(grads.reshape(4, 2, width // 4, size), 0, 1).reshape(2, wide // 2, 2, shard, size)
        full = jnp.swapaxes(jnp.where(core == 0, full, full[:, :, ::-1]), 0, 1)
        total = lax.psum_scatter(full, "wide", scatter_dimension=0, axis_index_groups=groups)
        return total.reshape(2 * block, size)

    def from_opposite(paired):
        return move(paired, lambda a, z: (a, z ^ 2) if a % 2 != z // 2 else None)

    def to_owner(paired, opposite):
        summed = paired.astype(F32) + opposite.astype(F32)
        passed = move(summed[shard:], lambda a, z: (a ^ 1, z) if a % 2 == z // 2 else None)
        return jnp.where(home, summed[:shard], passed)

    def grads_of(kernel, name, cost, size, scratch, *operands, added=0):
        return kernel_call(
            kernel, name, cost, (scalars, *operands),
            [SMEM] + [VMEM] * len(operands),
            [shape((2 * width + 4 * added, size), BF16)],
            [ANY],
            scratch=scratch,
        )[0]

    grads_unit = grads_of(
        unit_grads, "unit_grads", 9, 2 * hidden_units, unit_scratch, low_three, grad_pre, top_rows, low_act
    )
    unit_total = between_back(grads_unit)
    sums_shape = shape((8, width), F32)
    heads_shape = shape((8, cols), F32)
    drop_scratch = [pltpu.VMEM((pairs, rows, LANES), BF16)]
    grad_two, low_grad_two, low_cross, cq_grad, ck_grad, cv_grad, back_two, sums_two, heads_two = kernel_call(
        partial(cross_backward, relay), "cross_backward", 21,
        (scalars, resid_two, top_rows, back_three, after(other_back, grads_unit), ln_gain, cross_q, cross_k, cross_v, cross_o, cross_den, rest_w),
        [SMEM] + [VMEM] * 10 + [ANY],
        [wide_f32, low_shape, att_shape, head_b, frame_b, frame_b, low_shape, sums_shape, heads_shape],
        scratch=drop_scratch + head_scratch,
    )
    def cross_rule(a, z):
        if a % 2 == z % 2:
            return None
        return (a - 2, z ^ 1) if z % 2 == 0 else (a + 2, z ^ 1)

    def pair_rule(a, z):
        return None if a % 2 == z % 2 else (a, z ^ 1)

    def from_main(value, step):
        return move(value, lambda a, z: (a, z ^ step) if a % 2 == z % 2 else None)

    def per_batch(near_copy, far_copy, dtype):
        near_copy, far_copy = near_copy.astype(dtype), far_copy.astype(dtype)
        return jnp.stack(
            [jnp.where(batch == 0, near_copy, far_copy), jnp.where(batch == 0, far_copy, near_copy)]
        )

    def token_block(mid, from_pair, from_cross):
        above = jnp.where(odd == 1, from_pair, from_cross)
        below = jnp.where(odd == 1, from_cross, from_pair)
        return jnp.concatenate([mid[:swing] + above, mid[swing:-swing], mid[-swing:] + below], axis=0)

    edge_shape = shape((swing, width), BF16)
    slice_shapes = [shape((tok_rows, width), BF16), edge_shape, edge_shape]
    grads_cross = grads_of(
        cross_grads, "cross_grads", 8, width, head_scratch,
        low_two, frame_window, low_grad_two, low_cross, cq_grad, ck_grad, cv_grad,
    )
    kept, given = kernel_call(
        partial(frame_backward, relay), "frame_backward", 7,
        (scalars, after(ck_grad, grads_cross), cv_grad, rest_w),
        [SMEM] + [VMEM] * 2 + [ANY],
        [shape((frame_rows, width), BF16)] * 2,
        scratch=[pltpu.VMEM((frames, width), F32)] + head_scratch,
    )
    out_mid, out_pair, out_cross = kernel_call(
        finish_output, "finish_output", 3,
        (scalars, resid_two, part_three, after(other_three, kept), out_bias),
        [SMEM] + [VMEM] * 4,
        slice_shapes,
    )
    half_sum = (kept.astype(F32) + swap(given).astype(F32)).astype(BF16)
    half_sum = after(half_sum, out_mid)
    to_pair = jnp.concatenate([half_sum[near:], out_pair], axis=0)
    to_cross = jnp.concatenate([half_sum[:near], out_cross], axis=0)
    from_pair = move(to_pair, pair_rule)
    from_cross = move(to_cross, cross_rule)
    cross_total = between_back(after(grads_cross, unit_total, to_pair, to_cross))
    grad_one, low_grad_one, low_self, sq_grad, sk_grad, sv_grad, back_one, sums_one, heads_one = kernel_call(
        self_backward, "self_backward", 12,
        (scalars, resid_one, grad_two, back_two, after(swap(back_two), to_pair, to_cross), ln_gain, self_q, self_k, self_v, self_o, self_den, *self_w),
        [SMEM] + [VMEM] * 10 + [ANY] * 4,
        [wide_f32, low_shape, att_shape, head_b, head_b, head_b, low_shape, sums_shape, heads_shape],
        scratch=drop_scratch + head_scratch,
    )
    extra = jnp.where(
        odd == 1,
        jnp.concatenate([from_pair[:far], from_cross[:near]], axis=0),
        jnp.concatenate([from_cross[:near], from_pair[:far]], axis=0),
    )
    out_rows = token_block(out_mid, from_pair[far:], from_cross[near:])
    copies_block = after(jnp.concatenate([half_sum + extra, out_rows], axis=0), back_one)
    copies_opposite = from_main(copies_block, 2)
    copies_beside = from_main(copies_block, 1)
    in_mid, in_pair, in_cross, vectors = kernel_call(
        input_backward, "input_backward", 4,
        (scalars, hidden_rows, grad_one, back_one, after(swap(back_one), copies_block), ln_gain, sums_one, sums_two, heads_one, heads_two, unit_sums),
        [SMEM] + [VMEM] * 10,
        slice_shapes + [shape((16, width), F32)],
    )
    in_from_pair = move(in_pair, pair_rule)
    in_from_cross = move(in_cross, cross_rule)
    added = vectors.shape[0]
    grads_self = grads_of(
        self_grads, "self_grads", 5, width, [pltpu.VMEM((added, width), BF16)] + head_scratch,
        after(low_one, in_mid), low_grad_one, low_self, sq_grad, sk_grad, sv_grad, vectors,
        added=added,
    )
    in_rows = after(token_block(in_mid, in_from_pair, in_from_cross), grads_self)
    if relay:
        self_total = between_back(after(grads_self, cross_total, in_rows, copies_beside))
    else:
        parts = grads_self.reshape(4, -1, width)[:, : width // 2].reshape(-1, width)
        self_total = jnp.concatenate([between_back(parts), jnp.zeros((added, width), BF16)], axis=0)
    in_opposite = from_main(in_rows, 2)
    in_beside = from_main(in_rows, 1)
    early = jnp.concatenate([unit_total, cross_total], axis=1)
    early_across = move(early[block:], lambda a, z: (a, z ^ 1))
    early_paired = (early[:block].astype(F32) + early_across.astype(F32)).astype(BF16)
    copies_third = from_main(copies_opposite, 1)
    early_opposite = from_opposite(early_paired)
    self_total = after(self_total, early_paired)
    self_across = move(self_total[block:], lambda a, z: (a, z ^ 1))
    self_paired = (self_total[:block].astype(F32) + self_across[:block].astype(F32)).astype(BF16)
    if relay:
        vectors = self_total[2 * block :].astype(F32) + self_across[block:].astype(F32)
        vectors = vectors + move(vectors, lambda a, z: (a, z ^ 2))
    else:
        vectors = lax.psum(lax.psum(vectors, "narrow"), "wide", axis_index_groups=groups)
    in_third = from_main(after(in_opposite, early_paired), 1)
    self_opposite = from_opposite(self_paired)
    grad_early = to_owner(early_paired, after(early_opposite, self_paired))
    grad_unit, grad_cross = grad_early[:, : 2 * hidden_units], grad_early[:, 2 * hidden_units :]
    grad_self = to_owner(self_paired, self_opposite)

    def copied(first, last, value, opposite, beside, third, dtype):
        near_copy = jnp.where(main, value[first:last], beside[first:last])
        far_copy = jnp.where(main, opposite[first:last], third[first:last])
        return per_batch(near_copy, far_copy, dtype)

    copies = (copies_block, copies_opposite, copies_beside, copies_third)
    encoded_grad = copied(0, frame_rows, *copies, F32)
    output = copied(frame_rows, frame_rows + tok_rows, *copies, BF16)
    input_grad = copied(0, tok_rows, in_rows, in_opposite, in_beside, in_third, F32)

    def unpacked(grad):
        stack = jnp.stack([grad[:, head_cols * k : head_cols * (k + 1)] for k in range(3)])
        return stack, grad[:, 3 * head_cols :].T

    grad_self_proj, grad_out_one = unpacked(grad_self)
    grad_cross_proj, grad_out_two = unpacked(grad_cross)

    mine = lax.dynamic_slice_in_dim(vectors, 9 + 2 * odd, 2, 0)
    mine = jnp.where(home, mine, swap(mine))
    return (
        output,
        input_grad,
        encoded_grad,
        vectors[:3],
        vectors[3:6],
        mine[0].reshape(4, head_cols),
        vectors[6:9],
        mine[1],
        grad_self_proj,
        grad_cross_proj,
        jnp.stack([grad_out_one, grad_out_two]),
        grad_unit[:, :hidden_units],
        grad_unit[:, hidden_units:].T,
    )


def solution(mesh):
    in_specs = (
        P(None, "wide", None),
        P(None, "wide", None),
        P(),
        P(),
        P(),
        P(),
        P(None, "narrow"),
        P(),
        P("narrow"),
        P(None, "wide", "narrow"),
        P(None, "wide", "narrow"),
        P(None, "narrow", "wide"),
        P("wide", "narrow"),
        P("narrow", "wide"),
        P(None, "wide", None),
    )
    out_specs = (
        P(None, "wide", None),
        P(None, "wide", None),
        P(None, "wide", None),
        P(),
        P(),
        P(None, "narrow"),
        P(),
        P("narrow"),
        P(None, "wide", "narrow"),
        P(None, "wide", "narrow"),
        P(None, "narrow", "wide"),
        P("wide", "narrow"),
        P("narrow", "wide"),
    )
    return jax.shard_map(body, mesh=mesh, in_specs=in_specs, out_specs=out_specs, check_vma=False)
```

```python
from functools import partial

import jax
import jax.numpy as jnp
from jax import lax
from jax.experimental import pallas as pl
from jax.experimental.pallas import tpu as pltpu
from jax.sharding import PartitionSpec as P

HD = 64
LANES = 128
MAXLEN = 448
JITTER = 156
EPSILON = 1e-05
F32 = jnp.float32
BF16 = jnp.bfloat16
NN = (((1,), (0,)), ((), ()))
NT = (((1,), (1,)), ((), ()))
TN = (((0,), (0,)), ((), ()))
AXES = ("wide", "narrow")


def mm(left, right, dims=NN):
    return lax.dot_general(left, right, dims, preferred_element_type=F32)


def normalise(values):
    centre = values - jnp.mean(values, axis=-1, keepdims=True)
    spread = jnp.mean(centre * centre, axis=-1, keepdims=True)
    inverse = lax.rsqrt(spread + EPSILON)
    return centre * inverse, inverse


def norm_back(grad_rows, unit_rows, inverse, gain):
    scaled = grad_rows * gain
    centred = scaled - jnp.mean(scaled, axis=-1, keepdims=True)
    return (centred - unit_rows * jnp.mean(scaled * unit_rows, axis=-1, keepdims=True)) * inverse


def erf(x):
    x = jnp.clip(x, -3.832506856900711, 3.832506856900711)
    x2 = x * x
    top = x2 * 0.00022905065861350646 + 0.0034082910107109506
    top = top * x2 + 0.050955695062380861
    top = top * x2 + 0.18520832239976145
    top = top * x2 + 1.128379143519084
    low = x2 * -1.1791602954361697e-7 + 0.000023547966471313185
    low = low * x2 + 0.0010179625278914885
    low = low * x2 + 0.014070470171167667
    low = low * x2 + 0.11098505178285362
    low = low * x2 + 0.49746925110067538
    low = low * x2 + 1.0
    return x * top / low


def fetch(scalars, blocks, whole, sems, mixed=False, column=0):
    rows = whole.shape[1] // 8
    copies = []
    for group in range(2):
        for chip in range(4):
            for half in range(2):
                first = (2 * group + half) * rows
                if len(blocks) == 4:
                    source, place = blocks[chip], jnp.bitwise_xor(scalars[0], chip)
                else:
                    source, place = blocks[0], chip
                    first += 4 * chip * rows
                    if mixed:
                        core = scalars[5]
                        first = 4 * jnp.bitwise_xor(core, half) + 2 * core + jnp.bitwise_xor(scalars[6], group)
                        first = pl.multiple_of(rows * (8 * chip + first), rows)
                at = 2 * rows * place + rows * jnp.bitwise_xor(scalars[5], half)
                copies.append(
                    pltpu.make_async_copy(
                        source.at[pl.ds(first, rows), pl.ds(column, whole.shape[2])],
                        whole.at[group, pl.ds(pl.multiple_of(at, rows), rows), :],
                        sems.at[len(copies)],
                    )
                )
    for copy in copies:
        copy.start()
    return copies


def first_half(shape):
    return lax.broadcasted_iota(jnp.int32, shape, len(shape) - 1) < HD


def lay_window(scalars, own, partner, halo, out, margin, other):
    size = own.shape[0]
    odd = scalars[6]
    main = scalars[7] == 1
    before = jnp.where(odd == 0, margin, other)
    out[pl.ds(pl.multiple_of(before, 32), size), :] = jnp.where(main, own[...], partner[...])
    near_side = jnp.where(main, partner[:other, :], own[:other, :])
    far_side = jnp.where(main, partner[size - other :, :], own[size - other :, :])

    @pl.when(odd == 0)
    def _():
        out[:margin, :] = halo[...]
        out[margin + size :, :] = near_side

    @pl.when(odd == 1)
    def _():
        out[other + size :, :] = halo[...]
        out[:other, :] = far_side


def valid_rows(scalars, rows):
    place = lax.broadcasted_iota(jnp.int32, (rows, 1), 0)
    return (place >= scalars[1]) & (place < scalars[2])


def both(first, second, at, size):
    return jnp.concatenate([first[:, at : at + size], second[:, at : at + size]], axis=1)


def bias_row(biases, at, size):
    parts = biases[:, at : at + size].astype(F32)
    rows = [parts[8 * g : 8 * g + 1] + parts[8 * g + 2 : 8 * g + 3] + parts[8 * g + 4 : 8 * g + 5] for g in range(2)]
    return jnp.concatenate(rows, axis=1)


def halves(refs, cols):
    joined = jnp.concatenate([refs[p] for p in range(refs.shape[0])], axis=1)
    return joined[:, :cols], joined[:, cols:]


def by_pairs(values, out):
    for p in range(out.shape[0]):
        out[p] = values[:, p * LANES : (p + 1) * LANES]


def attend(pairs, rows, allowed, guard, q_all, k_all, v_all, o_out, den_out):
    half = first_half((rows, LANES))
    zero = jnp.zeros((), BF16)

    def one_pair(p, carry):
        q_pair, k_pair, v_pair = q_all[p], k_all[p], v_all[p]
        outs, dens = [], []
        for keep in (half, jnp.logical_not(half)):
            raw = mm(jnp.where(keep, q_pair, zero), k_pair, NT)
            weights = jnp.where(allowed, jnp.exp(raw), 0.0)
            total = jnp.sum(weights, axis=1, keepdims=True)
            if guard:
                total = jnp.where(total > 0.0, total, 1.0)
            outs.append(mm(weights.astype(BF16), v_pair) / total)
            dens.append(jnp.broadcast_to(total, (rows, LANES)))
        o_out[p] = jnp.where(half, outs[0], outs[1])
        den_out[p] = jnp.where(half, dens[0], dens[1])
        return carry

    lax.fori_loop(0, pairs, one_pair, 0)


def out_product(o_all, whole, cols):
    first, second = halves(o_all, cols)
    first, second = first.astype(BF16), second.astype(BF16)
    return mm(first, whole[0, :, 3 * cols :], NT) + mm(second, whole[1, :, 3 * cols :], NT)


def self_forward(
    scalars, own, partner, halo, gains, shifts, biases, w0, w1, w2, w3,
    hidden_out, norm_out, q_out, k_out, v_out, o_out, den_out, part_out, whole, sems,
):
    copies = fetch(scalars, (w0, w1, w2, w3), whole, sems)
    rows = hidden_out.shape[0]
    pairs = q_out.shape[0]
    cols = pairs * LANES // 2
    margin = halo.shape[0]
    lay_window(scalars, own, partner, halo, hidden_out, margin, margin)
    unit, _ = normalise(hidden_out[...].astype(F32))
    norm = (unit * gains[0:1, :] + shifts[0:1, :]).astype(BF16)
    norm_out[...] = norm
    valid = valid_rows(scalars, rows)
    for copy in copies:
        copy.wait()
    first = mm(norm, whole[0, :, : 3 * cols])
    second = mm(norm, whole[1, :, : 3 * cols])
    query = (both(first, second, 0, cols) + bias_row(biases, 0 * cols, cols)).astype(BF16).astype(F32)
    by_pairs(jnp.where(valid, query * HD ** -0.5, 0.0).astype(BF16), q_out)
    by_pairs(both(first, second, cols, cols).astype(BF16), k_out)
    by_pairs((both(first, second, 2 * cols, cols) + bias_row(biases, 1 * cols, cols)).astype(BF16), v_out)
    q_place = lax.broadcasted_iota(jnp.int32, (rows, rows), 0)
    k_place = lax.broadcasted_iota(jnp.int32, (rows, rows), 1)
    allowed = (k_place <= q_place) & (k_place >= scalars[1])
    attend(pairs, rows, allowed, True, q_out, k_out, v_out, o_out, den_out)
    part_out[...] = out_product(o_out, whole, cols).astype(BF16)


def frame_project(
    mixed, scalars, own, partner, halo, biases, w0, frame_out, k_out, v_out, whole, sems
):
    copies = fetch(scalars, (w0,), whole, sems, mixed)
    pairs = k_out.shape[0]
    cols = pairs * LANES // 2
    margin = halo.shape[0]
    lay_window(scalars, own, partner, halo, frame_out, margin, own.shape[0] - margin)
    for copy in copies:
        copy.wait()
    first = mm(frame_out[...], whole[0, :, cols : 3 * cols])
    second = mm(frame_out[...], whole[1, :, cols : 3 * cols])
    by_pairs(both(first, second, 0, cols).astype(BF16), k_out)
    by_pairs((both(first, second, cols, cols) + bias_row(biases, 3 * cols, cols)).astype(BF16), v_out)


def cross_forward(
    mixed, scalars, hidden, mine, other, gains, shifts, outs_bias, biases, k_all, v_all, w0,
    resid_out, norm_out, q_out, o_out, den_out, part_out, whole, sems,
):
    copies = fetch(scalars, (w0,), whole, sems, mixed)
    rows = hidden.shape[0]
    pairs = q_out.shape[0]
    cols = pairs * LANES // 2
    summed = mine[...].astype(F32) + other[...].astype(F32)
    resid = hidden[...].astype(F32) + (summed + outs_bias[0:1, :])
    resid_out[...] = resid
    unit, _ = normalise(resid)
    norm = (unit * gains[1:2, :] + shifts[1:2, :]).astype(BF16)
    norm_out[...] = norm
    valid = valid_rows(scalars, rows)
    for copy in copies:
        copy.wait()
    query = jnp.concatenate([mm(norm, whole[0, :, :cols]), mm(norm, whole[1, :, :cols])], axis=1)
    query = (query + bias_row(biases, 2 * cols, cols)).astype(BF16).astype(F32)
    by_pairs(jnp.where(valid, query * HD ** -0.5, 0.0).astype(BF16), q_out)
    frame = lax.broadcasted_iota(jnp.int32, (1, k_all.shape[1]), 1)
    allowed = (frame >= scalars[3]) & (frame < scalars[4])
    attend(pairs, rows, allowed, False, q_out, k_all, v_all, o_out, den_out)
    part_out[...] = out_product(o_out, whole, cols).astype(BF16)


CHUNK = 768


def unit_forward(
    mixed, scalars, resid, mine, other, gains, shifts, outs_bias, fc_bias, own, partner, halo,
    w0,
    resid_out, norm_out, top_out, act_out, pre_out, part_out, back_out, sum_out, whole, sems,
):
    copies = fetch(scalars, (w0,), whole, sems, mixed, whole.shape[1])
    margin = halo.shape[0]
    lay_window(scalars, own, partner, halo, top_out, margin, margin)
    valid = valid_rows(scalars, resid.shape[0])
    top_out[...] = jnp.where(valid, top_out[...], jnp.zeros((), BF16))
    summed = mine[...].astype(F32) + other[...].astype(F32)
    resid_two = resid[...] + (summed + outs_bias[1:2, :])
    resid_out[...] = resid_two
    unit, _ = normalise(resid_two)
    norm_out[...] = (unit * gains[2:3, :] + shifts[2:3, :]).astype(BF16)
    for copy in copies:
        copy.wait()
    units = act_out.shape[1] // 2
    steps = units // CHUNK

    def one_chunk(j, carry):
        group = j // steps
        at_in = pl.ds(pl.multiple_of((j - group * steps) * CHUNK, CHUNK), CHUNK)
        at_back = pl.ds(pl.multiple_of(units + (j - group * steps) * CHUNK, CHUNK), CHUNK)
        at = pl.ds(pl.multiple_of(j * CHUNK, CHUNK), CHUNK)
        parts = fc_bias[:, at_in].astype(F32)
        parts = jnp.where(group == 0, parts[:8], parts[8:])
        pre = mm(norm_out[...], whole[group, :, at_in]) + (parts[1:2] + parts[3:4] + parts[5:6])
        cdf = 0.5 * (1.0 + erf(pre * 0.7071067811865476))
        act_out[:, at] = (pre * cdf).astype(BF16)
        slope = cdf + pre * (jnp.exp(-0.5 * pre * pre) * 0.3989422804014327)
        grad = (slope * mm(top_out[...], whole[group, :, at_back])).astype(BF16)
        pre_out[:, at] = grad
        sum_out[:, at] = jnp.sum(grad.astype(F32), axis=0, keepdims=True)
        return carry

    lax.fori_loop(0, 2 * steps, one_chunk, 0)
    back_out[...] = (
        mm(pre_out[:, :units], whole[0, :, :units], NT) + mm(pre_out[:, units:], whole[1, :, :units], NT)
    ).astype(BF16)
    part_out[...] = (
        mm(act_out[:, :units], whole[0, :, units:], NT) + mm(act_out[:, units:], whole[1, :, units:], NT)
    ).astype(BF16)


def send_rows(scalars, total, mid_out, pair_out, cross_out):
    margin = pair_out.shape[0]
    size = mid_out.shape[0]
    odd = scalars[6] == 1
    low = total.astype(BF16)
    head = low[:margin]
    tail = low[margin + size :]
    mid_out[...] = low[margin : margin + size]
    pair_out[...] = jnp.where(odd, head, tail)
    cross_out[...] = jnp.where(odd, tail, head)


def finish_output(scalars, resid, mine, other, outs_bias, mid_out, pair_out, cross_out):
    summed = mine[...].astype(F32) + other[...].astype(F32)
    total = resid[...] + (summed + outs_bias[2:3, :])
    total = jnp.where(valid_rows(scalars, resid.shape[0]), total, 0.0)
    send_rows(scalars, total, mid_out, pair_out, cross_out)


def column_sum(values):
    return jnp.sum(values, axis=0, keepdims=True)


def attend_back(pairs, rows, allowed, drop, q_all, k_all, v_all, o_all, den_all, dq_out, dk_out, dv_out):
    count = k_all.shape[1]
    half = first_half((count, LANES))
    zero = jnp.zeros((), BF16)
    upper = lax.broadcasted_iota(jnp.int32, (LANES, rows), 0) < HD

    def one_pair(p, carry):
        q_pair, k_pair, v_pair = q_all[p], k_all[p], v_all[p]
        grad = drop[p].astype(F32)
        den = den_all[p]
        grad_sums = (grad / den).astype(BF16)
        drift_all = (grad * o_all[p] / den).T
        found = []
        for t in range(2):
            keep = half if t == 0 else jnp.logical_not(half)
            drift = jnp.sum(drift_all[t * HD : (t + 1) * HD, :], axis=0, keepdims=True)
            raw = mm(jnp.where(keep, k_pair, zero), q_pair, NT)
            weights = jnp.where(allowed, jnp.exp(raw), 0.0)
            prob = mm(jnp.where(keep, v_pair, zero), grad_sums, NT)
            score = (weights * (prob - drift)).astype(BF16)
            found.append(
                (
                    mm(k_pair, score, TN),
                    mm(score, q_pair),
                    mm(weights.astype(BF16), grad_sums),
                )
            )
        dq_out[p] = (jnp.where(upper, found[0][0], found[1][0]).T * HD ** -0.5).astype(BF16)
        dk_out[p] = jnp.where(half, found[0][1], found[1][1]).astype(dk_out.dtype)
        dv_out[p] = jnp.where(half, found[0][2], found[1][2]).astype(dv_out.dtype)
        return carry

    lax.fori_loop(0, pairs, one_pair, 0)


def open_gradient(grad, whole, o_all, grad_out, low_out, att_out, drop, copies):
    pairs = drop.shape[0]
    cols = pairs * LANES // 2
    grad_out[...] = grad
    low = grad.astype(BF16)
    low_out[...] = low
    for p in range(pairs):
        att_out[:, p * LANES : (p + 1) * LANES] = o_all[p].astype(BF16)
    for copy in copies:
        copy.wait()
    first = mm(low, whole[0, :, 3 * cols :]).astype(BF16)
    second = mm(low, whole[1, :, 3 * cols :]).astype(BF16)
    by_pairs(jnp.concatenate([first, second], axis=1), drop)


def head_sums(dq_out, dv_out, heads_out):
    for p in range(dq_out.shape[0]):
        heads_out[0:1, p * LANES : (p + 1) * LANES] = column_sum(dq_out[p].astype(F32))
        heads_out[1:2, p * LANES : (p + 1) * LANES] = column_sum(dv_out[p].astype(F32))


def cross_backward(
    mixed, scalars, resid, cotangent, mine, other, gains, q_all, k_all, v_all, o_all, den_all,
    w0,
    grad_out, low_out, att_out, dq_out, dk_out, dv_out, part_out, sums_out, heads_out,
    drop, whole, sems,
):
    copies = fetch(scalars, (w0,), whole, sems, mixed)
    rows = resid.shape[0]
    pairs = q_all.shape[0]
    cols = pairs * LANES // 2
    unit, inverse = normalise(resid[...])
    grad_norm = mine[...].astype(F32) + other[...].astype(F32)
    top = cotangent[...].astype(F32)
    grad = top + norm_back(grad_norm, unit, inverse, gains[2:3, :])
    sums_out[0:1, :] = column_sum(grad_norm * unit)
    sums_out[1:2, :] = column_sum(grad_norm)
    sums_out[2:3, :] = column_sum(top)
    sums_out[3:4, :] = column_sum(grad)
    open_gradient(grad, whole, o_all, grad_out, low_out, att_out, drop, copies)
    frame = lax.broadcasted_iota(jnp.int32, (k_all.shape[1], 1), 0)
    allowed = (frame >= scalars[3]) & (frame < scalars[4])
    attend_back(pairs, rows, allowed, drop, q_all, k_all, v_all, o_all, den_all, dq_out, dk_out, dv_out)
    first, second = halves(dq_out, cols)
    part_out[...] = (mm(first, whole[0, :, :cols], NT) + mm(second, whole[1, :, :cols], NT)).astype(BF16)
    head_sums(dq_out, dv_out, heads_out)


def self_backward(
    scalars, resid, top, mine, other, gains, q_all, k_all, v_all, o_all, den_all,
    w0, w1, w2, w3,
    grad_out, low_out, att_out, dq_out, dk_out, dv_out, part_out, sums_out, heads_out,
    drop, whole, sems,
):
    copies = fetch(scalars, (w0, w1, w2, w3), whole, sems)
    rows = resid.shape[0]
    pairs = q_all.shape[0]
    cols = pairs * LANES // 2
    unit, inverse = normalise(resid[...])
    grad_norm = mine[...].astype(F32) + other[...].astype(F32)
    grad = top[...] + norm_back(grad_norm, unit, inverse, gains[1:2, :])
    sums_out[0:1, :] = column_sum(grad_norm * unit)
    sums_out[1:2, :] = column_sum(grad_norm)
    sums_out[2:3, :] = column_sum(grad)
    open_gradient(grad, whole, o_all, grad_out, low_out, att_out, drop, copies)
    k_place = lax.broadcasted_iota(jnp.int32, (rows, rows), 0)
    q_place = lax.broadcasted_iota(jnp.int32, (rows, rows), 1)
    allowed = (k_place <= q_place) & (k_place >= scalars[1])
    attend_back(pairs, rows, allowed, drop, q_all, k_all, v_all, o_all, den_all, dq_out, dk_out, dv_out)
    pieces = [halves(piece, cols) for piece in (dq_out, dk_out, dv_out)]
    total = jnp.zeros((rows, part_out.shape[1]), F32)
    for group in range(2):
        joined = jnp.concatenate([piece[group] for piece in pieces], axis=1)
        total = total + mm(joined, whole[group, :, : 3 * cols], NT)
    part_out[...] = total.astype(BF16)
    head_sums(dq_out, dv_out, heads_out)


def input_backward(
    scalars, hidden, top, mine, other, gains, sums_one, sums_two, heads_one, heads_two, unit_sums,
    mid_out, pair_out, cross_out, vec_out,
):
    unit, inverse = normalise(hidden[...].astype(F32))
    grad_norm = mine[...].astype(F32) + other[...].astype(F32)
    grad = top[...] + norm_back(grad_norm, unit, inverse, gains[0:1, :])
    send_rows(scalars, grad, mid_out, pair_out, cross_out)
    heads = [heads_one[0:1, :], heads_one[1:2, :], heads_two[0:1, :], heads_two[1:2, :]]
    cols = heads[0].shape[1] // 2
    units = unit_sums.shape[1] // 2
    own = jnp.concatenate([row[:, :cols] for row in heads], axis=1)
    rest = jnp.concatenate([row[:, cols:] for row in heads], axis=1)
    own_units, rest_units = unit_sums[:, :units], unit_sums[:, units:]
    odd = scalars[6] == 1
    rows = [
        column_sum(grad_norm * unit), sums_one[0:1, :], sums_two[0:1, :],
        column_sum(grad_norm), sums_one[1:2, :], sums_two[1:2, :],
        sums_one[2:3, :], sums_two[3:4, :], sums_two[2:3, :],
        jnp.where(odd, rest, own), jnp.where(odd, rest_units, own_units),
        jnp.where(odd, own, rest), jnp.where(odd, own_units, rest_units),
    ]
    for k, row in enumerate(rows):
        vec_out[k : k + 1, :] = row
    vec_out[len(rows) :, :] = jnp.zeros((vec_out.shape[0] - len(rows), vec_out.shape[1]), F32)


def frame_backward(mixed, scalars, dk_all, dv_all, w0, kept_out, given_out, total, whole, sems):
    copies = fetch(scalars, (w0,), whole, sems, mixed)
    pairs = dk_all.shape[0]
    cols = pairs * LANES // 2
    size = kept_out.shape[0]
    frames = dk_all.shape[1]
    near = (frames - size) * 3 // 8
    far = frames - size - near
    step = frames // 2
    for copy in copies:
        copy.wait()

    def one_part(j, carry):
        at = pl.ds(pl.multiple_of(j * step, step), step)
        keys = jnp.concatenate([dk_all[p, at, :] for p in range(pairs)], axis=1)
        values = jnp.concatenate([dv_all[p, at, :] for p in range(pairs)], axis=1)
        part = jnp.zeros((step, total.shape[1]), F32)
        for group in range(2):
            cut = slice(group * cols, (group + 1) * cols)
            joined = jnp.concatenate([keys[:, cut], values[:, cut]], axis=1)
            part = part + mm(joined, whole[group, :, cols : 3 * cols], NT)
        total[at, :] = part
        return carry

    lax.fori_loop(0, 2, one_part, 0)
    odd = scalars[6]
    main = scalars[7] == 1
    lead = pl.multiple_of(jnp.where(odd == 0, near, far), 32)
    near_at = pl.multiple_of(jnp.where(odd == 0, 0, far + size), 32)
    far_at = pl.multiple_of(jnp.where(odd == 0, near + size, 0), 32)
    mid = total[pl.ds(lead, size), :].astype(BF16)
    near_part = total[pl.ds(near_at, near), :].astype(BF16)
    far_part = total[pl.ds(far_at, far), :].astype(BF16)

    @pl.when(main)
    def _():
        kept_out[...] = mid
        given_out[:near, :] = near_part
        given_out[near:, :] = far_part

    @pl.when(jnp.logical_not(main))
    def _():
        given_out[...] = mid
        kept_out[:near, :] = near_part
        kept_out[near:, :] = far_part


def send_grads(scalars, whole, out, sems, extra=None):
    rows = whole.shape[1] // 8
    added = 0 if extra is None else extra.shape[0]
    copies = []
    for chip in range(4):
        start = chip * (4 * rows + added)
        for group in range(2):
            for half in range(2):
                at = 2 * rows * chip + rows * jnp.bitwise_xor(scalars[5], half)
                copies.append(
                    pltpu.make_async_copy(
                        whole.at[group, pl.ds(pl.multiple_of(at, rows), rows), :],
                        out.at[pl.ds(start + (2 * group + half) * rows, rows), :],
                        sems.at[len(copies)],
                    )
                )
        if added:
            copies.append(
                pltpu.make_async_copy(extra, out.at[pl.ds(start + 4 * rows, added), :], sems.at[len(copies)])
            )
    for copy in copies:
        copy.start()
    for copy in copies:
        copy.wait()


def unit_grads(scalars, norm, pre, top, act, out, whole, sems):
    units = pre.shape[1] // 2
    found = mm(norm[...], pre[...], TN).astype(BF16)
    for group in range(2):
        whole[group, :, :units] = found[:, group * units : (group + 1) * units]
    found = mm(top[...], act[...], TN).astype(BF16)
    for group in range(2):
        whole[group, :, units:] = found[:, group * units : (group + 1) * units]
    send_grads(scalars, whole, out, sems)


def all_heads(refs):
    return jnp.concatenate([refs[p] for p in range(refs.shape[0])], axis=1)


def by_groups(found, whole):
    for group in range(2):
        parts = []
        for piece in found:
            size = piece.shape[1] // 2
            parts.append(piece[:, group * size : (group + 1) * size])
        whole[group] = jnp.concatenate(parts, axis=1).astype(BF16)


def cross_grads(scalars, norm, frames, low, att, dq, dk, dv, out, whole, sems):
    cols = att.shape[1]
    pair = mm(frames[...], jnp.concatenate([all_heads(dk), all_heads(dv)], axis=1), TN)
    found = [mm(norm[...], all_heads(dq), TN), pair[:, :cols], pair[:, cols:], mm(low[...], att[...], TN)]
    by_groups(found, whole)
    send_grads(scalars, whole, out, sems)


def self_grads(scalars, norm, low, att, dq, dk, dv, vectors, out, low_vectors, whole, sems):
    low_vectors[...] = vectors[...].astype(BF16)
    cols = att.shape[1]
    three = mm(norm[...], jnp.concatenate([all_heads(dq), all_heads(dk), all_heads(dv)], axis=1), TN)
    found = [three[:, :cols], three[:, cols : 2 * cols], three[:, 2 * cols :], mm(low[...], att[...], TN)]
    by_groups(found, whole)
    send_grads(scalars, whole, out, sems, low_vectors)


SMEM = pl.BlockSpec(memory_space=pltpu.SMEM)
VMEM = pl.BlockSpec(memory_space=pltpu.VMEM)
ANY = pl.BlockSpec(memory_space=pl.ANY)


def shape(dims, dtype):
    return jax.ShapeDtypeStruct(tuple(dims), dtype)


def kernel_call(kernel, name, cost, operands, spaces, outs, out_spaces=None, scratch=()):
    return pl.pallas_call(
        kernel,
        out_shape=tuple(outs),
        in_specs=list(spaces),
        out_specs=tuple(out_spaces or [VMEM] * len(outs)),
        scratch_shapes=list(scratch),
        compiler_params=pltpu.CompilerParams(vmem_limit_bytes=56 * 1024 * 1024),
        cost_estimate=pl.CostEstimate(flops=int(cost * 2e9), transcendentals=0, bytes_accessed=1 << 20),
        name=name,
    )(*operands)


def body(
    hidden, encoded, token_lengths, frame_counts, ln_gain, ln_bias, head_bias, out_bias, fc_bias,
    self_proj, cross_proj, out_proj, fc_in, fc_out, cotangent,
):
    wide = lax.axis_size("wide")
    depth = lax.axis_size("narrow")
    tok_rows, width = hidden.shape[1:]
    frame_rows = encoded.shape[1]
    swing = (MAXLEN - tok_rows) // 2
    ratio = frame_rows // tok_rows
    near = ratio * swing
    far = frame_rows - near
    assert far >= near + JITTER and 8 * near == 3 * frame_rows
    assert depth == 4 and hidden.shape[0] == 2
    rows = tok_rows + 2 * swing
    frames = near + frame_rows + far
    shard = width // wide
    block = 2 * shard
    head_cols = head_bias.shape[1]
    cols = 2 * head_cols
    pairs = cols // LANES
    hidden_units = fc_bias.shape[0]
    units = 2 * hidden_units

    w = lax.axis_index("wide")
    n = lax.axis_index("narrow")
    chip = w // 2
    core = w % 2
    batch = n // 2
    odd = n % 2
    item = 2 * chip + odd
    main = core == odd
    home = core == batch
    relay = wide == 8

    def move(value, rule):
        pairs_list = []
        for ws in range(wide):
            for ns in range(depth):
                target = rule(ws, ns)
                if target is not None and 0 <= target[0] < wide:
                    pairs_list.append((ws * depth + ns, target[0] * depth + target[1]))
        return lax.ppermute(value, AXES, pairs_list)

    def swap(value):
        return move(value, lambda a, z: (a ^ 1, z))

    def after(value, *events):
        return lax.optimization_barrier((value, *events))[0]

    def pick(value, index):
        return lax.dynamic_index_in_dim(value, index, 0, keepdims=False)

    bias_vector = jnp.concatenate([head_bias.reshape(-1), fc_bias])
    bias_high = lax.reduce_precision(bias_vector, 8, 7)
    bias_rest = bias_vector - bias_high
    bias_middle = lax.reduce_precision(bias_rest, 8, 7)
    bias_parts = jnp.stack([bias_high, bias_middle, bias_rest - bias_middle]).astype(BF16)
    bias_parts = jnp.concatenate([bias_parts.reshape(6, width), jnp.zeros((2, width), BF16)], axis=0)

    def group(stack, out):
        return jnp.concatenate([stack[0], stack[1], stack[2], out.T], axis=1)

    def away(value):
        return move(value, lambda a, z: (a ^ 1, z) if a % 2 != z // 2 else None)

    def two_groups(value):
        opposite = move(value, lambda a, z: (a, z ^ 2) if a % 2 == z // 2 else None)
        same = jnp.where(home, value, opposite)
        return same, move(same, lambda a, z: (a, z ^ 1))

    groups = [list(range(k, wide, 2)) for k in range(2)]

    def in_quarters(joined):
        if relay:
            return lax.all_gather(joined, "wide", axis=0, tiled=True, axis_index_groups=groups)
        size = joined.shape[1]
        full = lax.all_gather(joined.reshape(2, 2, shard, size), "wide", axis_index_groups=groups)
        full = jnp.where(core == 0, full, full[:, :, ::-1])
        full = jnp.swapaxes(full, 0, 1).reshape(2, 4, width // 4, size)
        return jnp.swapaxes(full, 0, 1).reshape(-1, size)

    def between_chips(joined, *events):
        if relay:
            joined = after(joined, *events)
            return [joined] + [move(joined, partial(lambda k, a, z: (a ^ k, z), 2 * k)) for k in (1, 2, 3)]
        full = in_quarters(joined)
        return [full[j * width // 2 : (j + 1) * width // 2] for j in range(4)]

    def edge(value, margin):
        start = jnp.where(odd == 0, value.shape[1] - margin, 0)
        return lax.dynamic_slice(value, (batch, start, 0), (1, margin, width))[0]

    def halo_rule(a, z):
        if a % 2 == z % 2:
            return None
        return (a + 1, z) if z % 2 == 0 else (a - 1, z)

    edges = jnp.concatenate([edge(hidden, swing), edge(cotangent, swing), edge(encoded, near)], axis=0)
    halo = move(edges, halo_rule)
    halo = jnp.where(main, halo, move(halo, lambda a, z: (a ^ 1, z) if a % 2 == z % 2 else None))
    hidden_halo, top_halo, frame_halo = halo[:swing], halo[swing : 2 * swing], halo[2 * swing :]

    rest_piece = jnp.concatenate([group(cross_proj, out_proj[1]), fc_in, fc_out.T], axis=1)
    if relay:
        rest_w = lax.all_gather(rest_piece, AXES, axis=0, tiled=True)
    else:
        rest_here = jnp.concatenate([rest_piece, away(rest_piece)], axis=0)
        rest_w = in_quarters(jnp.concatenate(two_groups(rest_here), axis=0))
    self_piece = group(self_proj, out_proj[0])
    self_got = two_groups(jnp.concatenate([self_piece, away(self_piece), bias_parts], axis=0))
    self_own = after(jnp.concatenate([x[:block] for x in self_got], axis=0), halo)
    self_w = between_chips(self_own)
    biases = jnp.concatenate([x[block:] for x in self_got], axis=0)

    own_hidden = pick(hidden, batch)
    own_top = pick(after(cotangent, self_own), batch)
    own_frames = pick(after(encoded, self_own), batch)
    token_lengths = after(token_lengths, self_own)
    lengths = pick(token_lengths, batch)
    counts = pick(frame_counts, batch)
    items = jnp.arange(lengths.shape[0], dtype=jnp.int32)
    tok_lo = jnp.sum(jnp.where(items < item, lengths, 0)) - (tok_rows * item - swing)
    tok_hi = tok_lo + jnp.sum(jnp.where(items == item, lengths, 0))
    frame_start = frame_rows * item - jnp.where(odd == 0, near, far)
    frame_lo = jnp.sum(jnp.where(items < item, counts, 0)) - frame_start
    frame_hi = frame_lo + jnp.sum(jnp.where(items == item, counts, 0))
    nothing = jnp.zeros((), jnp.int32)
    here, order = (chip, core) if relay else (nothing, nothing)
    scalars = jnp.stack(
        [here, tok_lo, tok_hi, frame_lo, frame_hi, order, odd, main.astype(jnp.int32)]
    ).astype(jnp.int32)

    low_shape = shape((rows, width), BF16)
    wide_f32 = shape((rows, width), F32)
    head_b = shape((pairs, rows, LANES), BF16)
    head_f = shape((pairs, rows, LANES), F32)
    frame_b = shape((pairs, frames, LANES), BF16)
    att_shape = shape((rows, cols), BF16)
    frame_full = shape((frames, width), BF16)
    sems = pltpu.SemaphoreType.DMA((20,))
    head_scratch = [pltpu.VMEM((2, width, width), BF16), sems]
    unit_scratch = [pltpu.VMEM((2, width, 2 * hidden_units), BF16), sems]

    hidden_rows, low_one, self_q, self_k, self_v, self_o, self_den, part = kernel_call(
        self_forward, "self_forward", 8,
        (scalars, own_hidden, swap(own_hidden), hidden_halo, ln_gain, ln_bias, biases, *self_w),
        [SMEM] + [VMEM] * 6 + [ANY] * 4,
        [low_shape, low_shape, head_b, head_b, head_b, head_f, head_f, low_shape],
        scratch=head_scratch,
    )
    frame_window, cross_k, cross_v = kernel_call(
        partial(frame_project, relay), "frame_project", 7,
        (scalars, own_frames, swap(own_frames), after(frame_halo, part), biases, rest_w),
        [SMEM] + [VMEM] * 4 + [ANY],
        [frame_full, frame_b, frame_b],
        scratch=head_scratch,
    )
    resid_one, low_two, cross_q, cross_o, cross_den, part_two = kernel_call(
        partial(cross_forward, relay), "cross_forward", 11,
        (scalars, hidden_rows, part, swap(part), ln_gain, ln_bias, out_bias, biases, cross_k, cross_v, rest_w),
        [SMEM] + [VMEM] * 9 + [ANY],
        [wide_f32, low_shape, head_b, head_f, head_f, low_shape],
        scratch=head_scratch,
    )
    act_shape = shape((rows, units), BF16)
    resid_two, low_three, top_rows, low_act, grad_pre, part_three, back_three, unit_sums = kernel_call(
        partial(unit_forward, relay), "unit_forward", 14,
        (scalars, resid_one, part_two, swap(part_two), ln_gain, ln_bias, out_bias, biases, own_top, swap(own_top), top_halo, rest_w),
        [SMEM] + [VMEM] * 10 + [ANY],
        [wide_f32, low_shape, low_shape, act_shape, act_shape, low_shape, low_shape, shape((1, units), F32)],
        scratch=unit_scratch,
    )
    other_back = swap(back_three)
    other_three = swap(part_three)

    def between_back(grads):
        if relay:
            return lax.psum_scatter(grads, "wide", scatter_dimension=0, tiled=True, axis_index_groups=groups)
        size = grads.shape[1]
        full = jnp.swapaxes(grads.reshape(4, 2, width // 4, size), 0, 1).reshape(2, wide // 2, 2, shard, size)
        full = jnp.swapaxes(jnp.where(core == 0, full, full[:, :, ::-1]), 0, 1)
        total = lax.psum_scatter(full, "wide", scatter_dimension=0, axis_index_groups=groups)
        return total.reshape(2 * block, size)

    def from_opposite(paired):
        return move(paired, lambda a, z: (a, z ^ 2) if a % 2 != z // 2 else None)

    def to_owner(paired, opposite):
        summed = paired.astype(F32) + opposite.astype(F32)
        passed = move(summed[shard:], lambda a, z: (a ^ 1, z) if a % 2 == z // 2 else None)
        return jnp.where(home, summed[:shard], passed)

    def grads_of(kernel, name, cost, size, scratch, *operands, added=0):
        return kernel_call(
            kernel, name, cost, (scalars, *operands),
            [SMEM] + [VMEM] * len(operands),
            [shape((2 * width + 4 * added, size), BF16)],
            [ANY],
            scratch=scratch,
        )[0]

    grads_unit = grads_of(
        unit_grads, "unit_grads", 9, 2 * hidden_units, unit_scratch, low_three, grad_pre, top_rows, low_act
    )
    unit_total = between_back(grads_unit)
    sums_shape = shape((8, width), F32)
    heads_shape = shape((8, cols), F32)
    drop_scratch = [pltpu.VMEM((pairs, rows, LANES), BF16)]
    grad_two, low_grad_two, low_cross, cq_grad, ck_grad, cv_grad, back_two, sums_two, heads_two = kernel_call(
        partial(cross_backward, relay), "cross_backward", 21,
        (scalars, resid_two, top_rows, back_three, after(other_back, grads_unit), ln_gain, cross_q, cross_k, cross_v, cross_o, cross_den, rest_w),
        [SMEM] + [VMEM] * 10 + [ANY],
        [wide_f32, low_shape, att_shape, head_b, frame_b, frame_b, low_shape, sums_shape, heads_shape],
        scratch=drop_scratch + head_scratch,
    )
    def cross_rule(a, z):
        if a % 2 == z % 2:
            return None
        return (a - 2, z ^ 1) if z % 2 == 0 else (a + 2, z ^ 1)

    def pair_rule(a, z):
        return None if a % 2 == z % 2 else (a, z ^ 1)

    def from_main(value, step):
        return move(value, lambda a, z: (a, z ^ step) if a % 2 == z % 2 else None)

    def per_batch(near_copy, far_copy, dtype):
        near_copy, far_copy = near_copy.astype(dtype), far_copy.astype(dtype)
        return jnp.stack(
            [jnp.where(batch == 0, near_copy, far_copy), jnp.where(batch == 0, far_copy, near_copy)]
        )

    def token_block(mid, from_pair, from_cross):
        above = jnp.where(odd == 1, from_pair, from_cross)
        below = jnp.where(odd == 1, from_cross, from_pair)
        return jnp.concatenate([mid[:swing] + above, mid[swing:-swing], mid[-swing:] + below], axis=0)

    edge_shape = shape((swing, width), BF16)
    slice_shapes = [shape((tok_rows, width), BF16), edge_shape, edge_shape]
    grads_cross = grads_of(
        cross_grads, "cross_grads", 8, width, head_scratch,
        low_two, frame_window, low_grad_two, low_cross, cq_grad, ck_grad, cv_grad,
    )
    kept, given = kernel_call(
        partial(frame_backward, relay), "frame_backward", 7,
        (scalars, after(ck_grad, grads_cross), cv_grad, rest_w),
        [SMEM] + [VMEM] * 2 + [ANY],
        [shape((frame_rows, width), BF16)] * 2,
        scratch=[pltpu.VMEM((frames, width), F32)] + head_scratch,
    )
    out_mid, out_pair, out_cross = kernel_call(
        finish_output, "finish_output", 3,
        (scalars, resid_two, part_three, after(other_three, kept), out_bias),
        [SMEM] + [VMEM] * 4,
        slice_shapes,
    )
    half_sum = (kept.astype(F32) + swap(given).astype(F32)).astype(BF16)
    half_sum = after(half_sum, out_mid)
    to_pair = jnp.concatenate([half_sum[near:], out_pair], axis=0)
    to_cross = jnp.concatenate([half_sum[:near], out_cross], axis=0)
    from_pair = move(to_pair, pair_rule)
    from_cross = move(to_cross, cross_rule)
    cross_total = between_back(after(grads_cross, unit_total, to_pair, to_cross))
    grad_one, low_grad_one, low_self, sq_grad, sk_grad, sv_grad, back_one, sums_one, heads_one = kernel_call(
        self_backward, "self_backward", 12,
        (scalars, resid_one, grad_two, back_two, after(swap(back_two), to_pair, to_cross), ln_gain, self_q, self_k, self_v, self_o, self_den, *self_w),
        [SMEM] + [VMEM] * 10 + [ANY] * 4,
        [wide_f32, low_shape, att_shape, head_b, head_b, head_b, low_shape, sums_shape, heads_shape],
        scratch=drop_scratch + head_scratch,
    )
    extra = jnp.where(
        odd == 1,
        jnp.concatenate([from_pair[:far], from_cross[:near]], axis=0),
        jnp.concatenate([from_cross[:near], from_pair[:far]], axis=0),
    )
    out_rows = token_block(out_mid, from_pair[far:], from_cross[near:])
    copies_block = after(jnp.concatenate([half_sum + extra, out_rows], axis=0), back_one)
    copies_opposite = from_main(copies_block, 2)
    copies_beside = from_main(copies_block, 1)
    in_mid, in_pair, in_cross, vectors = kernel_call(
        input_backward, "input_backward", 4,
        (scalars, hidden_rows, grad_one, back_one, after(swap(back_one), copies_block), ln_gain, sums_one, sums_two, heads_one, heads_two, unit_sums),
        [SMEM] + [VMEM] * 10,
        slice_shapes + [shape((16, width), F32)],
    )
    in_from_pair = move(in_pair, pair_rule)
    in_from_cross = move(in_cross, cross_rule)
    added = vectors.shape[0]
    grads_self = grads_of(
        self_grads, "self_grads", 5, width, [pltpu.VMEM((added, width), BF16)] + head_scratch,
        after(low_one, in_mid), low_grad_one, low_self, sq_grad, sk_grad, sv_grad, vectors,
        added=added,
    )
    in_rows = after(token_block(in_mid, in_from_pair, in_from_cross), grads_self)
    if relay:
        self_total = between_back(after(grads_self, cross_total, in_rows, copies_beside))
    else:
        parts = grads_self.reshape(4, -1, width)[:, : width // 2].reshape(-1, width)
        self_total = jnp.concatenate([between_back(parts), jnp.zeros((added, width), BF16)], axis=0)
    in_opposite = from_main(in_rows, 2)
    in_beside = from_main(in_rows, 1)
    early = jnp.concatenate([unit_total, cross_total], axis=1)
    early_across = move(early[block:], lambda a, z: (a, z ^ 1))
    early_paired = (early[:block].astype(F32) + early_across.astype(F32)).astype(BF16)
    copies_third = from_main(copies_opposite, 1)
    early_opposite = from_opposite(early_paired)
    self_total = after(self_total, early_paired)
    self_across = move(self_total[block:], lambda a, z: (a, z ^ 1))
    self_paired = (self_total[:block].astype(F32) + self_across[:block].astype(F32)).astype(BF16)
    if relay:
        vectors = self_total[2 * block :].astype(F32) + self_across[block:].astype(F32)
        vectors = vectors + move(vectors, lambda a, z: (a, z ^ 2))
    else:
        vectors = lax.psum(lax.psum(vectors, "narrow"), "wide", axis_index_groups=groups)
    in_third = from_main(after(in_opposite, early_paired), 1)
    self_opposite = from_opposite(self_paired)
    grad_early = to_owner(early_paired, after(early_opposite, self_paired))
    grad_unit, grad_cross = grad_early[:, : 2 * hidden_units], grad_early[:, 2 * hidden_units :]
    grad_self = to_owner(self_paired, self_opposite)

    def copied(first, last, value, opposite, beside, third, dtype):
        near_copy = jnp.where(main, value[first:last], beside[first:last])
        far_copy = jnp.where(main, opposite[first:last], third[first:last])
        return per_batch(near_copy, far_copy, dtype)

    copies = (copies_block, copies_opposite, copies_beside, copies_third)
    encoded_grad = copied(0, frame_rows, *copies, F32)
    output = copied(frame_rows, frame_rows + tok_rows, *copies, BF16)
    input_grad = copied(0, tok_rows, in_rows, in_opposite, in_beside, in_third, F32)

    def unpacked(grad):
        stack = jnp.stack([grad[:, head_cols * k : head_cols * (k + 1)] for k in range(3)])
        return stack, grad[:, 3 * head_cols :].T

    grad_self_proj, grad_out_one = unpacked(grad_self)
    grad_cross_proj, grad_out_two = unpacked(grad_cross)

    mine = lax.dynamic_slice_in_dim(vectors, 9 + 2 * odd, 2, 0)
    mine = jnp.where(home, mine, swap(mine))
    return (
        output,
        input_grad,
        encoded_grad,
        vectors[:3],
        vectors[3:6],
        mine[0].reshape(4, head_cols),
        vectors[6:9],
        mine[1],
        grad_self_proj,
        grad_cross_proj,
        jnp.stack([grad_out_one, grad_out_two]),
        grad_unit[:, :hidden_units],
        grad_unit[:, hidden_units:].T,
    )


def solution(mesh):
    in_specs = (
        P(None, "wide", None),
        P(None, "wide", None),
        P(),
        P(),
        P(),
        P(),
        P(None, "narrow"),
        P(),
        P("narrow"),
        P(None, "wide", "narrow"),
        P(None, "wide", "narrow"),
        P(None, "narrow", "wide"),
        P("wide", "narrow"),
        P("narrow", "wide"),
        P(None, "wide", None),
    )
    out_specs = (
        P(None, "wide", None),
        P(None, "wide", None),
        P(None, "wide", None),
        P(),
        P(),
        P(None, "narrow"),
        P(),
        P("narrow"),
        P(None, "wide", "narrow"),
        P(None, "wide", "narrow"),
        P(None, "narrow", "wide"),
        P("wide", "narrow"),
        P("narrow", "wide"),
    )
    return jax.shard_map(body, mesh=mesh, in_specs=in_specs, out_specs=out_specs, check_vma=False)
```

```python
from functools import partial

import jax
import jax.numpy as jnp
from jax import lax
from jax.experimental import pallas as pl
from jax.experimental.pallas import tpu as pltpu
from jax.sharding import PartitionSpec as P

HD = 64
LANES = 128
MAXLEN = 448
JITTER = 156
EPSILON = 1e-05
F32 = jnp.float32
BF16 = jnp.bfloat16
NN = (((1,), (0,)), ((), ()))
NT = (((1,), (1,)), ((), ()))
TN = (((0,), (0,)), ((), ()))
AXES = ("wide", "narrow")


def mm(left, right, dims=NN):
    return lax.dot_general(left, right, dims, preferred_element_type=F32)


def normalise(values):
    centre = values - jnp.mean(values, axis=-1, keepdims=True)
    spread = jnp.mean(centre * centre, axis=-1, keepdims=True)
    inverse = lax.rsqrt(spread + EPSILON)
    return centre * inverse, inverse


def norm_back(grad_rows, unit_rows, inverse, gain):
    scaled = grad_rows * gain
    centred = scaled - jnp.mean(scaled, axis=-1, keepdims=True)
    return (centred - unit_rows * jnp.mean(scaled * unit_rows, axis=-1, keepdims=True)) * inverse


def erf(x):
    x = jnp.clip(x, -3.832506856900711, 3.832506856900711)
    x2 = x * x
    top = x2 * 0.00022905065861350646 + 0.0034082910107109506
    top = top * x2 + 0.050955695062380861
    top = top * x2 + 0.18520832239976145
    top = top * x2 + 1.128379143519084
    low = x2 * -1.1791602954361697e-7 + 0.000023547966471313185
    low = low * x2 + 0.0010179625278914885
    low = low * x2 + 0.014070470171167667
    low = low * x2 + 0.11098505178285362
    low = low * x2 + 0.49746925110067538
    low = low * x2 + 1.0
    return x * top / low


def fetch(scalars, blocks, whole, sems, mixed=False, column=0):
    rows = whole.shape[1] // 8
    copies = []
    for group in range(2):
        for chip in range(4):
            for half in range(2):
                first = (2 * group + half) * rows
                if len(blocks) == 4:
                    source, place = blocks[chip], jnp.bitwise_xor(scalars[0], chip)
                else:
                    source, place = blocks[0], chip
                    first += 4 * chip * rows
                    if mixed:
                        core = scalars[5]
                        first = 4 * jnp.bitwise_xor(core, half) + 2 * core + jnp.bitwise_xor(scalars[6], group)
                        first = pl.multiple_of(rows * (8 * chip + first), rows)
                at = 2 * rows * place + rows * jnp.bitwise_xor(scalars[5], half)
                copies.append(
                    pltpu.make_async_copy(
                        source.at[pl.ds(first, rows), pl.ds(column, whole.shape[2])],
                        whole.at[group, pl.ds(pl.multiple_of(at, rows), rows), :],
                        sems.at[len(copies)],
                    )
                )
    for copy in copies:
        copy.start()
    return copies


def first_half(shape):
    return lax.broadcasted_iota(jnp.int32, shape, len(shape) - 1) < HD


def lay_window(scalars, own, partner, halo, out, margin, other):
    size = own.shape[0]
    odd = scalars[6]
    main = scalars[7] == 1
    before = jnp.where(odd == 0, margin, other)
    out[pl.ds(pl.multiple_of(before, 32), size), :] = jnp.where(main, own[...], partner[...])
    near_side = jnp.where(main, partner[:other, :], own[:other, :])
    far_side = jnp.where(main, partner[size - other :, :], own[size - other :, :])

    @pl.when(odd == 0)
    def _():
        out[:margin, :] = halo[...]
        out[margin + size :, :] = near_side

    @pl.when(odd == 1)
    def _():
        out[other + size :, :] = halo[...]
        out[:other, :] = far_side


def valid_rows(scalars, rows):
    place = lax.broadcasted_iota(jnp.int32, (rows, 1), 0)
    return (place >= scalars[1]) & (place < scalars[2])


def both(first, second, at, size):
    return jnp.concatenate([first[:, at : at + size], second[:, at : at + size]], axis=1)


def bias_row(biases, at, size):
    parts = biases[:, at : at + size].astype(F32)
    rows = [parts[8 * g : 8 * g + 1] + parts[8 * g + 2 : 8 * g + 3] + parts[8 * g + 4 : 8 * g + 5] for g in range(2)]
    return jnp.concatenate(rows, axis=1)


def halves(refs, cols):
    joined = jnp.concatenate([refs[p] for p in range(refs.shape[0])], axis=1)
    return joined[:, :cols], joined[:, cols:]


def by_pairs(values, out):
    for p in range(out.shape[0]):
        out[p] = values[:, p * LANES : (p + 1) * LANES]


def attend(pairs, rows, allowed, guard, q_all, k_all, v_all, o_out, den_out):
    half = first_half((rows, LANES))
    zero = jnp.zeros((), BF16)

    def one_pair(p, carry):
        q_pair, k_pair, v_pair = q_all[p], k_all[p], v_all[p]
        outs, dens = [], []
        for keep in (half, jnp.logical_not(half)):
            raw = mm(jnp.where(keep, q_pair, zero), k_pair, NT)
            weights = jnp.where(allowed, jnp.exp(raw), 0.0)
            total = jnp.sum(weights, axis=1, keepdims=True)
            if guard:
                total = jnp.where(total > 0.0, total, 1.0)
            outs.append(mm(weights.astype(BF16), v_pair) / total)
            dens.append(jnp.broadcast_to(total, (rows, LANES)))
        o_out[p] = jnp.where(half, outs[0], outs[1])
        den_out[p] = jnp.where(half, dens[0], dens[1])
        return carry

    lax.fori_loop(0, pairs, one_pair, 0)


def out_product(o_all, whole, cols):
    first, second = halves(o_all, cols)
    first, second = first.astype(BF16), second.astype(BF16)
    return mm(first, whole[0, :, 3 * cols :], NT) + mm(second, whole[1, :, 3 * cols :], NT)


def self_forward(
    scalars, own, partner, halo, gains, shifts, biases, w0, w1, w2, w3,
    hidden_out, norm_out, q_out, k_out, v_out, o_out, den_out, part_out, whole, sems,
):
    copies = fetch(scalars, (w0, w1, w2, w3), whole, sems)
    rows = hidden_out.shape[0]
    pairs = q_out.shape[0]
    cols = pairs * LANES // 2
    margin = halo.shape[0]
    lay_window(scalars, own, partner, halo, hidden_out, margin, margin)
    unit, _ = normalise(hidden_out[...].astype(F32))
    norm = (unit * gains[0:1, :] + shifts[0:1, :]).astype(BF16)
    norm_out[...] = norm
    valid = valid_rows(scalars, rows)
    for copy in copies:
        copy.wait()
    first = mm(norm, whole[0, :, : 3 * cols])
    second = mm(norm, whole[1, :, : 3 * cols])
    query = (both(first, second, 0, cols) + bias_row(biases, 0 * cols, cols)).astype(BF16).astype(F32)
    by_pairs(jnp.where(valid, query * HD ** -0.5, 0.0).astype(BF16), q_out)
    by_pairs(both(first, second, cols, cols).astype(BF16), k_out)
    by_pairs((both(first, second, 2 * cols, cols) + bias_row(biases, 1 * cols, cols)).astype(BF16), v_out)
    q_place = lax.broadcasted_iota(jnp.int32, (rows, rows), 0)
    k_place = lax.broadcasted_iota(jnp.int32, (rows, rows), 1)
    allowed = (k_place <= q_place) & (k_place >= scalars[1])
    attend(pairs, rows, allowed, True, q_out, k_out, v_out, o_out, den_out)
    part_out[...] = out_product(o_out, whole, cols).astype(BF16)


def frame_project(
    mixed, scalars, own, partner, halo, biases, w0, frame_out, k_out, v_out, whole, sems
):
    copies = fetch(scalars, (w0,), whole, sems, mixed)
    pairs = k_out.shape[0]
    cols = pairs * LANES // 2
    margin = halo.shape[0]
    lay_window(scalars, own, partner, halo, frame_out, margin, own.shape[0] - margin)
    for copy in copies:
        copy.wait()
    first = mm(frame_out[...], whole[0, :, cols : 3 * cols])
    second = mm(frame_out[...], whole[1, :, cols : 3 * cols])
    by_pairs(both(first, second, 0, cols).astype(BF16), k_out)
    by_pairs((both(first, second, cols, cols) + bias_row(biases, 3 * cols, cols)).astype(BF16), v_out)


def cross_forward(
    mixed, scalars, hidden, mine, other, gains, shifts, outs_bias, biases, k_all, v_all, w0,
    resid_out, norm_out, q_out, o_out, den_out, part_out, whole, sems,
):
    copies = fetch(scalars, (w0,), whole, sems, mixed)
    rows = hidden.shape[0]
    pairs = q_out.shape[0]
    cols = pairs * LANES // 2
    summed = mine[...].astype(F32) + other[...].astype(F32)
    resid = hidden[...].astype(F32) + (summed + outs_bias[0:1, :])
    resid_out[...] = resid
    unit, _ = normalise(resid)
    norm = (unit * gains[1:2, :] + shifts[1:2, :]).astype(BF16)
    norm_out[...] = norm
    valid = valid_rows(scalars, rows)
    for copy in copies:
        copy.wait()
    query = jnp.concatenate([mm(norm, whole[0, :, :cols]), mm(norm, whole[1, :, :cols])], axis=1)
    query = (query + bias_row(biases, 2 * cols, cols)).astype(BF16).astype(F32)
    by_pairs(jnp.where(valid, query * HD ** -0.5, 0.0).astype(BF16), q_out)
    frame = lax.broadcasted_iota(jnp.int32, (1, k_all.shape[1]), 1)
    allowed = (frame >= scalars[3]) & (frame < scalars[4])
    attend(pairs, rows, allowed, False, q_out, k_all, v_all, o_out, den_out)
    part_out[...] = out_product(o_out, whole, cols).astype(BF16)


CHUNK = 768


def unit_forward(
    mixed, scalars, resid, mine, other, gains, shifts, outs_bias, fc_bias, own, partner, halo,
    w0,
    resid_out, norm_out, top_out, act_out, pre_out, part_out, back_out, sum_out, whole, sems,
):
    copies = fetch(scalars, (w0,), whole, sems, mixed, whole.shape[1])
    margin = halo.shape[0]
    lay_window(scalars, own, partner, halo, top_out, margin, margin)
    valid = valid_rows(scalars, resid.shape[0])
    top_out[...] = jnp.where(valid, top_out[...], jnp.zeros((), BF16))
    summed = mine[...].astype(F32) + other[...].astype(F32)
    resid_two = resid[...] + (summed + outs_bias[1:2, :])
    resid_out[...] = resid_two
    unit, _ = normalise(resid_two)
    norm_out[...] = (unit * gains[2:3, :] + shifts[2:3, :]).astype(BF16)
    for copy in copies:
        copy.wait()
    units = act_out.shape[1] // 2
    steps = units // CHUNK

    def one_chunk(j, carry):
        group = j // steps
        at_in = pl.ds(pl.multiple_of((j - group * steps) * CHUNK, CHUNK), CHUNK)
        at_back = pl.ds(pl.multiple_of(units + (j - group * steps) * CHUNK, CHUNK), CHUNK)
        at = pl.ds(pl.multiple_of(j * CHUNK, CHUNK), CHUNK)
        parts = fc_bias[:, at_in].astype(F32)
        parts = jnp.where(group == 0, parts[:8], parts[8:])
        pre = mm(norm_out[...], whole[group, :, at_in]) + (parts[1:2] + parts[3:4] + parts[5:6])
        cdf = 0.5 * (1.0 + erf(pre * 0.7071067811865476))
        act_out[:, at] = (pre * cdf).astype(BF16)
        slope = cdf + pre * (jnp.exp(-0.5 * pre * pre) * 0.3989422804014327)
        grad = (slope * mm(top_out[...], whole[group, :, at_back])).astype(BF16)
        pre_out[:, at] = grad
        sum_out[:, at] = jnp.sum(grad.astype(F32), axis=0, keepdims=True)
        return carry

    lax.fori_loop(0, 2 * steps, one_chunk, 0)
    back_out[...] = (
        mm(pre_out[:, :units], whole[0, :, :units], NT) + mm(pre_out[:, units:], whole[1, :, :units], NT)
    ).astype(BF16)
    part_out[...] = (
        mm(act_out[:, :units], whole[0, :, units:], NT) + mm(act_out[:, units:], whole[1, :, units:], NT)
    ).astype(BF16)


def send_rows(scalars, total, mid_out, pair_out, cross_out):
    margin = pair_out.shape[0]
    size = mid_out.shape[0]
    odd = scalars[6] == 1
    low = total.astype(BF16)
    head = low[:margin]
    tail = low[margin + size :]
    mid_out[...] = low[margin : margin + size]
    pair_out[...] = jnp.where(odd, head, tail)
    cross_out[...] = jnp.where(odd, tail, head)


def finish_output(scalars, resid, mine, other, outs_bias, mid_out, pair_out, cross_out):
    summed = mine[...].astype(F32) + other[...].astype(F32)
    total = resid[...] + (summed + outs_bias[2:3, :])
    total = jnp.where(valid_rows(scalars, resid.shape[0]), total, 0.0)
    send_rows(scalars, total, mid_out, pair_out, cross_out)


def column_sum(values):
    return jnp.sum(values, axis=0, keepdims=True)


def attend_back(pairs, rows, allowed, drop, q_all, k_all, v_all, o_all, den_all, dq_out, dk_out, dv_out):
    count = k_all.shape[1]
    half = first_half((count, LANES))
    zero = jnp.zeros((), BF16)
    upper = lax.broadcasted_iota(jnp.int32, (LANES, rows), 0) < HD

    def one_pair(p, carry):
        q_pair, k_pair, v_pair = q_all[p], k_all[p], v_all[p]
        grad = drop[p].astype(F32)
        den = den_all[p]
        grad_sums = (grad / den).astype(BF16)
        drift_all = (grad * o_all[p] / den).T
        found = []
        for t in range(2):
            keep = half if t == 0 else jnp.logical_not(half)
            drift = jnp.sum(drift_all[t * HD : (t + 1) * HD, :], axis=0, keepdims=True)
            raw = mm(jnp.where(keep, k_pair, zero), q_pair, NT)
            weights = jnp.where(allowed, jnp.exp(raw), 0.0)
            prob = mm(jnp.where(keep, v_pair, zero), grad_sums, NT)
            score = (weights * (prob - drift)).astype(BF16)
            found.append(
                (
                    mm(k_pair, score, TN),
                    mm(score, q_pair),
                    mm(weights.astype(BF16), grad_sums),
                )
            )
        dq_out[p] = (jnp.where(upper, found[0][0], found[1][0]).T * HD ** -0.5).astype(BF16)
        dk_out[p] = jnp.where(half, found[0][1], found[1][1]).astype(dk_out.dtype)
        dv_out[p] = jnp.where(half, found[0][2], found[1][2]).astype(dv_out.dtype)
        return carry

    lax.fori_loop(0, pairs, one_pair, 0)


def open_gradient(grad, whole, o_all, grad_out, low_out, att_out, drop, copies):
    pairs = drop.shape[0]
    cols = pairs * LANES // 2
    grad_out[...] = grad
    low = grad.astype(BF16)
    low_out[...] = low
    for p in range(pairs):
        att_out[:, p * LANES : (p + 1) * LANES] = o_all[p].astype(BF16)
    for copy in copies:
        copy.wait()
    first = mm(low, whole[0, :, 3 * cols :]).astype(BF16)
    second = mm(low, whole[1, :, 3 * cols :]).astype(BF16)
    by_pairs(jnp.concatenate([first, second], axis=1), drop)


def head_sums(dq_out, dv_out, heads_out):
    for p in range(dq_out.shape[0]):
        heads_out[0:1, p * LANES : (p + 1) * LANES] = column_sum(dq_out[p].astype(F32))
        heads_out[1:2, p * LANES : (p + 1) * LANES] = column_sum(dv_out[p].astype(F32))


def cross_backward(
    mixed, scalars, resid, cotangent, mine, other, gains, q_all, k_all, v_all, o_all, den_all,
    w0,
    grad_out, low_out, att_out, dq_out, dk_out, dv_out, part_out, sums_out, heads_out,
    drop, whole, sems,
):
    copies = fetch(scalars, (w0,), whole, sems, mixed)
    rows = resid.shape[0]
    pairs = q_all.shape[0]
    cols = pairs * LANES // 2
    unit, inverse = normalise(resid[...])
    grad_norm = mine[...].astype(F32) + other[...].astype(F32)
    top = cotangent[...].astype(F32)
    grad = top + norm_back(grad_norm, unit, inverse, gains[2:3, :])
    sums_out[0:1, :] = column_sum(grad_norm * unit)
    sums_out[1:2, :] = column_sum(grad_norm)
    sums_out[2:3, :] = column_sum(top)
    sums_out[3:4, :] = column_sum(grad)
    open_gradient(grad, whole, o_all, grad_out, low_out, att_out, drop, copies)
    frame = lax.broadcasted_iota(jnp.int32, (k_all.shape[1], 1), 0)
    allowed = (frame >= scalars[3]) & (frame < scalars[4])
    attend_back(pairs, rows, allowed, drop, q_all, k_all, v_all, o_all, den_all, dq_out, dk_out, dv_out)
    first, second = halves(dq_out, cols)
    part_out[...] = (mm(first, whole[0, :, :cols], NT) + mm(second, whole[1, :, :cols], NT)).astype(BF16)
    head_sums(dq_out, dv_out, heads_out)


def self_backward(
    scalars, resid, top, mine, other, gains, q_all, k_all, v_all, o_all, den_all,
    w0, w1, w2, w3,
    grad_out, low_out, att_out, dq_out, dk_out, dv_out, part_out, sums_out, heads_out,
    drop, whole, sems,
):
    copies = fetch(scalars, (w0, w1, w2, w3), whole, sems)
    rows = resid.shape[0]
    pairs = q_all.shape[0]
    cols = pairs * LANES // 2
    unit, inverse = normalise(resid[...])
    grad_norm = mine[...].astype(F32) + other[...].astype(F32)
    grad = top[...] + norm_back(grad_norm, unit, inverse, gains[1:2, :])
    sums_out[0:1, :] = column_sum(grad_norm * unit)
    sums_out[1:2, :] = column_sum(grad_norm)
    sums_out[2:3, :] = column_sum(grad)
    open_gradient(grad, whole, o_all, grad_out, low_out, att_out, drop, copies)
    k_place = lax.broadcasted_iota(jnp.int32, (rows, rows), 0)
    q_place = lax.broadcasted_iota(jnp.int32, (rows, rows), 1)
    allowed = (k_place <= q_place) & (k_place >= scalars[1])
    attend_back(pairs, rows, allowed, drop, q_all, k_all, v_all, o_all, den_all, dq_out, dk_out, dv_out)
    pieces = [halves(piece, cols) for piece in (dq_out, dk_out, dv_out)]
    total = jnp.zeros((rows, part_out.shape[1]), F32)
    for group in range(2):
        joined = jnp.concatenate([piece[group] for piece in pieces], axis=1)
        total = total + mm(joined, whole[group, :, : 3 * cols], NT)
    part_out[...] = total.astype(BF16)
    head_sums(dq_out, dv_out, heads_out)


def input_backward(
    scalars, hidden, top, mine, other, gains, sums_one, sums_two, heads_one, heads_two, unit_sums,
    mid_out, pair_out, cross_out, vec_out,
):
    unit, inverse = normalise(hidden[...].astype(F32))
    grad_norm = mine[...].astype(F32) + other[...].astype(F32)
    grad = top[...] + norm_back(grad_norm, unit, inverse, gains[0:1, :])
    send_rows(scalars, grad, mid_out, pair_out, cross_out)
    heads = [heads_one[0:1, :], heads_one[1:2, :], heads_two[0:1, :], heads_two[1:2, :]]
    cols = heads[0].shape[1] // 2
    units = unit_sums.shape[1] // 2
    own = jnp.concatenate([row[:, :cols] for row in heads], axis=1)
    rest = jnp.concatenate([row[:, cols:] for row in heads], axis=1)
    own_units, rest_units = unit_sums[:, :units], unit_sums[:, units:]
    odd = scalars[6] == 1
    rows = [
        column_sum(grad_norm * unit), sums_one[0:1, :], sums_two[0:1, :],
        column_sum(grad_norm), sums_one[1:2, :], sums_two[1:2, :],
        sums_one[2:3, :], sums_two[3:4, :], sums_two[2:3, :],
        jnp.where(odd, rest, own), jnp.where(odd, rest_units, own_units),
        jnp.where(odd, own, rest), jnp.where(odd, own_units, rest_units),
    ]
    for k, row in enumerate(rows):
        vec_out[k : k + 1, :] = row
    vec_out[len(rows) :, :] = jnp.zeros((vec_out.shape[0] - len(rows), vec_out.shape[1]), F32)


def frame_backward(mixed, scalars, dk_all, dv_all, w0, kept_out, given_out, total, whole, sems):
    copies = fetch(scalars, (w0,), whole, sems, mixed)
    pairs = dk_all.shape[0]
    cols = pairs * LANES // 2
    size = kept_out.shape[0]
    frames = dk_all.shape[1]
    near = (frames - size) * 3 // 8
    far = frames - size - near
    step = frames // 2
    for copy in copies:
        copy.wait()

    def one_part(j, carry):
        at = pl.ds(pl.multiple_of(j * step, step), step)
        keys = jnp.concatenate([dk_all[p, at, :] for p in range(pairs)], axis=1)
        values = jnp.concatenate([dv_all[p, at, :] for p in range(pairs)], axis=1)
        part = jnp.zeros((step, total.shape[1]), F32)
        for group in range(2):
            cut = slice(group * cols, (group + 1) * cols)
            joined = jnp.concatenate([keys[:, cut], values[:, cut]], axis=1)
            part = part + mm(joined, whole[group, :, cols : 3 * cols], NT)
        total[at, :] = part
        return carry

    lax.fori_loop(0, 2, one_part, 0)
    odd = scalars[6]
    main = scalars[7] == 1
    lead = pl.multiple_of(jnp.where(odd == 0, near, far), 32)
    near_at = pl.multiple_of(jnp.where(odd == 0, 0, far + size), 32)
    far_at = pl.multiple_of(jnp.where(odd == 0, near + size, 0), 32)
    mid = total[pl.ds(lead, size), :].astype(BF16)
    near_part = total[pl.ds(near_at, near), :].astype(BF16)
    far_part = total[pl.ds(far_at, far), :].astype(BF16)

    @pl.when(main)
    def _():
        kept_out[...] = mid
        given_out[:near, :] = near_part
        given_out[near:, :] = far_part

    @pl.when(jnp.logical_not(main))
    def _():
        given_out[...] = mid
        kept_out[:near, :] = near_part
        kept_out[near:, :] = far_part


def send_grads(scalars, whole, out, sems, extra=None):
    rows = whole.shape[1] // 8
    added = 0 if extra is None else extra.shape[0]
    copies = []
    for chip in range(4):
        start = chip * (4 * rows + added)
        for group in range(2):
            for half in range(2):
                at = 2 * rows * chip + rows * jnp.bitwise_xor(scalars[5], half)
                copies.append(
                    pltpu.make_async_copy(
                        whole.at[group, pl.ds(pl.multiple_of(at, rows), rows), :],
                        out.at[pl.ds(start + (2 * group + half) * rows, rows), :],
                        sems.at[len(copies)],
                    )
                )
        if added:
            copies.append(
                pltpu.make_async_copy(extra, out.at[pl.ds(start + 4 * rows, added), :], sems.at[len(copies)])
            )
    for copy in copies:
        copy.start()
    for copy in copies:
        copy.wait()


def unit_grads(scalars, norm, pre, top, act, out, whole, sems):
    units = pre.shape[1] // 2
    found = mm(norm[...], pre[...], TN).astype(BF16)
    for group in range(2):
        whole[group, :, :units] = found[:, group * units : (group + 1) * units]
    found = mm(top[...], act[...], TN).astype(BF16)
    for group in range(2):
        whole[group, :, units:] = found[:, group * units : (group + 1) * units]
    send_grads(scalars, whole, out, sems)


def all_heads(refs):
    return jnp.concatenate([refs[p] for p in range(refs.shape[0])], axis=1)


def by_groups(found, whole):
    for group in range(2):
        parts = []
        for piece in found:
            size = piece.shape[1] // 2
            parts.append(piece[:, group * size : (group + 1) * size])
        whole[group] = jnp.concatenate(parts, axis=1).astype(BF16)


def cross_grads(scalars, norm, frames, low, att, dq, dk, dv, out, whole, sems):
    cols = att.shape[1]
    pair = mm(frames[...], jnp.concatenate([all_heads(dk), all_heads(dv)], axis=1), TN)
    found = [mm(norm[...], all_heads(dq), TN), pair[:, :cols], pair[:, cols:], mm(low[...], att[...], TN)]
    by_groups(found, whole)
    send_grads(scalars, whole, out, sems)


def self_grads(scalars, norm, low, att, dq, dk, dv, vectors, out, low_vectors, whole, sems):
    low_vectors[...] = vectors[...].astype(BF16)
    cols = att.shape[1]
    three = mm(norm[...], jnp.concatenate([all_heads(dq), all_heads(dk), all_heads(dv)], axis=1), TN)
    found = [three[:, :cols], three[:, cols : 2 * cols], three[:, 2 * cols :], mm(low[...], att[...], TN)]
    by_groups(found, whole)
    send_grads(scalars, whole, out, sems, low_vectors)


SMEM = pl.BlockSpec(memory_space=pltpu.SMEM)
VMEM = pl.BlockSpec(memory_space=pltpu.VMEM)
ANY = pl.BlockSpec(memory_space=pl.ANY)


def shape(dims, dtype):
    return jax.ShapeDtypeStruct(tuple(dims), dtype)


def kernel_call(kernel, name, cost, operands, spaces, outs, out_spaces=None, scratch=()):
    return pl.pallas_call(
        kernel,
        out_shape=tuple(outs),
        in_specs=list(spaces),
        out_specs=tuple(out_spaces or [VMEM] * len(outs)),
        scratch_shapes=list(scratch),
        compiler_params=pltpu.CompilerParams(vmem_limit_bytes=56 * 1024 * 1024),
        cost_estimate=pl.CostEstimate(flops=int(cost * 2e9), transcendentals=0, bytes_accessed=1 << 20),
        name=name,
    )(*operands)


def body(
    hidden, encoded, token_lengths, frame_counts, ln_gain, ln_bias, head_bias, out_bias, fc_bias,
    self_proj, cross_proj, out_proj, fc_in, fc_out, cotangent,
):
    wide = lax.axis_size("wide")
    depth = lax.axis_size("narrow")
    tok_rows, width = hidden.shape[1:]
    frame_rows = encoded.shape[1]
    swing = (MAXLEN - tok_rows) // 2
    ratio = frame_rows // tok_rows
    near = ratio * swing
    far = frame_rows - near
    assert far >= near + JITTER and 8 * near == 3 * frame_rows
    assert depth == 4 and hidden.shape[0] == 2
    rows = tok_rows + 2 * swing
    frames = near + frame_rows + far
    shard = width // wide
    block = 2 * shard
    head_cols = head_bias.shape[1]
    cols = 2 * head_cols
    pairs = cols // LANES
    hidden_units = fc_bias.shape[0]
    units = 2 * hidden_units

    w = lax.axis_index("wide")
    n = lax.axis_index("narrow")
    chip = w // 2
    core = w % 2
    batch = n // 2
    odd = n % 2
    item = 2 * chip + odd
    main = core == odd
    home = core == batch
    relay = wide == 8

    def move(value, rule):
        pairs_list = []
        for ws in range(wide):
            for ns in range(depth):
                target = rule(ws, ns)
                if target is not None and 0 <= target[0] < wide:
                    pairs_list.append((ws * depth + ns, target[0] * depth + target[1]))
        return lax.ppermute(value, AXES, pairs_list)

    def swap(value):
        return move(value, lambda a, z: (a ^ 1, z))

    def after(value, *events):
        return lax.optimization_barrier((value, *events))[0]

    def pick(value, index):
        return lax.dynamic_index_in_dim(value, index, 0, keepdims=False)

    bias_vector = jnp.concatenate([head_bias.reshape(-1), fc_bias])
    bias_high = lax.reduce_precision(bias_vector, 8, 7)
    bias_rest = bias_vector - bias_high
    bias_middle = lax.reduce_precision(bias_rest, 8, 7)
    bias_parts = jnp.stack([bias_high, bias_middle, bias_rest - bias_middle]).astype(BF16)
    bias_parts = jnp.concatenate([bias_parts.reshape(6, width), jnp.zeros((2, width), BF16)], axis=0)

    def group(stack, out):
        return jnp.concatenate([stack[0], stack[1], stack[2], out.T], axis=1)

    def away(value):
        return move(value, lambda a, z: (a ^ 1, z) if a % 2 != z // 2 else None)

    def two_groups(value):
        opposite = move(value, lambda a, z: (a, z ^ 2) if a % 2 == z // 2 else None)
        same = jnp.where(home, value, opposite)
        return same, move(same, lambda a, z: (a, z ^ 1))

    groups = [list(range(k, wide, 2)) for k in range(2)]

    def in_quarters(joined):
        if relay:
            return lax.all_gather(joined, "wide", axis=0, tiled=True, axis_index_groups=groups)
        size = joined.shape[1]
        full = lax.all_gather(joined.reshape(2, 2, shard, size), "wide", axis_index_groups=groups)
        full = jnp.where(core == 0, full, full[:, :, ::-1])
        full = jnp.swapaxes(full, 0, 1).reshape(2, 4, width // 4, size)
        return jnp.swapaxes(full, 0, 1).reshape(-1, size)

    def between_chips(joined, *events):
        if relay:
            joined = after(joined, *events)
            return [joined] + [move(joined, partial(lambda k, a, z: (a ^ k, z), 2 * k)) for k in (1, 2, 3)]
        full = in_quarters(joined)
        return [full[j * width // 2 : (j + 1) * width // 2] for j in range(4)]

    def edge(value, margin):
        start = jnp.where(odd == 0, value.shape[1] - margin, 0)
        return lax.dynamic_slice(value, (batch, start, 0), (1, margin, width))[0]

    def halo_rule(a, z):
        if a % 2 == z % 2:
            return None
        return (a + 1, z) if z % 2 == 0 else (a - 1, z)

    edges = jnp.concatenate([edge(hidden, swing), edge(cotangent, swing), edge(encoded, near)], axis=0)
    halo = move(edges, halo_rule)
    halo = jnp.where(main, halo, move(halo, lambda a, z: (a ^ 1, z) if a % 2 == z % 2 else None))
    hidden_halo, top_halo, frame_halo = halo[:swing], halo[swing : 2 * swing], halo[2 * swing :]

    rest_piece = jnp.concatenate([group(cross_proj, out_proj[1]), fc_in, fc_out.T], axis=1)
    if relay:
        rest_w = lax.all_gather(rest_piece, AXES, axis=0, tiled=True)
    else:
        rest_here = jnp.concatenate([rest_piece, away(rest_piece)], axis=0)
        rest_w = in_quarters(jnp.concatenate(two_groups(rest_here), axis=0))
    self_piece = group(self_proj, out_proj[0])
    self_got = two_groups(jnp.concatenate([self_piece, away(self_piece), bias_parts], axis=0))
    self_own = after(jnp.concatenate([x[:block] for x in self_got], axis=0), halo)
    self_w = between_chips(self_own)
    biases = jnp.concatenate([x[block:] for x in self_got], axis=0)

    own_hidden = pick(hidden, batch)
    own_top = pick(after(cotangent, self_own), batch)
    own_frames = pick(after(encoded, self_own), batch)
    token_lengths = after(token_lengths, self_own)
    lengths = pick(token_lengths, batch)
    counts = pick(frame_counts, batch)
    items = jnp.arange(lengths.shape[0], dtype=jnp.int32)
    tok_lo = jnp.sum(jnp.where(items < item, lengths, 0)) - (tok_rows * item - swing)
    tok_hi = tok_lo + jnp.sum(jnp.where(items == item, lengths, 0))
    frame_start = frame_rows * item - jnp.where(odd == 0, near, far)
    frame_lo = jnp.sum(jnp.where(items < item, counts, 0)) - frame_start
    frame_hi = frame_lo + jnp.sum(jnp.where(items == item, counts, 0))
    nothing = jnp.zeros((), jnp.int32)
    here, order = (chip, core) if relay else (nothing, nothing)
    scalars = jnp.stack(
        [here, tok_lo, tok_hi, frame_lo, frame_hi, order, odd, main.astype(jnp.int32)]
    ).astype(jnp.int32)

    low_shape = shape((rows, width), BF16)
    wide_f32 = shape((rows, width), F32)
    head_b = shape((pairs, rows, LANES), BF16)
    head_f = shape((pairs, rows, LANES), F32)
    frame_b = shape((pairs, frames, LANES), BF16)
    att_shape = shape((rows, cols), BF16)
    frame_full = shape((frames, width), BF16)
    sems = pltpu.SemaphoreType.DMA((20,))
    head_scratch = [pltpu.VMEM((2, width, width), BF16), sems]
    unit_scratch = [pltpu.VMEM((2, width, 2 * hidden_units), BF16), sems]

    hidden_rows, low_one, self_q, self_k, self_v, self_o, self_den, part = kernel_call(
        self_forward, "self_forward", 8,
        (scalars, own_hidden, swap(own_hidden), hidden_halo, ln_gain, ln_bias, biases, *self_w),
        [SMEM] + [VMEM] * 6 + [ANY] * 4,
        [low_shape, low_shape, head_b, head_b, head_b, head_f, head_f, low_shape],
        scratch=head_scratch,
    )
    frame_window, cross_k, cross_v = kernel_call(
        partial(frame_project, relay), "frame_project", 7,
        (scalars, own_frames, swap(own_frames), after(frame_halo, part), biases, rest_w),
        [SMEM] + [VMEM] * 4 + [ANY],
        [frame_full, frame_b, frame_b],
        scratch=head_scratch,
    )
    resid_one, low_two, cross_q, cross_o, cross_den, part_two = kernel_call(
        partial(cross_forward, relay), "cross_forward", 11,
        (scalars, hidden_rows, part, swap(part), ln_gain, ln_bias, out_bias, biases, cross_k, cross_v, rest_w),
        [SMEM] + [VMEM] * 9 + [ANY],
        [wide_f32, low_shape, head_b, head_f, head_f, low_shape],
        scratch=head_scratch,
    )
    act_shape = shape((rows, units), BF16)
    resid_two, low_three, top_rows, low_act, grad_pre, part_three, back_three, unit_sums = kernel_call(
        partial(unit_forward, relay), "unit_forward", 14,
        (scalars, resid_one, part_two, swap(part_two), ln_gain, ln_bias, out_bias, biases, own_top, swap(own_top), top_halo, rest_w),
        [SMEM] + [VMEM] * 10 + [ANY],
        [wide_f32, low_shape, low_shape, act_shape, act_shape, low_shape, low_shape, shape((1, units), F32)],
        scratch=unit_scratch,
    )
    other_back = swap(back_three)
    other_three = swap(part_three)

    def between_back(grads):
        if relay:
            return lax.psum_scatter(grads, "wide", scatter_dimension=0, tiled=True, axis_index_groups=groups)
        size = grads.shape[1]
        full = jnp.swapaxes(grads.reshape(4, 2, width // 4, size), 0, 1).reshape(2, wide // 2, 2, shard, size)
        full = jnp.swapaxes(jnp.where(core == 0, full, full[:, :, ::-1]), 0, 1)
        total = lax.psum_scatter(full, "wide", scatter_dimension=0, axis_index_groups=groups)
        return total.reshape(2 * block, size)

    def from_opposite(paired):
        return move(paired, lambda a, z: (a, z ^ 2) if a % 2 != z // 2 else None)

    def to_owner(paired, opposite):
        summed = paired.astype(F32) + opposite.astype(F32)
        passed = move(summed[shard:].astype(BF16), lambda a, z: (a ^ 1, z) if a % 2 == z // 2 else None)
        return jnp.where(home, summed[:shard], passed.astype(F32))

    def grads_of(kernel, name, cost, size, scratch, *operands, added=0):
        return kernel_call(
            kernel, name, cost, (scalars, *operands),
            [SMEM] + [VMEM] * len(operands),
            [shape((2 * width + 4 * added, size), BF16)],
            [ANY],
            scratch=scratch,
        )[0]

    grads_unit = grads_of(
        unit_grads, "unit_grads", 9, 2 * hidden_units, unit_scratch, low_three, grad_pre, top_rows, low_act
    )
    unit_total = between_back(grads_unit)
    sums_shape = shape((8, width), F32)
    heads_shape = shape((8, cols), F32)
    drop_scratch = [pltpu.VMEM((pairs, rows, LANES), BF16)]
    grad_two, low_grad_two, low_cross, cq_grad, ck_grad, cv_grad, back_two, sums_two, heads_two = kernel_call(
        partial(cross_backward, relay), "cross_backward", 21,
        (scalars, resid_two, top_rows, back_three, after(other_back, grads_unit), ln_gain, cross_q, cross_k, cross_v, cross_o, cross_den, rest_w),
        [SMEM] + [VMEM] * 10 + [ANY],
        [wide_f32, low_shape, att_shape, head_b, frame_b, frame_b, low_shape, sums_shape, heads_shape],
        scratch=drop_scratch + head_scratch,
    )
    def cross_rule(a, z):
        if a % 2 == z % 2:
            return None
        return (a - 2, z ^ 1) if z % 2 == 0 else (a + 2, z ^ 1)

    def pair_rule(a, z):
        return None if a % 2 == z % 2 else (a, z ^ 1)

    def from_main(value, step):
        return move(value, lambda a, z: (a, z ^ step) if a % 2 == z % 2 else None)

    def per_batch(near_copy, far_copy, dtype):
        near_copy, far_copy = near_copy.astype(dtype), far_copy.astype(dtype)
        return jnp.stack(
            [jnp.where(batch == 0, near_copy, far_copy), jnp.where(batch == 0, far_copy, near_copy)]
        )

    def token_block(mid, from_pair, from_cross):
        above = jnp.where(odd == 1, from_pair, from_cross)
        below = jnp.where(odd == 1, from_cross, from_pair)
        return jnp.concatenate([mid[:swing] + above, mid[swing:-swing], mid[-swing:] + below], axis=0)

    edge_shape = shape((swing, width), BF16)
    slice_shapes = [shape((tok_rows, width), BF16), edge_shape, edge_shape]
    grads_cross = grads_of(
        cross_grads, "cross_grads", 8, width, head_scratch,
        low_two, frame_window, low_grad_two, low_cross, cq_grad, ck_grad, cv_grad,
    )
    kept, given = kernel_call(
        partial(frame_backward, relay), "frame_backward", 7,
        (scalars, after(ck_grad, grads_cross), cv_grad, rest_w),
        [SMEM] + [VMEM] * 2 + [ANY],
        [shape((frame_rows, width), BF16)] * 2,
        scratch=[pltpu.VMEM((frames, width), F32)] + head_scratch,
    )
    out_mid, out_pair, out_cross = kernel_call(
        finish_output, "finish_output", 3,
        (scalars, resid_two, part_three, after(other_three, kept), out_bias),
        [SMEM] + [VMEM] * 4,
        slice_shapes,
    )
    half_sum = (kept.astype(F32) + swap(given).astype(F32)).astype(BF16)
    half_sum = after(half_sum, out_mid)
    to_pair = jnp.concatenate([half_sum[near:], out_pair], axis=0)
    to_cross = jnp.concatenate([half_sum[:near], out_cross], axis=0)
    from_pair = move(to_pair, pair_rule)
    from_cross = move(to_cross, cross_rule)
    cross_total = between_back(after(grads_cross, unit_total, to_pair, to_cross))
    grad_one, low_grad_one, low_self, sq_grad, sk_grad, sv_grad, back_one, sums_one, heads_one = kernel_call(
        self_backward, "self_backward", 12,
        (scalars, resid_one, grad_two, back_two, after(swap(back_two), to_pair, to_cross), ln_gain, self_q, self_k, self_v, self_o, self_den, *self_w),
        [SMEM] + [VMEM] * 10 + [ANY] * 4,
        [wide_f32, low_shape, att_shape, head_b, head_b, head_b, low_shape, sums_shape, heads_shape],
        scratch=drop_scratch + head_scratch,
    )
    extra = jnp.where(
        odd == 1,
        jnp.concatenate([from_pair[:far], from_cross[:near]], axis=0),
        jnp.concatenate([from_cross[:near], from_pair[:far]], axis=0),
    )
    out_rows = token_block(out_mid, from_pair[far:], from_cross[near:])
    copies_block = after(jnp.concatenate([half_sum + extra, out_rows], axis=0), back_one)
    copies_opposite = from_main(copies_block, 2)
    copies_beside = from_main(copies_block, 1)
    in_mid, in_pair, in_cross, vectors = kernel_call(
        input_backward, "input_backward", 4,
        (scalars, hidden_rows, grad_one, back_one, after(swap(back_one), copies_block), ln_gain, sums_one, sums_two, heads_one, heads_two, unit_sums),
        [SMEM] + [VMEM] * 10,
        slice_shapes + [shape((16, width), F32)],
    )
    in_from_pair = move(in_pair, pair_rule)
    in_from_cross = move(in_cross, cross_rule)
    added = vectors.shape[0]
    grads_self = grads_of(
        self_grads, "self_grads", 5, width, [pltpu.VMEM((added, width), BF16)] + head_scratch,
        after(low_one, in_mid), low_grad_one, low_self, sq_grad, sk_grad, sv_grad, vectors,
        added=added,
    )
    in_rows = after(token_block(in_mid, in_from_pair, in_from_cross), grads_self)
    if relay:
        self_total = between_back(after(grads_self, cross_total, in_rows, copies_beside))
    else:
        parts = grads_self.reshape(4, -1, width)[:, : width // 2].reshape(-1, width)
        self_total = jnp.concatenate([between_back(parts), jnp.zeros((added, width), BF16)], axis=0)
    in_opposite = from_main(in_rows, 2)
    in_beside = from_main(in_rows, 1)
    early = jnp.concatenate([unit_total, cross_total], axis=1)
    early_across = move(early[block:], lambda a, z: (a, z ^ 1))
    early_paired = (early[:block].astype(F32) + early_across.astype(F32)).astype(BF16)
    copies_third = from_main(copies_opposite, 1)
    early_opposite = from_opposite(early_paired)
    self_total = after(self_total, early_paired)
    self_across = move(self_total[block:], lambda a, z: (a, z ^ 1))
    self_paired = (self_total[:block].astype(F32) + self_across[:block].astype(F32)).astype(BF16)
    if relay:
        vectors = self_total[2 * block :].astype(F32) + self_across[block:].astype(F32)
        vectors = vectors + move(vectors, lambda a, z: (a, z ^ 2))
    else:
        vectors = lax.psum(lax.psum(vectors, "narrow"), "wide", axis_index_groups=groups)
    in_third = from_main(after(in_opposite, early_paired), 1)
    self_opposite = from_opposite(self_paired)
    grad_early = to_owner(early_paired, after(early_opposite, self_paired))
    grad_unit, grad_cross = grad_early[:, : 2 * hidden_units], grad_early[:, 2 * hidden_units :]
    grad_self = to_owner(self_paired, self_opposite)

    def copied(first, last, value, opposite, beside, third, dtype):
        near_copy = jnp.where(main, value[first:last], beside[first:last])
        far_copy = jnp.where(main, opposite[first:last], third[first:last])
        return per_batch(near_copy, far_copy, dtype)

    copies = (copies_block, copies_opposite, copies_beside, copies_third)
    encoded_grad = copied(0, frame_rows, *copies, F32)
    output = copied(frame_rows, frame_rows + tok_rows, *copies, BF16)
    input_grad = copied(0, tok_rows, in_rows, in_opposite, in_beside, in_third, F32)

    def unpacked(grad):
        stack = jnp.stack([grad[:, head_cols * k : head_cols * (k + 1)] for k in range(3)])
        return stack, grad[:, 3 * head_cols :].T

    grad_self_proj, grad_out_one = unpacked(grad_self)
    grad_cross_proj, grad_out_two = unpacked(grad_cross)

    mine = lax.dynamic_slice_in_dim(vectors, 9 + 2 * odd, 2, 0)
    mine = jnp.where(home, mine, swap(mine))
    return (
        output,
        input_grad,
        encoded_grad,
        vectors[:3],
        vectors[3:6],
        mine[0].reshape(4, head_cols),
        vectors[6:9],
        mine[1],
        grad_self_proj,
        grad_cross_proj,
        jnp.stack([grad_out_one, grad_out_two]),
        grad_unit[:, :hidden_units],
        grad_unit[:, hidden_units:].T,
    )


def solution(mesh):
    in_specs = (
        P(None, "wide", None),
        P(None, "wide", None),
        P(),
        P(),
        P(),
        P(),
        P(None, "narrow"),
        P(),
        P("narrow"),
        P(None, "wide", "narrow"),
        P(None, "wide", "narrow"),
        P(None, "narrow", "wide"),
        P("wide", "narrow"),
        P("narrow", "wide"),
        P(None, "wide", None),
    )
    out_specs = (
        P(None, "wide", None),
        P(None, "wide", None),
        P(None, "wide", None),
        P(),
        P(),
        P(None, "narrow"),
        P(),
        P("narrow"),
        P(None, "wide", "narrow"),
        P(None, "wide", "narrow"),
        P(None, "narrow", "wide"),
        P("wide", "narrow"),
        P("narrow", "wide"),
    )
    return jax.shard_map(body, mesh=mesh, in_specs=in_specs, out_specs=out_specs, check_vma=False)
```
